32 devices in a mesh: dp: 8 (over y, x, core), ctx: 4 (over z).
Axes of the slice: x: 2, y: 2, z: 4, core: 2. Of those that a mesh axis runs over, the one named last changes fastest.
Arguments:
- frames: bfloat16 [8192, 1024], P(('dp', 'ctx')), parts along dimension 0, may hold values from -20 to 20
- tile_source: int32 [512], P('dp'), parts along dimension 0, may hold values from 0 to 63, as said below
- tile_utt: int32 [512], P('dp'), parts along dimension 0, may hold values from 0 to 3, never falling along the last dimension, each value on 1 to 33 neighbouring positions
- query_weight: bfloat16 [1024, 512], replicated, may hold values from -1.625 to 1.625
- key_weight: bfloat16 [1024, 512], replicated, may hold values from -0.1875 to 0.1875
- value_weight: bfloat16 [1024, 512], replicated, may hold values from -0.1875 to 0.1875
- output_weight: bfloat16 [512, 1024], replicated, may hold values from -1.5 to 1.5
- depth_weight: float32 [31, 1024], replicated, may hold values from -1 to 1
- bn_scale: float32 [1024], replicated, may hold values from 0.5 to 2
- bn_shift: float32 [1024], replicated, may hold values from -3 to 3
Outputs:
- encoded: bfloat16 [8192, 1024], P(('dp', 'ctx')), parts along dimension 0
The draws below stay inside these ranges and needn't reach their ends.
There are 8 independent parts, one for each index of `dp`. The reference program is written for one: setup_inputs(seed, part) draws one part's arguments, and reference() takes and returns one part's arrays. A program takes and returns all parts, laid end to end along the dimension named above; an argument that names none is the same for every part. Nothing has to cross between parts.
Inputs may be any that keep to these rules, and one draw needn't show every extreme that they name: `tile_source`: A permutation of the tiles of a part. The tiles that one shard receives come at most 4 from any one shard, and exactly 4 from some shard; for one tile position within a shard, the sources over all shards lie on distinct shards. `tile_utt`: never falls along the tiles; each of the 4 utterances holds 1 to 33 tiles, one exactly 33.
All inputs are finite; a program needn't handle non-finite values.
Results may differ from the reference program's by a relative error of at most 0.0068.
Values may be sent and summed in bfloat16 or wider, within the bound.
No kernel may reach another device: no remote copies, remote signals or barrier semaphores. Data moves between devices by JAX's collectives and lax.ppermute only.
A program may use at most 64 MiB of HBM per device.

```python
import math
import jax
import jax.numpy as jnp
import numpy as np
from jax import lax

D = 1024
HEADS = 4
HEAD_DIM = 128
KERNEL = 31
TILE = 16
UTTS = 4
TILES_DEV = 16
N_TILES = 64
ROWS_DEV = 256
ROWS = 1024
UTT_MAX = 33
N_CTX = 4


def draw_frames(key, part):
    first_key = jax.random.fold_in(key, 1)
    result = jax.random.truncated_normal(first_key, -6.0, 6.0, (ROWS, D), jnp.float32)
    return result.astype(jnp.bfloat16)


def projection_pair(key):
    first_key = jax.random.fold_in(key, 21)
    second_key = jax.random.fold_in(key, 22)
    proj_width = HEADS * HEAD_DIM
    factor = D ** (-0.5)
    key_matrix = jax.random.truncated_normal(first_key, -6.0, 6.0, (D, proj_width), jnp.float32) * factor
    query_matrix = jax.random.truncated_normal(second_key, -6.0, 6.0, (D, proj_width), jnp.float32) * factor
    return (query_matrix, key_matrix)


def draw_query_weight(key, part):
    return projection_pair(key)[0].astype(jnp.bfloat16)


def draw_key_weight(key, part):
    return projection_pair(key)[1].astype(jnp.bfloat16)


def draw_tile_source(key, part):
    shard_count = N_CTX
    labels = jax.random.permutation(jax.random.fold_in(key, 11), shard_count)
    inverse = jnp.argsort(labels)
    draw_span = max(shard_count, TILES_DEV)
    offsets = jax.random.permutation(jax.random.fold_in(key, 12), draw_span)[:TILES_DEV] % shard_count
    positions = jnp.arange(N_TILES, dtype=jnp.int32)
    dest_shard = positions // TILES_DEV
    slot_index = positions % TILES_DEV
    source_shard = labels[(inverse[dest_shard] + offsets[slot_index]) % shard_count]
    split_keys = jax.random.split(jax.random.fold_in(key, 13), shard_count)
    orders = jax.vmap(lambda single: jax.random.permutation(single, TILES_DEV))(split_keys)
    return (source_shard * TILES_DEV + orders[source_shard, slot_index]).astype(jnp.int32)


def profile(amount, total, most, skew):
    loads = [(1 << 20) // math.isqrt(standing ** skew) + 1 for standing in range(2, amount + 1)]
    surplus, holding = total - most - (amount - 1), [1] * (amount - 1)
    while surplus > 0:
        movable = [i for i in range(amount - 1) if holding[i] < most]
        mass, budget = sum([loads[i] for i in movable]), surplus
        for i in movable:
            more = min(most - holding[i], max(1, budget * loads[i] // mass), surplus)
            holding[i] = holding[i] + more
            surplus = surplus - more
    return np.array([most] + holding)


def uneven(own_key, number_of, total, reach, skew):
    if number_of == 2:
        one = jax.random.randint(own_key, (), max(1, total - reach), min(reach, total - 1) + 1)
        return jnp.stack([one, total - one])
    sizes = jnp.asarray(profile(number_of, total, reach, skew), jnp.int32)
    couples = (number_of - 1) // 2
    donor, receiver = sizes[1:1 + 2 * couples:2], sizes[2:2 + 2 * couples:2]
    slack = jnp.minimum(donor - 1, reach - receiver)
    passed = jax.random.randint(jax.random.fold_in(own_key, 1), (couples,), 0, 1 << 20) % (slack + 1)
    sizes = sizes.at[1:1 + 2 * couples:2].set(donor - passed).at[2:2 + 2 * couples:2].set(receiver + passed)
    return sizes[jax.random.permutation(jax.random.fold_in(own_key, 2), number_of)]


def noise(stream_key, extent, width, most, kind=jnp.bfloat16):
    entries = width * jax.random.normal(stream_key, extent, jnp.float32)
    return jnp.clip(entries, min=-most, max=most).astype(kind)


def setup_inputs(seed: int = 0, part: int = 0) -> dict:
    splits = jax.random.split(jax.random.key(seed), 11)
    part_splits = jax.random.split(jax.random.fold_in(splits[10], part), 11)
    return {
        "frames": draw_frames(jax.random.fold_in(jax.random.fold_in(splits[10], part), 71), part),
        "tile_source": draw_tile_source(jax.random.fold_in(jax.random.fold_in(splits[10], part), 71), part),
        "tile_utt": jnp.searchsorted(jnp.cumsum(uneven(part_splits[2], UTTS, N_TILES, UTT_MAX, 2)), jnp.arange(N_TILES), side="right").astype(jnp.int32),
        "query_weight": draw_query_weight(jax.random.fold_in(splits[10], 71), part),
        "key_weight": draw_key_weight(jax.random.fold_in(splits[10], 71), part),
        "value_weight": noise(splits[5], (D, HEADS * HEAD_DIM), D ** -0.5, 0.1875),
        "output_weight": noise(splits[6], (HEADS * HEAD_DIM, D), 16 ** -0.5, 1.5),
        "depth_weight": noise(splits[7], (KERNEL, D), KERNEL ** -0.5, 1.0, jnp.float32),
        "bn_scale": jnp.clip(jnp.exp(jax.random.uniform(splits[8], (D,), jnp.float32, math.log(0.5), math.log(2.0))), 0.5, 2.0),
        "bn_shift": noise(splits[9], (D,), 0.5, 3.0, jnp.float32),
    }


def layer_norm(rows):
    values = rows.astype(jnp.float32)
    center = values - lax.optimization_barrier(jnp.mean(values, axis=-1, keepdims=True))
    spread = lax.optimization_barrier(jnp.mean(center * center, axis=-1, keepdims=True))
    return center * lax.rsqrt(spread + 1e-05)

def reference(frames, tile_source, tile_utt, query_weight, key_weight, value_weight, output_weight, depth_weight, bn_scale, bn_shift):
    tile_rows = frames.reshape(N_TILES, TILE, D)
    grouped = jnp.take(tile_rows, tile_source, axis=0).reshape(ROWS, D)
    normed = layer_norm(grouped).astype(jnp.bfloat16)
    queries = jnp.dot(normed, query_weight, preferred_element_type=jnp.float32).astype(jnp.bfloat16).reshape(ROWS, HEADS, HEAD_DIM)
    key_rows = jnp.dot(normed, key_weight, preferred_element_type=jnp.float32).astype(jnp.bfloat16).reshape(ROWS, HEADS, HEAD_DIM)
    value_rows = jnp.dot(normed, value_weight, preferred_element_type=jnp.float32).astype(jnp.bfloat16).reshape(ROWS, HEADS, HEAD_DIM)
    row_utt = jnp.repeat(tile_utt, TILE)
    score_scale = 1.0 / math.sqrt(HEAD_DIM)
    key_float = key_rows.astype(jnp.float32)
    value_float = value_rows.astype(jnp.float32)

    def one_block(block_index):
        first_row = block_index * ROWS_DEV
        block_queries = lax.dynamic_slice_in_dim(queries, first_row, ROWS_DEV, 0).astype(jnp.float32)
        block_utt = lax.dynamic_slice_in_dim(row_utt, first_row, ROWS_DEV, 0)
        scores = jnp.einsum('qhd,khd->hqk', block_queries, key_float) * score_scale
        allowed = (block_utt[:, None] == row_utt[None, :])[None]
        row_max = lax.optimization_barrier(jnp.max(jnp.where(allowed, scores, -1e+30), axis=-1, keepdims=True))
        weights = jnp.where(allowed, jnp.exp(scores - row_max), 0.0)
        row_sum = lax.optimization_barrier(jnp.sum(weights, axis=-1, keepdims=True))
        rounded = lax.optimization_barrier(weights.astype(jnp.bfloat16)).astype(jnp.float32)
        summed = jnp.einsum('hqk,khd->hqd', rounded, value_float)
        return jnp.transpose(summed / row_sum, (1, 0, 2)).reshape(ROWS_DEV, HEADS * HEAD_DIM)
    attended = lax.map(one_block, jnp.arange(N_CTX, dtype=jnp.int32)).reshape(ROWS, HEADS * HEAD_DIM).astype(jnp.bfloat16)
    residual = (grouped.astype(jnp.float32) + jnp.dot(attended, output_weight, preferred_element_type=jnp.float32)).astype(jnp.bfloat16)
    shaped = lax.optimization_barrier(layer_norm(residual).astype(jnp.bfloat16)).astype(jnp.float32)
    margin = (KERNEL - 1) // 2
    padded = jnp.pad(shaped, ((margin, margin), (0, 0)))
    padded_utt = jnp.pad(row_utt, (margin, margin), constant_values=-1)
    convolved = jnp.zeros((ROWS, D), jnp.float32)
    for offset in range(KERNEL):
        aligned = (padded_utt[offset:offset + ROWS] == row_utt)[:, None]
        convolved = convolved + jnp.where(aligned, padded[offset:offset + ROWS], 0.0) * depth_weight[offset]
    activation = convolved * bn_scale + bn_shift
    return (residual.astype(jnp.float32) + activation * jax.nn.sigmoid(activation)).astype(jnp.bfloat16)
```

```python
import functools
import math

import jax
import jax.numpy as jnp
from jax import lax
from jax.experimental import pallas as pl
from jax.experimental.pallas import tpu as pltpu
from jax.sharding import PartitionSpec as P

HEADS = 4
HEAD_DIM = 128
KERNEL = 31
TILE = 16
NEGATIVE = -1e30

VMEM = pl.BlockSpec(memory_space=pltpu.VMEM)
SMEM = pl.BlockSpec(memory_space=pltpu.SMEM)
ANY = pl.BlockSpec(memory_space=pl.ANY)


def layer_norm(rows):
    values = rows.astype(jnp.float32)
    center = values - jnp.mean(values, axis=-1, keepdims=True)
    spread = jnp.mean(center * center, axis=-1, keepdims=True)
    return center * lax.rsqrt(spread + 1e-05)


def key_value_kernel(rows_ref, key_weight_ref, value_weight_ref, key_ref, value_ref):
    normed = layer_norm(rows_ref[...]).astype(jnp.bfloat16)
    key_ref[...] = jnp.dot(
        normed, key_weight_ref[...], preferred_element_type=jnp.float32
    ).astype(jnp.bfloat16)
    value_ref[...] = jnp.dot(
        normed, value_weight_ref[...], preferred_element_type=jnp.float32
    ).astype(jnp.bfloat16)


def key_value(rows, key_weight, value_weight):
    shape = jax.ShapeDtypeStruct((rows.shape[0], key_weight.shape[1]), jnp.bfloat16)
    flops = 4 * rows.shape[0] * rows.shape[1] * key_weight.shape[1]
    return pl.pallas_call(
        key_value_kernel,
        out_shape=(shape, shape),
        in_specs=[VMEM] * 3,
        out_specs=(VMEM, VMEM),
        cost_estimate=pl.CostEstimate(flops=flops, bytes_accessed=3 << 20, transcendentals=0),
        name="key_value",
    )(rows, key_weight, value_weight)


def block_kernel(count, me_ref, source_ref, utt_ref, key_utt_ref, *refs):
    chunks = refs[:count]
    keys = refs[count : 2 * count]
    values = refs[2 * count : 3 * count]
    query_weight, output_weight, taps, scale, shift, out_ref = refs[3 * count : 3 * count + 6]
    grouped, query_utt, residual_rows, shaped_rows, sems = refs[3 * count + 6 :]
    me = me_ref[0]
    rows_dev = out_ref.shape[0]
    tiles_dev = rows_dev // TILE
    held = tiles_dev + 2
    total = tiles_dev * count
    first = me * tiles_dev - 1

    def tile_at(i):
        return jnp.clip(first + i, 0, total - 1)

    for i in range(held):
        source = source_ref[tile_at(i)]
        shard = source // tiles_dev
        row = pl.multiple_of((source % tiles_dev) * TILE, TILE)
        behind = lax.rem(me - shard + count, count)
        for step in range(count):

            @pl.when(behind == step)
            def _(step=step, row=row, i=i):
                pltpu.make_async_copy(
                    chunks[step].at[pl.ds(row, TILE), :],
                    grouped.at[pl.ds(i * TILE, TILE), :],
                    sems.at[i],
                ).start()

        query_utt[pl.ds(i * TILE, TILE), :] = jnp.full((TILE, 128), utt_ref[tile_at(i)], jnp.int32)
    for i in range(held):
        pltpu.make_async_copy(
            chunks[0].at[pl.ds(0, TILE), :], grouped.at[pl.ds(i * TILE, TILE), :], sems.at[i]
        ).wait()
    normed = layer_norm(grouped[...]).astype(jnp.bfloat16)
    queries = jnp.dot(normed, query_weight[...], preferred_element_type=jnp.float32).astype(
        jnp.bfloat16
    )
    allowed = query_utt[:, :1] == key_utt_ref[...]
    exponent_scale = math.log2(math.e) / math.sqrt(HEAD_DIM)
    heads = []
    for head in range(HEADS):
        columns = slice(head * HEAD_DIM, (head + 1) * HEAD_DIM)
        key_head = jnp.concatenate([key[:, columns] for key in keys], axis=0)
        value_head = jnp.concatenate([value[:, columns] for value in values], axis=0)
        scores = lax.dot_general(
            queries[:, columns],
            key_head,
            (((1,), (1,)), ((), ())),
            preferred_element_type=jnp.float32,
        )
        scores = jnp.where(allowed, scores, NEGATIVE)
        top = jnp.max(scores, axis=-1, keepdims=True)
        weights = jnp.exp2((scores - top) * exponent_scale)
        row_sum = jnp.sum(weights, axis=-1, keepdims=True)
        summed = jnp.dot(
            weights.astype(jnp.bfloat16), value_head, preferred_element_type=jnp.float32
        )
        heads.append((summed / row_sum).astype(jnp.bfloat16))
    attended = jnp.concatenate(heads, axis=1)
    residual = (
        grouped[...].astype(jnp.float32)
        + jnp.dot(attended, output_weight[...], preferred_element_type=jnp.float32)
    ).astype(jnp.bfloat16)
    residual_rows[...] = residual
    shaped_rows[...] = layer_norm(residual).astype(jnp.bfloat16).astype(jnp.float32)

    def one_tile(i, carried):
        here = utt_ref[tile_at(i + 1)]
        before = jnp.where((first + i >= 0) & (utt_ref[tile_at(i)] == here), 1.0, 0.0)
        after = jnp.where((first + i + 2 < total) & (utt_ref[tile_at(i + 2)] == here), 1.0, 0.0)
        row = pl.multiple_of(i * TILE, TILE)
        for block in range(out_ref.shape[1] // 128):
            columns = slice(block * 128, (block + 1) * 128)
            window = [
                shaped_rows[pl.ds(row, TILE), columns] * before,
                shaped_rows[pl.ds(row + TILE, TILE), columns],
                shaped_rows[pl.ds(row + 2 * TILE, TILE), columns] * after,
            ]
            window = jnp.concatenate(window, axis=0)
            convolved = None
            for part in range(8):
                total_part = None
                for start in range(0, 32, 8):
                    tap = start + part - 1
                    if tap < 0:
                        continue
                    term = window[start : start + 24] * taps[tap : tap + 1, columns]
                    total_part = term if total_part is None else total_part + term
                if part:
                    total_part = pltpu.roll(total_part, 24 - part, axis=0)
                total_part = total_part[:TILE]
                convolved = total_part if convolved is None else convolved + total_part
            activation = convolved * scale[:, columns] + shift[:, columns]
            kept = residual_rows[pl.ds(row + TILE, TILE), columns].astype(jnp.float32)
            out_ref[pl.ds(row, TILE), columns] = (
                kept + activation / (1.0 + jnp.exp(-activation))
            ).astype(jnp.bfloat16)
        return carried

    lax.fori_loop(0, tiles_dev, one_tile, 0)


def per_device(
    frames,
    tile_source,
    tile_utt,
    query_weight,
    key_weight,
    value_weight,
    output_weight,
    depth_weight,
    bn_scale,
    bn_shift,
):
    count = lax.axis_size("ctx")
    me = lax.axis_index("ctx")
    rows_dev, width = frames.shape
    tiles_dev = rows_dev // TILE
    ring = [(i, (i + 1) % count) for i in range(count)]
    chunks = [frames]
    for _ in range(count - 1):
        chunks.append(lax.ppermute(chunks[-1], "ctx", ring))
    pairs = [key_value(chunk, key_weight, value_weight) for chunk in chunks]
    shards = lax.rem(me - jnp.arange(count, dtype=jnp.int32) + count, count)
    arrived = (shards[:, None] * tiles_dev + jnp.arange(tiles_dev, dtype=jnp.int32)).reshape(-1)
    key_utt = jnp.sum(jnp.where(arrived[:, None] == tile_source[None, :], tile_utt[None, :], 0), axis=1)
    key_utt = jnp.repeat(key_utt, TILE).reshape(1, -1)
    held_rows = rows_dev + 2 * TILE
    return pl.pallas_call(
        functools.partial(block_kernel, count),
        out_shape=jax.ShapeDtypeStruct((rows_dev, width), jnp.bfloat16),
        in_specs=[SMEM] * 3 + [VMEM] + [ANY] * count + [VMEM] * (2 * count + 5),
        out_specs=VMEM,
        scratch_shapes=[
            pltpu.VMEM((held_rows, width), jnp.bfloat16),
            pltpu.VMEM((held_rows, 128), jnp.int32),
            pltpu.VMEM((held_rows, width), jnp.bfloat16),
            pltpu.VMEM((held_rows, width), jnp.float32),
            pltpu.SemaphoreType.DMA((tiles_dev + 2,)),
        ],
        cost_estimate=pl.CostEstimate(
            flops=2 << 30, bytes_accessed=8 << 20, transcendentals=1 << 20
        ),
        name="block",
    )(
        me.reshape(1),
        tile_source,
        tile_utt,
        key_utt,
        *chunks,
        *[pair[0] for pair in pairs],
        *[pair[1] for pair in pairs],
        query_weight,
        output_weight,
        depth_weight,
        bn_scale.reshape(1, -1),
        bn_shift.reshape(1, -1),
    )


def solution(mesh):
    return jax.shard_map(
        per_device,
        mesh=mesh,
        in_specs=(P(("dp", "ctx"), None), P("dp"), P("dp"), P(), P(), P(), P(), P(), P(), P()),
        out_specs=P(("dp", "ctx"), None),
        check_vma=False,
    )
```

```python
import functools
import math

import jax
import jax.numpy as jnp
from jax import lax
from jax.experimental import pallas as pl
from jax.experimental.pallas import tpu as pltpu
from jax.sharding import PartitionSpec as P

HEADS = 4
HEAD_DIM = 128
KERNEL = 31
TILE = 16
UTTS = 4
NEGATIVE = -1e30

VMEM = pl.BlockSpec(memory_space=pltpu.VMEM)
SMEM = pl.BlockSpec(memory_space=pltpu.SMEM)


def params(mib):
    return pltpu.CompilerParams(vmem_limit_bytes=mib << 20)


def layer_norm(rows):
    values = rows.astype(jnp.float32)
    center = values - jnp.mean(values, axis=-1, keepdims=True)
    spread = jnp.mean(center * center, axis=-1, keepdims=True)
    return center * lax.rsqrt(spread + 1e-05)


def project(rows, weight_ref):
    return jnp.dot(rows, weight_ref[...], preferred_element_type=jnp.float32).astype(jnp.bfloat16)


def attend_and_convolve(
    first,
    total,
    utt_ref,
    grouped,
    query_utt,
    key_utt,
    key_parts,
    value_parts,
    query_weight,
    output_weight,
    taps,
    scale,
    shift,
    out_ref,
    padded,
    residual_rows,
):
    rows_dev, width = out_ref.shape
    tiles_dev = rows_dev // TILE
    held = tiles_dev + 2

    def tile_at(i):
        return jnp.clip(first + i, 0, total - 1)

    padded[...] = jnp.zeros_like(padded)
    queries = project(layer_norm(grouped[...]).astype(jnp.bfloat16), query_weight)
    allowed = query_utt[:, :1] == key_utt
    exponent_scale = math.log2(math.e) / math.sqrt(HEAD_DIM)
    heads = []
    for head in range(HEADS):
        columns = slice(head * HEAD_DIM, (head + 1) * HEAD_DIM)
        key_head = jnp.concatenate([part[:, columns] for part in key_parts], axis=0)
        value_head = jnp.concatenate([part[:, columns] for part in value_parts], axis=0)
        scores = lax.dot_general(
            queries[:, columns],
            key_head,
            (((1,), (1,)), ((), ())),
            preferred_element_type=jnp.float32,
        )
        scores = jnp.where(allowed, scores, NEGATIVE)
        top = jnp.max(scores, axis=-1, keepdims=True)
        weights = jnp.exp2((scores - top) * exponent_scale)
        row_sum = jnp.sum(weights, axis=-1, keepdims=True)
        summed = jnp.dot(
            weights.astype(jnp.bfloat16), value_head, preferred_element_type=jnp.float32
        )
        heads.append((summed / row_sum).astype(jnp.bfloat16))
    attended = jnp.concatenate(heads, axis=1)
    residual = (
        grouped[...].astype(jnp.float32)
        + jnp.dot(attended, output_weight[...], preferred_element_type=jnp.float32)
    ).astype(jnp.bfloat16)
    residual_rows[...] = residual[TILE : TILE + rows_dev]
    shaped = layer_norm(residual).astype(jnp.bfloat16).astype(jnp.float32)
    places = []
    place = jnp.int32(1)
    for i in range(held):
        if i:
            place = place + 1
            place = place + jnp.where(utt_ref[tile_at(i)] == utt_ref[tile_at(i - 1)], 0, 1)
        inside = (first + i >= 0) & (first + i < total)
        target = jnp.where(inside, place, padded.shape[1] // TILE - 1)
        row = pl.multiple_of(target * TILE, TILE)
        for block in range(width // 128):
            padded[block, pl.ds(row, TILE), :] = shaped[
                i * TILE : (i + 1) * TILE, block * 128 : (block + 1) * 128
            ]
        places.append(place)

    def one_tile(i, place):
        gap = jnp.where(utt_ref[tile_at(i + 1)] == utt_ref[tile_at(i)], 0, 1)
        place = place + 1 + gap
        start = pl.multiple_of(place * TILE, TILE)
        row = pl.multiple_of(i * TILE, TILE)
        for block in range(width // 128):
            columns = slice(block * 128, (block + 1) * 128)
            sums = [None] * 4
            for tap in range(KERNEL):
                term = (
                    padded[block, pl.ds(start + (tap - KERNEL // 2), TILE), :]
                    * taps[tap : tap + 1, columns]
                )
                sums[tap % 4] = term if sums[tap % 4] is None else sums[tap % 4] + term
            convolved = (sums[0] + sums[1]) + (sums[2] + sums[3])
            half = 0.5 * (convolved * scale[:, columns] + shift[:, columns])
            kept = residual_rows[pl.ds(row, TILE), columns].astype(jnp.float32)
            out_ref[pl.ds(row, TILE), columns] = (kept + (half + half * jnp.tanh(half))).astype(
                jnp.bfloat16
            )
        return place

    lax.fori_loop(0, tiles_dev, one_tile, places[0], unroll=2)


def padded_rows(tiles_dev):
    return (1 + tiles_dev + 2 + (UTTS - 1) + 2) * TILE


def block_scratch(rows_dev, width):
    held_rows = rows_dev + 2 * TILE
    return [
        pltpu.VMEM((held_rows, width), jnp.bfloat16),
        pltpu.VMEM((held_rows, 128), jnp.int32),
        pltpu.VMEM((width // 128, padded_rows(rows_dev // TILE), 128), jnp.float32),
        pltpu.VMEM((rows_dev, width), jnp.bfloat16),
    ]


def key_value_kernel(rows_ref, key_weight_ref, value_weight_ref, key_ref, value_ref):
    normed = layer_norm(rows_ref[...]).astype(jnp.bfloat16)
    key_ref[...] = project(normed, key_weight_ref)
    value_ref[...] = project(normed, value_weight_ref)


def key_value(rows, key_weight, value_weight):
    shape = jax.ShapeDtypeStruct((rows.shape[0], key_weight.shape[1]), jnp.bfloat16)
    flops = 4 * rows.shape[0] * rows.shape[1] * key_weight.shape[1]
    return pl.pallas_call(
        key_value_kernel,
        out_shape=(shape, shape),
        in_specs=[VMEM] * 3,
        out_specs=(VMEM, VMEM),
        cost_estimate=pl.CostEstimate(flops=flops, bytes_accessed=3 << 20, transcendentals=0),
        name="key_value",
    )(rows, key_weight, value_weight)


def ring_kernel(count, me_ref, source_ref, utt_ref, key_utt_ref, *refs):
    chunks = refs[:count]
    keys = refs[count : 2 * count]
    values = refs[2 * count : 3 * count]
    weights_and_out = refs[3 * count : 3 * count + 6]
    grouped, query_utt, padded, residual_rows, sems = refs[3 * count + 6 :]
    me = me_ref[0]
    tiles_dev = weights_and_out[-1].shape[0] // TILE
    held = tiles_dev + 2
    total = tiles_dev * count
    first = me * tiles_dev - 1
    for i in range(held):
        position = jnp.clip(first + i, 0, total - 1)
        source = source_ref[position]
        row = pl.multiple_of((source % tiles_dev) * TILE, TILE)
        behind = lax.rem(me - source // tiles_dev + count, count)
        for step in range(count):

            @pl.when(behind == step)
            def _(step=step, row=row, i=i):
                pltpu.make_async_copy(
                    chunks[step].at[pl.ds(row, TILE), :],
                    grouped.at[pl.ds(i * TILE, TILE), :],
                    sems.at[i],
                ).start()

        query_utt[pl.ds(i * TILE, TILE), :] = jnp.full((TILE, 128), utt_ref[position], jnp.int32)
    for i in range(held):
        pltpu.make_async_copy(
            chunks[0].at[pl.ds(0, TILE), :], grouped.at[pl.ds(i * TILE, TILE), :], sems.at[i]
        ).wait()
    attend_and_convolve(
        first, total, utt_ref, grouped, query_utt, key_utt_ref[...], keys, values,
        *weights_and_out, padded, residual_rows,
    )


def ring_block(
    frames, tile_source, tile_utt, query_weight, key_weight, value_weight, output_weight,
    depth_weight, bn_scale, bn_shift,
):
    count = lax.axis_size("ctx")
    me = lax.axis_index("ctx")
    rows_dev, width = frames.shape
    tiles_dev = rows_dev // TILE
    ring = [(i, (i + 1) % count) for i in range(count)]
    chunks = [frames]
    for _ in range(count - 1):
        chunks.append(lax.ppermute(chunks[-1], "ctx", ring))
    pairs = [key_value(chunk, key_weight, value_weight) for chunk in chunks]
    shards = lax.rem(me - jnp.arange(count, dtype=jnp.int32) + count, count)
    arrived = (shards[:, None] * tiles_dev + jnp.arange(tiles_dev, dtype=jnp.int32)).reshape(-1)
    key_utt = jnp.sum(
        jnp.where(arrived[:, None] == tile_source[None, :], tile_utt[None, :], 0), axis=1
    )
    key_utt = jnp.repeat(key_utt, TILE).reshape(1, -1)
    return pl.pallas_call(
        functools.partial(ring_kernel, count),
        out_shape=jax.ShapeDtypeStruct((rows_dev, width), jnp.bfloat16),
        in_specs=[SMEM] * 3
        + [VMEM]
        + [pl.BlockSpec(memory_space=pl.ANY)] * count
        + [VMEM] * (2 * count + 5),
        out_specs=VMEM,
        scratch_shapes=block_scratch(rows_dev, width)
        + [pltpu.SemaphoreType.DMA((tiles_dev + 2,))],
        cost_estimate=pl.CostEstimate(
            flops=2 << 30, bytes_accessed=8 << 20, transcendentals=1 << 20
        ),
        name="ring_block",
    )(
        me.reshape(1), tile_source, tile_utt, key_utt, *chunks,
        *[pair[0] for pair in pairs], *[pair[1] for pair in pairs],
        query_weight, output_weight, depth_weight, bn_scale.reshape(1, -1), bn_shift.reshape(1, -1),
    )


COUNT = 4
SWAP_OUTER = [(0, 1), (1, 0), (2, 3), (3, 2)]
SWAP_INNER = [(1, 2), (2, 1)]
TO_ENDS = [(1, 0), (2, 3)]
FROM_ENDS = [(0, 1), (3, 2)]


def quarter_of(source_shard, target):
    return jnp.where(source_shard % 2 == 1, target, COUNT - 1 - target)


def arrange_kernel(me_ref, source_ref, rows_ref, low_ref, last_ref, high_ref, start_ref, filled):
    me = me_ref[0]
    tiles_dev = rows_ref.shape[0] // TILE
    quarter_rows = rows_ref.shape[0] // COUNT
    for target in range(COUNT):
        filled[target] = 0

    def one(position, carried):
        source = source_ref[position]

        @pl.when(source // tiles_dev == me)
        def _():
            target = position // tiles_dev
            rank = filled[target]
            filled[target] = rank + 1
            quarter = quarter_of(me, target)
            tile = rows_ref[pl.ds(pl.multiple_of((source % tiles_dev) * TILE, TILE), TILE), :]
            row = pl.multiple_of(quarter * quarter_rows + rank * TILE, TILE)

            @pl.when(quarter < COUNT - 1)
            def _():
                low_ref[pl.ds(row, TILE), :] = tile

            @pl.when(quarter == COUNT - 1)
            def _():
                last_ref[pl.ds(pl.multiple_of(rank * TILE, TILE), TILE), :] = tile

            @pl.when(quarter > 0)
            def _():
                high_ref[pl.ds(pl.multiple_of(row - quarter_rows, TILE), TILE), :] = tile

            @pl.when(quarter == 0)
            def _():
                start_ref[pl.ds(row, TILE), :] = tile

        return carried

    lax.fori_loop(0, COUNT * tiles_dev, one, 0, unroll=4)


def tables_kernel(source_ref, utt_ref, rank_ref, key_utt_ref, filled):
    total = source_ref.shape[0]
    tiles_dev = total // COUNT
    per_pair = tiles_dev // COUNT
    for pair in range(COUNT * COUNT):
        filled[pair] = 0

    def one(position, carried):
        pair = (source_ref[position] // tiles_dev) * COUNT + position // tiles_dev
        rank = filled[pair]
        filled[pair] = rank + 1
        rank_ref[position] = rank
        key_utt_ref[pair * per_pair + rank] = utt_ref[position]
        return carried

    lax.fori_loop(0, total, one, 0, unroll=4)


def held_tiles(me_ref, source_ref, rank_ref, rows_dev):
    me = me_ref[0]
    tiles_dev = rows_dev // TILE
    total = tiles_dev * COUNT
    for i in range(tiles_dev + 2):
        position = jnp.clip(me * tiles_dev - 1 + i, 0, total - 1)
        source = source_ref[position] // tiles_dev
        quarter = quarter_of(source, position // tiles_dev)
        row = quarter * (rows_dev // COUNT) + rank_ref[position] * TILE
        yield i, me ^ source, quarter, row


def early_kernel(
    me_ref, source_ref, rank_ref,
    low, last, high, near, near_last, inner, inner_end,
    key_weight, value_weight, key_ref, value_ref, grouped, rows,
):
    me = me_ref[0]
    is_end = (me == 0) | (me == COUNT - 1)
    rows_dev = high.shape[0] + last.shape[0]
    piece = low.shape[0]
    quarter_rows = last.shape[0]
    rows[0:piece] = low[...]
    rows[piece:rows_dev] = last[...]
    base = rows_dev
    rows[base : base + piece] = near[...]

    @pl.when(is_end)
    def _():
        rows[base + piece : base + 2 * piece] = inner_end[...]

    @pl.when(jnp.logical_not(is_end))
    def _():
        rows[base + piece : base + 2 * piece] = inner[...]

    rows[base + 2 * piece :] = near_last[...]
    for i, apart, quarter, row in held_tiles(me_ref, source_ref, rank_ref, rows_dev):
        second = jnp.where(is_end, 2, 3)
        place = row
        place = jnp.where(
            apart == 1, jnp.where(quarter == 3, base + 2 * piece - 3 * quarter_rows, base) + row, place
        )
        place = jnp.where(apart == second, base + piece - quarter_rows + row, place)

        @pl.when((apart <= 1) | (apart == second))
        def _(i=i, place=place):
            grouped[i * TILE : (i + 1) * TILE] = rows[
                pl.ds(pl.multiple_of(place, TILE), TILE), :
            ]

    normed = layer_norm(rows[...]).astype(jnp.bfloat16)
    key_ref[...] = project(normed, key_weight)
    value_ref[...] = project(normed, value_weight)


def middle_kernel(me_ref, first, second, key_weight, value_weight, key_ref, value_ref):
    rows = jnp.concatenate([first[...], second[...]], axis=0)
    normed = layer_norm(rows).astype(jnp.bfloat16)
    key_ref[...] = project(normed, key_weight)
    value_ref[...] = project(normed, value_weight)


def final_kernel(
    me_ref, source_ref, utt_ref, rank_ref, key_utt_table,
    early_grouped, far, far_end, early_key, early_value, middle_key, middle_value,
    key_weight, value_weight, query_weight, output_weight, taps, scale, shift,
    out_ref, grouped, query_utt, padded, residual_rows, late,
):
    me = me_ref[0]
    is_end = (me == 0) | (me == COUNT - 1)
    rows_dev = out_ref.shape[0]
    tiles_dev = rows_dev // TILE
    total = tiles_dev * COUNT
    first = me * tiles_dev - 1
    per_pair = tiles_dev // COUNT

    @pl.when(is_end)
    def _():
        late[...] = far_end[...]

    @pl.when(jnp.logical_not(is_end))
    def _():
        late[...] = far[...]

    third = jnp.where(is_end, 3, 2)
    for i, apart, _, row in held_tiles(me_ref, source_ref, rank_ref, rows_dev):
        rows_of_tile = slice(i * TILE, (i + 1) * TILE)

        @pl.when(apart == third)
        def _(row=row, rows_of_tile=rows_of_tile):
            grouped[rows_of_tile] = late[pl.ds(pl.multiple_of(row, TILE), TILE), :]

        @pl.when(apart != third)
        def _(rows_of_tile=rows_of_tile):
            grouped[rows_of_tile] = early_grouped[rows_of_tile]

        query_utt[rows_of_tile, :] = jnp.full(
            (TILE, 128), utt_ref[jnp.clip(first + i, 0, total - 1)], jnp.int32
        )
    normed = layer_norm(late[...]).astype(jnp.bfloat16)
    late_key = project(normed, key_weight)
    late_value = project(normed, value_weight)

    near = me ^ 1
    second = me ^ jnp.where(is_end, 2, 3)
    far_shard = me ^ third
    order = [(me, quarter, False) for quarter in (0, 1, 2, 3)]
    order += [(near, quarter, False) for quarter in (0, 1, 2)]
    order += [(second, quarter, False) for quarter in (1, 2, 3)]
    order += [(near, 3, True), (second, 0, True), (far_shard, 3, True)]
    order += [(far_shard, quarter, False) for quarter in (0, 1, 2)]
    lane_tile = lax.broadcasted_iota(jnp.int32, (1, 128), 1) // TILE
    pieces = []
    tile_values = []
    for shard, quarter, inner_only in order:
        target = jnp.where(shard % 2 == 1, quarter, COUNT - 1 - quarter)
        for rank in range(per_pair):
            utt = key_utt_table[(shard * COUNT + target) * per_pair + rank]
            if inner_only:
                utt = jnp.where(is_end, -1, utt)
            tile_values.append(utt)
    per_vector = 128 // TILE
    for start in range(0, len(tile_values), per_vector):
        vector = jnp.full((1, 128), tile_values[start], jnp.int32)
        for k in range(1, per_vector):
            vector = jnp.where(lane_tile == k, tile_values[start + k], vector)
        pieces.append(vector)
    key_utt = jnp.concatenate(pieces, axis=1)
    attend_and_convolve(
        first, total, utt_ref, grouped, query_utt, key_utt,
        [early_key, middle_key, late_key], [early_value, middle_value, late_value],
        query_weight, output_weight, taps, scale, shift, out_ref, padded, residual_rows,
    )


def after(value, other):
    return lax.optimization_barrier((value, other))[0]


def line_block(
    frames, tile_source, tile_utt, query_weight, key_weight, value_weight, output_weight,
    depth_weight, bn_scale, bn_shift,
):
    me = lax.axis_index("ctx").reshape(1)
    rows_dev, width = frames.shape
    quarter = rows_dev // COUNT
    piece = rows_dev - quarter
    total = tile_source.shape[0]
    wide = key_weight.shape[1]

    def shape(rows, columns=width, kind=jnp.bfloat16):
        return jax.ShapeDtypeStruct((rows, columns), kind)

    def cost(rows):
        return pl.CostEstimate(
            flops=4 * rows * width * wide, bytes_accessed=rows * width * 4, transcendentals=rows
        )

    low, last, high, start = pl.pallas_call(
        arrange_kernel,
        out_shape=(shape(piece), shape(quarter), shape(piece), shape(quarter)),
        in_specs=[SMEM] * 2 + [VMEM],
        out_specs=(VMEM,) * 4,
        scratch_shapes=[pltpu.SMEM((COUNT,), jnp.int32)],
        compiler_params=params(8),
        name="arrange",
    )(me, tile_source, frames)
    swap = functools.partial(lax.ppermute, axis_name="ctx")
    near = swap(low, perm=SWAP_OUTER)
    inner = swap(high, perm=SWAP_INNER)
    rank, key_utt = pl.pallas_call(
        tables_kernel,
        out_shape=(jax.ShapeDtypeStruct((total,), jnp.int32),) * 2,
        in_specs=[SMEM] * 2,
        out_specs=(SMEM, SMEM),
        scratch_shapes=[pltpu.SMEM((COUNT * COUNT,), jnp.int32)],
        compiler_params=params(4),
        name="tables",
    )(tile_source, tile_utt)
    far = swap(near, perm=SWAP_INNER)
    inner_end = swap(inner, perm=TO_ENDS)
    near_last = swap(after(last, near), perm=FROM_ENDS)
    far_end = swap(far, perm=TO_ENDS)
    inner_start = swap(after(start, far), perm=SWAP_INNER)
    far_last = swap(after(near_last, far), perm=SWAP_INNER)

    early_rows = rows_dev + 2 * piece + quarter
    early_key, early_value, grouped = pl.pallas_call(
        early_kernel,
        out_shape=(shape(early_rows, wide), shape(early_rows, wide), shape(rows_dev + 2 * TILE)),
        in_specs=[SMEM] * 3 + [VMEM] * 9,
        out_specs=(VMEM,) * 3,
        scratch_shapes=[pltpu.VMEM((early_rows, width), jnp.bfloat16)],
        compiler_params=params(16),
        cost_estimate=cost(early_rows),
        name="early",
    )(
        me, tile_source, rank, low, last, high, near, near_last, inner, inner_end,
        key_weight, value_weight,
    )
    middle_key, middle_value = pl.pallas_call(
        middle_kernel,
        out_shape=(shape(2 * quarter, wide),) * 2,
        in_specs=[SMEM] + [VMEM] * 4,
        out_specs=(VMEM,) * 2,
        compiler_params=params(8),
        cost_estimate=cost(2 * quarter),
        name="middle",
    )(me, inner_start, far_last, key_weight, value_weight)
    return pl.pallas_call(
        final_kernel,
        out_shape=shape(rows_dev),
        in_specs=[SMEM] * 5 + [VMEM] * 14,
        out_specs=VMEM,
        scratch_shapes=block_scratch(rows_dev, width) + [pltpu.VMEM((piece, width), jnp.bfloat16)],
        compiler_params=params(28),
        cost_estimate=pl.CostEstimate(
            flops=2 << 30, bytes_accessed=8 << 20, transcendentals=1 << 20
        ),
        name="final",
    )(
        me, tile_source, tile_utt, rank, key_utt,
        grouped, far, far_end, early_key, early_value, middle_key, middle_value,
        key_weight, value_weight, query_weight, output_weight,
        depth_weight, bn_scale.reshape(1, -1), bn_shift.reshape(1, -1),
    )


def per_device(*arrays):
    tiles_dev = arrays[0].shape[0] // TILE
    if lax.axis_size("ctx") == COUNT and tiles_dev % COUNT == 0:
        return line_block(*arrays)
    return ring_block(*arrays)


def solution(mesh):
    return jax.shard_map(
        per_device,
        mesh=mesh,
        in_specs=(P(("dp", "ctx"), None), P("dp"), P("dp"), P(), P(), P(), P(), P(), P(), P()),
        out_specs=P(("dp", "ctx"), None),
        check_vma=False,
    )
```

```python
import functools
import math

import jax
import jax.numpy as jnp
from jax import lax
from jax.experimental import pallas as pl
from jax.experimental.pallas import tpu as pltpu
from jax.sharding import PartitionSpec as P


HEADS = 4
HEAD_DIM = 128
KERNEL = 31
TILE = 16
UTTS = 4
ARRANGE = 56
NEGATIVE = -1e30

VMEM = pl.BlockSpec(memory_space=pltpu.VMEM)
SMEM = pl.BlockSpec(memory_space=pltpu.SMEM)
HBM = pl.BlockSpec(memory_space=pltpu.HBM)


def params(mib):
    return pltpu.CompilerParams(vmem_limit_bytes=mib << 20)


def layer_norm(rows):
    values = rows.astype(jnp.float32)
    center = values - jnp.mean(values, axis=-1, keepdims=True)
    spread = jnp.mean(center * center, axis=-1, keepdims=True)
    return center * lax.rsqrt(spread + 1e-05)


def project(rows, weight_ref):
    return jnp.dot(rows, weight_ref[...], preferred_element_type=jnp.float32).astype(jnp.bfloat16)


def attend_and_convolve(
    first,
    total,
    utt_ref,
    grouped,
    query_utt,
    key_utt,
    key_parts,
    value_parts,
    query_weight,
    output_weight,
    taps,
    scale,
    shift,
    out_ref,
    padded,
    residual_rows,
):
    rows_dev, width = out_ref.shape
    tiles_dev = rows_dev // TILE
    held = tiles_dev + 2

    def tile_at(i):
        return jnp.clip(first + i, 0, total - 1)

    padded[...] = jnp.zeros_like(padded)
    queries = project(layer_norm(grouped[...]).astype(jnp.bfloat16), query_weight)
    allowed = query_utt[:, :1] == key_utt
    exponent_scale = math.log2(math.e) / math.sqrt(HEAD_DIM)
    heads = []
    for head in range(HEADS):
        columns = slice(head * HEAD_DIM, (head + 1) * HEAD_DIM)
        key_head = jnp.concatenate([part[:, columns] for part in key_parts], axis=0)
        value_head = jnp.concatenate([part[:, columns] for part in value_parts], axis=0)
        scores = lax.dot_general(
            queries[:, columns],
            key_head,
            (((1,), (1,)), ((), ())),
            preferred_element_type=jnp.float32,
        )
        scores = jnp.where(allowed, scores, NEGATIVE)
        top = jnp.max(scores, axis=-1, keepdims=True)
        weights = jnp.exp2((scores - top) * exponent_scale)
        row_sum = jnp.sum(weights, axis=-1, keepdims=True)
        summed = jnp.dot(
            weights.astype(jnp.bfloat16), value_head, preferred_element_type=jnp.float32
        )
        heads.append((summed / row_sum).astype(jnp.bfloat16))
    attended = jnp.concatenate(heads, axis=1)
    residual = (
        grouped[...].astype(jnp.float32)
        + jnp.dot(attended, output_weight[...], preferred_element_type=jnp.float32)
    ).astype(jnp.bfloat16)
    residual_rows[...] = residual[TILE : TILE + rows_dev]
    shaped = layer_norm(residual).astype(jnp.bfloat16).astype(jnp.float32)
    places = []
    place = jnp.int32(1)
    for i in range(held):
        if i:
            place = place + 1
            place = place + jnp.where(utt_ref[tile_at(i)] == utt_ref[tile_at(i - 1)], 0, 1)
        inside = (first + i >= 0) & (first + i < total)
        target = jnp.where(inside, place, padded.shape[1] // TILE - 1)
        row = pl.multiple_of(target * TILE, TILE)
        for block in range(width // 128):
            padded[block, pl.ds(row, TILE), :] = shaped[
                i * TILE : (i + 1) * TILE, block * 128 : (block + 1) * 128
            ]
        places.append(place)

    def one_tile(i, place):
        gap = jnp.where(utt_ref[tile_at(i + 1)] == utt_ref[tile_at(i)], 0, 1)
        place = place + 1 + gap
        start = pl.multiple_of(place * TILE, TILE)
        row = pl.multiple_of(i * TILE, TILE)
        for block in range(width // 128):
            columns = slice(block * 128, (block + 1) * 128)
            sums = [None] * 4
            for tap in range(KERNEL):
                term = (
                    padded[block, pl.ds(start + (tap - KERNEL // 2), TILE), :]
                    * taps[tap : tap + 1, columns]
                )
                sums[tap % 4] = term if sums[tap % 4] is None else sums[tap % 4] + term
            convolved = (sums[0] + sums[1]) + (sums[2] + sums[3])
            half = 0.5 * (convolved * scale[:, columns] + shift[:, columns])
            kept = residual_rows[pl.ds(row, TILE), columns].astype(jnp.float32)
            out_ref[pl.ds(row, TILE), columns] = (kept + (half + half * jnp.tanh(half))).astype(
                jnp.bfloat16
            )
        return place

    lax.fori_loop(0, tiles_dev, one_tile, places[0], unroll=2)


def padded_rows(tiles_dev):
    return (1 + tiles_dev + 2 + (UTTS - 1) + 2) * TILE


def block_scratch(rows_dev, width):
    held_rows = rows_dev + 2 * TILE
    return [
        pltpu.VMEM((held_rows, width), jnp.bfloat16),
        pltpu.VMEM((held_rows, 128), jnp.int32),
        pltpu.VMEM((width // 128, padded_rows(rows_dev // TILE), 128), jnp.float32),
        pltpu.VMEM((rows_dev, width), jnp.bfloat16),
    ]


def key_value_kernel(rows_ref, key_weight_ref, value_weight_ref, key_ref, value_ref):
    normed = layer_norm(rows_ref[...]).astype(jnp.bfloat16)
    key_ref[...] = project(normed, key_weight_ref)
    value_ref[...] = project(normed, value_weight_ref)


def key_value(rows, key_weight, value_weight):
    shape = jax.ShapeDtypeStruct((rows.shape[0], key_weight.shape[1]), jnp.bfloat16)
    flops = 4 * rows.shape[0] * rows.shape[1] * key_weight.shape[1]
    return pl.pallas_call(
        key_value_kernel,
        out_shape=(shape, shape),
        in_specs=[VMEM] * 3,
        out_specs=(VMEM, VMEM),
        cost_estimate=pl.CostEstimate(flops=flops, bytes_accessed=3 << 20, transcendentals=0),
        name="key_value",
    )(rows, key_weight, value_weight)


def ring_kernel(count, me_ref, source_ref, utt_ref, key_utt_ref, *refs):
    chunks = refs[:count]
    keys = refs[count : 2 * count]
    values = refs[2 * count : 3 * count]
    weights_and_out = refs[3 * count : 3 * count + 6]
    grouped, query_utt, padded, residual_rows, sems = refs[3 * count + 6 :]
    me = me_ref[0]
    tiles_dev = weights_and_out[-1].shape[0] // TILE
    held = tiles_dev + 2
    total = tiles_dev * count
    first = me * tiles_dev - 1
    for i in range(held):
        position = jnp.clip(first + i, 0, total - 1)
        source = source_ref[position]
        row = pl.multiple_of((source % tiles_dev) * TILE, TILE)
        behind = lax.rem(me - source // tiles_dev + count, count)
        for step in range(count):

            @pl.when(behind == step)
            def _(step=step, row=row, i=i):
                pltpu.make_async_copy(
                    chunks[step].at[pl.ds(row, TILE), :],
                    grouped.at[pl.ds(i * TILE, TILE), :],
                    sems.at[i],
                ).start()

        query_utt[pl.ds(i * TILE, TILE), :] = jnp.full((TILE, 128), utt_ref[position], jnp.int32)
    for i in range(held):
        pltpu.make_async_copy(
            chunks[0].at[pl.ds(0, TILE), :], grouped.at[pl.ds(i * TILE, TILE), :], sems.at[i]
        ).wait()
    attend_and_convolve(
        first, total, utt_ref, grouped, query_utt, key_utt_ref[...], keys, values,
        *weights_and_out, padded, residual_rows,
    )


def ring_block(
    frames, tile_source, tile_utt, query_weight, key_weight, value_weight, output_weight,
    depth_weight, bn_scale, bn_shift,
):
    count = lax.axis_size("ctx")
    me = lax.axis_index("ctx")
    rows_dev, width = frames.shape
    tiles_dev = rows_dev // TILE
    ring = [(i, (i + 1) % count) for i in range(count)]
    chunks = [frames]
    for _ in range(count - 1):
        chunks.append(lax.ppermute(chunks[-1], "ctx", ring))
    pairs = [key_value(chunk, key_weight, value_weight) for chunk in chunks]
    shards = lax.rem(me - jnp.arange(count, dtype=jnp.int32) + count, count)
    arrived = (shards[:, None] * tiles_dev + jnp.arange(tiles_dev, dtype=jnp.int32)).reshape(-1)
    key_utt = jnp.sum(
        jnp.where(arrived[:, None] == tile_source[None, :], tile_utt[None, :], 0), axis=1
    )
    key_utt = jnp.repeat(key_utt, TILE).reshape(1, -1)
    return pl.pallas_call(
        functools.partial(ring_kernel, count),
        out_shape=jax.ShapeDtypeStruct((rows_dev, width), jnp.bfloat16),
        in_specs=[SMEM] * 3
        + [VMEM]
        + [pl.BlockSpec(memory_space=pl.ANY)] * count
        + [VMEM] * (2 * count + 5),
        out_specs=VMEM,
        scratch_shapes=block_scratch(rows_dev, width)
        + [pltpu.SemaphoreType.DMA((tiles_dev + 2,))],
        cost_estimate=pl.CostEstimate(
            flops=2 << 30, bytes_accessed=8 << 20, transcendentals=1 << 20
        ),
        name="ring_block",
    )(
        me.reshape(1), tile_source, tile_utt, key_utt, *chunks,
        *[pair[0] for pair in pairs], *[pair[1] for pair in pairs],
        query_weight, output_weight, depth_weight, bn_scale.reshape(1, -1), bn_shift.reshape(1, -1),
    )


COUNT = 4
SWAP_OUTER = [(0, 1), (1, 0), (2, 3), (3, 2)]
SWAP_INNER = [(1, 2), (2, 1)]
TO_ENDS = [(1, 0), (2, 3)]
FROM_ENDS = [(0, 1), (3, 2)]


def quarter_of(source_shard, target):
    return jnp.where(source_shard % 2 == 1, target, COUNT - 1 - target)


def divide(value, by):
    if by & (by - 1) == 0:
        return value >> (by.bit_length() - 1)
    return lax.div(value, by)


def arrange_kernel(
    me_ref, source_hbm, rows_hbm, low_ref, last_ref, high_ref, start_ref, source_ref, rows, slots, sems
):
    me = me_ref[0]
    rows_dev, quarter_rows = rows.shape[0], last_ref.shape[0]
    tiles_dev = rows_dev // TILE
    per_pair = tiles_dev // COUNT
    rows_copy = pltpu.make_async_copy(rows_hbm, rows, sems.at[0])
    source_copy = pltpu.make_async_copy(source_hbm, source_ref, sems.at[1])
    source_copy.start()
    rows_copy.start()
    source_copy.wait()
    for target in range(COUNT):
        place = quarter_of(me, target) * per_pair
        for position in range(target * tiles_dev, (target + 1) * tiles_dev):
            source = source_ref[position]
            shard = divide(source, tiles_dev)
            mine = shard == me
            slots[jnp.where(mine, place, tiles_dev)] = source - shard * tiles_dev
            place = place + mine.astype(jnp.int32)
    rows_copy.wait()
    for place in range(tiles_dev):
        tile = rows[pl.ds(pl.multiple_of(slots[place] * TILE, TILE), TILE), :]
        row = place * TILE
        if row < rows_dev - quarter_rows:
            low_ref[row : row + TILE] = tile
        else:
            row_here = row - (rows_dev - quarter_rows)
            last_ref[row_here : row_here + TILE] = tile
        if row >= quarter_rows:
            high_ref[row - quarter_rows : row - quarter_rows + TILE] = tile
        else:
            start_ref[row : row + TILE] = tile


def hold_kernel(*refs):
    count = (len(refs) - 1) // 2
    sems = refs[-1]
    copies = [
        pltpu.make_async_copy(refs[i], refs[count + i], sems.at[i]) for i in range(count)
    ]
    for copy in copies:
        copy.start()
    for copy in copies:
        copy.wait()


def hold(*arrays):
    return pl.pallas_call(
        hold_kernel,
        out_shape=tuple(jax.ShapeDtypeStruct(a.shape, a.dtype) for a in arrays),
        in_specs=[HBM] * len(arrays),
        out_specs=(VMEM,) * len(arrays),
        scratch_shapes=[pltpu.SemaphoreType.DMA((len(arrays),))],
        compiler_params=params(8),
        cost_estimate=pl.CostEstimate(flops=0, bytes_accessed=8 << 20, transcendentals=0),
        name="hold_call",
    )(*arrays)


def tables_kernel(source_ref, utt_ref, rank_ref, key_utt_ref, filled):
    total = source_ref.shape[0]
    tiles_dev = total // COUNT
    per_pair = tiles_dev // COUNT
    for pair in range(COUNT * COUNT):
        filled[pair] = 0

    def one(position, carried):
        pair = (source_ref[position] // tiles_dev) * COUNT + position // tiles_dev
        rank = filled[pair]
        filled[pair] = rank + 1
        rank_ref[position] = rank
        key_utt_ref[pair * per_pair + rank] = utt_ref[position]
        return carried

    lax.fori_loop(0, total, one, 0, unroll=4)


def held_tiles(me_ref, source_ref, rank_ref, rows_dev):
    me = me_ref[0]
    tiles_dev = rows_dev // TILE
    total = tiles_dev * COUNT
    for i in range(tiles_dev + 2):
        position = jnp.clip(me * tiles_dev - 1 + i, 0, total - 1)
        source = source_ref[position] // tiles_dev
        quarter = quarter_of(source, position // tiles_dev)
        row = quarter * (rows_dev // COUNT) + rank_ref[position] * TILE
        yield i, me ^ source, quarter, row


def early_kernel(
    me_ref, source_ref, rank_ref,
    low, last, high, near, near_last, inner, inner_end,
    key_weight, value_weight, key_ref, value_ref, grouped, rows,
):
    me = me_ref[0]
    is_end = (me == 0) | (me == COUNT - 1)
    rows_dev = high.shape[0] + last.shape[0]
    piece = low.shape[0]
    quarter_rows = last.shape[0]
    rows[0:piece] = low[...]
    rows[piece:rows_dev] = last[...]
    base = rows_dev
    rows[base : base + piece] = near[...]

    @pl.when(is_end)
    def _():
        rows[base + piece : base + 2 * piece] = inner_end[...]

    @pl.when(jnp.logical_not(is_end))
    def _():
        rows[base + piece : base + 2 * piece] = inner[...]

    rows[base + 2 * piece :] = near_last[...]
    for i, apart, quarter, row in held_tiles(me_ref, source_ref, rank_ref, rows_dev):
        second = jnp.where(is_end, 2, 3)
        place = row
        place = jnp.where(
            apart == 1, jnp.where(quarter == 3, base + 2 * piece - 3 * quarter_rows, base) + row, place
        )
        place = jnp.where(apart == second, base + piece - quarter_rows + row, place)

        @pl.when((apart <= 1) | (apart == second))
        def _(i=i, place=place):
            grouped[i * TILE : (i + 1) * TILE] = rows[
                pl.ds(pl.multiple_of(place, TILE), TILE), :
            ]

    normed = layer_norm(rows[...]).astype(jnp.bfloat16)
    key_ref[...] = project(normed, key_weight)
    value_ref[...] = project(normed, value_weight)


def middle_kernel(me_ref, first, second, key_weight, value_weight, key_ref, value_ref):
    rows = jnp.concatenate([first[...], second[...]], axis=0)
    normed = layer_norm(rows).astype(jnp.bfloat16)
    key_ref[...] = project(normed, key_weight)
    value_ref[...] = project(normed, value_weight)


def final_kernel(
    me_ref, source_ref, utt_ref, rank_ref, key_utt_table,
    early_grouped, far, far_end, early_key, early_value, middle_key, middle_value,
    key_weight, value_weight, query_weight, output_weight, taps, scale, shift,
    out_ref, grouped, query_utt, padded, residual_rows, late,
):
    me = me_ref[0]
    is_end = (me == 0) | (me == COUNT - 1)
    rows_dev = out_ref.shape[0]
    tiles_dev = rows_dev // TILE
    total = tiles_dev * COUNT
    first = me * tiles_dev - 1
    per_pair = tiles_dev // COUNT

    @pl.when(is_end)
    def _():
        late[...] = far_end[...]

    @pl.when(jnp.logical_not(is_end))
    def _():
        late[...] = far[...]

    third = jnp.where(is_end, 3, 2)
    for i, apart, _, row in held_tiles(me_ref, source_ref, rank_ref, rows_dev):
        rows_of_tile = slice(i * TILE, (i + 1) * TILE)

        @pl.when(apart == third)
        def _(row=row, rows_of_tile=rows_of_tile):
            grouped[rows_of_tile] = late[pl.ds(pl.multiple_of(row, TILE), TILE), :]

        @pl.when(apart != third)
        def _(rows_of_tile=rows_of_tile):
            grouped[rows_of_tile] = early_grouped[rows_of_tile]

        query_utt[rows_of_tile, :] = jnp.full(
            (TILE, 128), utt_ref[jnp.clip(first + i, 0, total - 1)], jnp.int32
        )
    normed = layer_norm(late[...]).astype(jnp.bfloat16)
    late_key = project(normed, key_weight)
    late_value = project(normed, value_weight)

    near = me ^ 1
    second = me ^ jnp.where(is_end, 2, 3)
    far_shard = me ^ third
    order = [(me, quarter, False) for quarter in (0, 1, 2, 3)]
    order += [(near, quarter, False) for quarter in (0, 1, 2)]
    order += [(second, quarter, False) for quarter in (1, 2, 3)]
    order += [(near, 3, True), (second, 0, True), (far_shard, 3, True)]
    order += [(far_shard, quarter, False) for quarter in (0, 1, 2)]
    lane_tile = lax.broadcasted_iota(jnp.int32, (1, 128), 1) // TILE
    pieces = []
    tile_values = []
    for shard, quarter, inner_only in order:
        target = jnp.where(shard % 2 == 1, quarter, COUNT - 1 - quarter)
        for rank in range(per_pair):
            utt = key_utt_table[(shard * COUNT + target) * per_pair + rank]
            if inner_only:
                utt = jnp.where(is_end, -1, utt)
            tile_values.append(utt)
    per_vector = 128 // TILE
    for start in range(0, len(tile_values), per_vector):
        vector = jnp.full((1, 128), tile_values[start], jnp.int32)
        for k in range(1, per_vector):
            vector = jnp.where(lane_tile == k, tile_values[start + k], vector)
        pieces.append(vector)
    key_utt = jnp.concatenate(pieces, axis=1)
    attend_and_convolve(
        first, total, utt_ref, grouped, query_utt, key_utt,
        [early_key, middle_key, late_key], [early_value, middle_value, late_value],
        query_weight, output_weight, taps, scale, shift, out_ref, padded, residual_rows,
    )


def after(value, other):
    return lax.optimization_barrier((value, other))[0]


def line_block(
    frames, tile_source, tile_utt, query_weight, key_weight, value_weight, output_weight,
    depth_weight, bn_scale, bn_shift,
):
    me = lax.axis_index("ctx").reshape(1)
    rows_dev, width = frames.shape
    quarter = rows_dev // COUNT
    piece = rows_dev - quarter
    total = tile_source.shape[0]
    wide = key_weight.shape[1]

    def shape(rows, columns=width, kind=jnp.bfloat16):
        return jax.ShapeDtypeStruct((rows, columns), kind)

    def cost(rows):
        return pl.CostEstimate(
            flops=4 * rows * width * wide, bytes_accessed=rows * width * 4, transcendentals=rows
        )

    low, last, high, start = pl.pallas_call(
        arrange_kernel,
        out_shape=tuple(pltpu.VMEM((n, width), frames.dtype) for n in (piece, quarter, piece, quarter)),
        in_specs=[SMEM] + [HBM] * 2,
        out_specs=(VMEM,) * 4,
        scratch_shapes=[
            pltpu.SMEM((total,), jnp.int32),
            pltpu.VMEM((rows_dev, width), jnp.bfloat16),
            pltpu.SMEM((rows_dev // TILE + 1,), jnp.int32),
            pltpu.SemaphoreType.DMA((2,)),
        ],
        compiler_params=params(ARRANGE),
        name="arrange",
    )(me, tile_source, frames)

    def swap(value, perm):
        return lax.ppermute(value, "ctx", perm)

    near = swap(low, SWAP_OUTER)
    inner = swap(high, SWAP_INNER)
    rank, key_utt = pl.pallas_call(
        tables_kernel,
        out_shape=(jax.ShapeDtypeStruct((total,), jnp.int32),) * 2,
        in_specs=[SMEM] * 2,
        out_specs=(SMEM, SMEM),
        scratch_shapes=[pltpu.SMEM((COUNT * COUNT,), jnp.int32)],
        compiler_params=params(4),
        name="tables_call",
    )(tile_source, tile_utt)
    key_weight, value_weight, query_weight, output_weight, depth_weight = hold(
        key_weight, value_weight, query_weight, output_weight, depth_weight
    )
    far = swap(near, SWAP_INNER)
    inner_end = swap(inner, TO_ENDS)
    near_last = swap(after(last, near), FROM_ENDS)
    far_end = swap(far, TO_ENDS)
    inner_start = swap(after(start, far), SWAP_INNER)
    far_last = swap(after(near_last, far), SWAP_INNER)

    early_rows = rows_dev + 2 * piece + quarter
    early_key, early_value, grouped = pl.pallas_call(
        early_kernel,
        out_shape=(shape(early_rows, wide), shape(early_rows, wide), shape(rows_dev + 2 * TILE)),
        in_specs=[SMEM] * 3 + [VMEM] * 9,
        out_specs=(VMEM,) * 3,
        scratch_shapes=[pltpu.VMEM((early_rows, width), jnp.bfloat16)],
        compiler_params=params(16),
        cost_estimate=cost(early_rows),
        name="early_call",
    )(
        me, tile_source, rank, low, last, high, near, near_last, inner, inner_end,
        key_weight, value_weight,
    )
    middle_key, middle_value = pl.pallas_call(
        middle_kernel,
        out_shape=(shape(2 * quarter, wide),) * 2,
        in_specs=[SMEM] + [VMEM] * 4,
        out_specs=(VMEM,) * 2,
        compiler_params=params(8),
        cost_estimate=cost(2 * quarter),
        name="middle_call",
    )(me, inner_start, far_last, key_weight, value_weight)
    return pl.pallas_call(
        final_kernel,
        out_shape=shape(rows_dev),
        in_specs=[SMEM] * 5 + [VMEM] * 14,
        out_specs=VMEM,
        scratch_shapes=block_scratch(rows_dev, width) + [pltpu.VMEM((piece, width), jnp.bfloat16)],
        compiler_params=params(28),
        cost_estimate=pl.CostEstimate(
            flops=2 << 30, bytes_accessed=8 << 20, transcendentals=1 << 20
        ),
        name="final",
    )(
        me, tile_source, tile_utt, rank, key_utt,
        grouped, far, far_end, early_key, early_value, middle_key, middle_value,
        key_weight, value_weight, query_weight, output_weight,
        depth_weight, bn_scale.reshape(1, -1), bn_shift.reshape(1, -1),
    )


def per_device(*arrays):
    tiles_dev = arrays[0].shape[0] // TILE
    if lax.axis_size("ctx") == COUNT and tiles_dev % COUNT == 0:
        return line_block(*arrays)
    return ring_block(*arrays)


def solution(mesh):
    return jax.shard_map(
        per_device,
        mesh=mesh,
        in_specs=(P(("dp", "ctx"), None), P("dp"), P("dp"), P(), P(), P(), P(), P(), P(), P()),
        out_specs=P(("dp", "ctx"), None),
        check_vma=False,
    )
```

```python
import functools
import math

import jax
import jax.numpy as jnp
from jax import lax
from jax.experimental import pallas as pl
from jax.experimental.pallas import tpu as pltpu
from jax.sharding import PartitionSpec as P


HEADS = 4
HEAD_DIM = 128
KERNEL = 31
TILE = 16
UTTS = 4
ARRANGE = 56
NEGATIVE = -1e30

VMEM = pl.BlockSpec(memory_space=pltpu.VMEM)
SMEM = pl.BlockSpec(memory_space=pltpu.SMEM)
HBM = pl.BlockSpec(memory_space=pltpu.HBM)


def params(mib):
    return pltpu.CompilerParams(vmem_limit_bytes=mib << 20)


def layer_norm(rows):
    values = rows.astype(jnp.float32)
    center = values - jnp.mean(values, axis=-1, keepdims=True)
    spread = jnp.mean(center * center, axis=-1, keepdims=True)
    return center * lax.rsqrt(spread + 1e-05)


def project(rows, weight_ref):
    return jnp.dot(rows, weight_ref[...], preferred_element_type=jnp.float32).astype(jnp.bfloat16)


def attend_and_convolve(
    first,
    total,
    utt_ref,
    grouped,
    query_utt,
    key_utt,
    key_parts,
    value_parts,
    query_weight,
    output_weight,
    taps,
    scale,
    shift,
    out_ref,
    padded,
    residual_rows,
):
    rows_dev, width = out_ref.shape
    tiles_dev = rows_dev // TILE
    held = tiles_dev + 2

    def tile_at(i):
        return jnp.clip(first + i, 0, total - 1)

    padded[...] = jnp.zeros_like(padded)
    queries = project(layer_norm(grouped[...]).astype(jnp.bfloat16), query_weight)
    allowed = query_utt[:, :1] == key_utt
    exponent_scale = math.log2(math.e) / math.sqrt(HEAD_DIM)
    heads = []
    for head in range(HEADS):
        columns = slice(head * HEAD_DIM, (head + 1) * HEAD_DIM)
        key_head = jnp.concatenate([part[:, columns] for part in key_parts], axis=0)
        value_head = jnp.concatenate([part[:, columns] for part in value_parts], axis=0)
        scores = lax.dot_general(
            queries[:, columns],
            key_head,
            (((1,), (1,)), ((), ())),
            preferred_element_type=jnp.float32,
        )
        scores = jnp.where(allowed, scores, NEGATIVE)
        top = jnp.max(scores, axis=-1, keepdims=True)
        weights = jnp.exp2((scores - top) * exponent_scale)
        row_sum = jnp.sum(weights, axis=-1, keepdims=True)
        summed = jnp.dot(
            weights.astype(jnp.bfloat16), value_head, preferred_element_type=jnp.float32
        )
        heads.append((summed / row_sum).astype(jnp.bfloat16))
    attended = jnp.concatenate(heads, axis=1)
    residual = (
        grouped[...].astype(jnp.float32)
        + jnp.dot(attended, output_weight[...], preferred_element_type=jnp.float32)
    ).astype(jnp.bfloat16)
    residual_rows[...] = residual[TILE : TILE + rows_dev]
    shaped = layer_norm(residual).astype(jnp.bfloat16).astype(jnp.float32)
    places = []
    place = jnp.int32(1)
    for i in range(held):
        if i:
            place = place + 1
            place = place + jnp.where(utt_ref[tile_at(i)] == utt_ref[tile_at(i - 1)], 0, 1)
        inside = (first + i >= 0) & (first + i < total)
        target = jnp.where(inside, place, padded.shape[1] // TILE - 1)
        row = pl.multiple_of(target * TILE, TILE)
        for block in range(width // 128):
            padded[block, pl.ds(row, TILE), :] = shaped[
                i * TILE : (i + 1) * TILE, block * 128 : (block + 1) * 128
            ]
        places.append(place)

    def one_tile(i, place):
        gap = jnp.where(utt_ref[tile_at(i + 1)] == utt_ref[tile_at(i)], 0, 1)
        place = place + 1 + gap
        start = pl.multiple_of(place * TILE, TILE)
        row = pl.multiple_of(i * TILE, TILE)
        for block in range(width // 128):
            columns = slice(block * 128, (block + 1) * 128)
            sums = [None] * 4
            for tap in range(KERNEL):
                term = (
                    padded[block, pl.ds(start + (tap - KERNEL // 2), TILE), :]
                    * taps[tap : tap + 1, columns]
                )
                sums[tap % 4] = term if sums[tap % 4] is None else sums[tap % 4] + term
            convolved = (sums[0] + sums[1]) + (sums[2] + sums[3])
            half = 0.5 * (convolved * scale[:, columns] + shift[:, columns])
            kept = residual_rows[pl.ds(row, TILE), columns].astype(jnp.float32)
            out_ref[pl.ds(row, TILE), columns] = (kept + (half + half * jnp.tanh(half))).astype(
                jnp.bfloat16
            )
        return place

    lax.fori_loop(0, tiles_dev, one_tile, places[0], unroll=2)


def padded_rows(tiles_dev):
    return (1 + tiles_dev + 2 + (UTTS - 1) + 2) * TILE


def block_scratch(rows_dev, width):
    held_rows = rows_dev + 2 * TILE
    return [
        pltpu.VMEM((held_rows, width), jnp.bfloat16),
        pltpu.VMEM((held_rows, 128), jnp.int32),
        pltpu.VMEM((width // 128, padded_rows(rows_dev // TILE), 128), jnp.float32),
        pltpu.VMEM((rows_dev, width), jnp.bfloat16),
    ]


def key_value_kernel(rows_ref, key_weight_ref, value_weight_ref, key_ref, value_ref):
    normed = layer_norm(rows_ref[...]).astype(jnp.bfloat16)
    key_ref[...] = project(normed, key_weight_ref)
    value_ref[...] = project(normed, value_weight_ref)


def key_value(rows, key_weight, value_weight):
    shape = jax.ShapeDtypeStruct((rows.shape[0], key_weight.shape[1]), jnp.bfloat16)
    flops = 4 * rows.shape[0] * rows.shape[1] * key_weight.shape[1]
    return pl.pallas_call(
        key_value_kernel,
        out_shape=(shape, shape),
        in_specs=[VMEM] * 3,
        out_specs=(VMEM, VMEM),
        cost_estimate=pl.CostEstimate(flops=flops, bytes_accessed=3 << 20, transcendentals=0),
        name="key_value",
    )(rows, key_weight, value_weight)


def ring_kernel(count, me_ref, source_ref, utt_ref, key_utt_ref, *refs):
    chunks = refs[:count]
    keys = refs[count : 2 * count]
    values = refs[2 * count : 3 * count]
    weights_and_out = refs[3 * count : 3 * count + 6]
    grouped, query_utt, padded, residual_rows, sems = refs[3 * count + 6 :]
    me = me_ref[0]
    tiles_dev = weights_and_out[-1].shape[0] // TILE
    held = tiles_dev + 2
    total = tiles_dev * count
    first = me * tiles_dev - 1
    for i in range(held):
        position = jnp.clip(first + i, 0, total - 1)
        source = source_ref[position]
        row = pl.multiple_of((source % tiles_dev) * TILE, TILE)
        behind = lax.rem(me - source // tiles_dev + count, count)
        for step in range(count):

            @pl.when(behind == step)
            def _(step=step, row=row, i=i):
                pltpu.make_async_copy(
                    chunks[step].at[pl.ds(row, TILE), :],
                    grouped.at[pl.ds(i * TILE, TILE), :],
                    sems.at[i],
                ).start()

        query_utt[pl.ds(i * TILE, TILE), :] = jnp.full((TILE, 128), utt_ref[position], jnp.int32)
    for i in range(held):
        pltpu.make_async_copy(
            chunks[0].at[pl.ds(0, TILE), :], grouped.at[pl.ds(i * TILE, TILE), :], sems.at[i]
        ).wait()
    attend_and_convolve(
        first, total, utt_ref, grouped, query_utt, key_utt_ref[...], keys, values,
        *weights_and_out, padded, residual_rows,
    )


def ring_block(
    frames, tile_source, tile_utt, query_weight, key_weight, value_weight, output_weight,
    depth_weight, bn_scale, bn_shift,
):
    count = lax.axis_size("ctx")
    me = lax.axis_index("ctx")
    rows_dev, width = frames.shape
    tiles_dev = rows_dev // TILE
    ring = [(i, (i + 1) % count) for i in range(count)]
    chunks = [frames]
    for _ in range(count - 1):
        chunks.append(lax.ppermute(chunks[-1], "ctx", ring))
    pairs = [key_value(chunk, key_weight, value_weight) for chunk in chunks]
    shards = lax.rem(me - jnp.arange(count, dtype=jnp.int32) + count, count)
    arrived = (shards[:, None] * tiles_dev + jnp.arange(tiles_dev, dtype=jnp.int32)).reshape(-1)
    key_utt = jnp.sum(
        jnp.where(arrived[:, None] == tile_source[None, :], tile_utt[None, :], 0), axis=1
    )
    key_utt = jnp.repeat(key_utt, TILE).reshape(1, -1)
    return pl.pallas_call(
        functools.partial(ring_kernel, count),
        out_shape=jax.ShapeDtypeStruct((rows_dev, width), jnp.bfloat16),
        in_specs=[SMEM] * 3
        + [VMEM]
        + [pl.BlockSpec(memory_space=pl.ANY)] * count
        + [VMEM] * (2 * count + 5),
        out_specs=VMEM,
        scratch_shapes=block_scratch(rows_dev, width)
        + [pltpu.SemaphoreType.DMA((tiles_dev + 2,))],
        cost_estimate=pl.CostEstimate(
            flops=2 << 30, bytes_accessed=8 << 20, transcendentals=1 << 20
        ),
        name="ring_block",
    )(
        me.reshape(1), tile_source, tile_utt, key_utt, *chunks,
        *[pair[0] for pair in pairs], *[pair[1] for pair in pairs],
        query_weight, output_weight, depth_weight, bn_scale.reshape(1, -1), bn_shift.reshape(1, -1),
    )


COUNT = 4
SWAP_OUTER = [(0, 1), (1, 0), (2, 3), (3, 2)]
SWAP_INNER = [(1, 2), (2, 1)]
TO_ENDS = [(1, 0), (2, 3)]
FROM_ENDS = [(0, 1), (3, 2)]


def quarter_of(source_shard, target):
    return jnp.where(source_shard % 2 == 1, target, COUNT - 1 - target)


def divide(value, by):
    if by & (by - 1) == 0:
        return value >> (by.bit_length() - 1)
    return lax.div(value, by)


def arrange_kernel(
    me_ref, source_hbm, rows_hbm, low_ref, last_ref, high_ref, start_ref, source_ref, rows, slots, sems
):
    me = me_ref[0]
    rows_dev, quarter_rows = rows.shape[0], last_ref.shape[0]
    tiles_dev = rows_dev // TILE
    per_pair = tiles_dev // COUNT
    rows_copy = pltpu.make_async_copy(rows_hbm, rows, sems.at[0])
    source_copy = pltpu.make_async_copy(source_hbm, source_ref, sems.at[1])
    source_copy.start()
    rows_copy.start()
    source_copy.wait()
    for target in range(COUNT):
        place = quarter_of(me, target) * per_pair
        for position in range(target * tiles_dev, (target + 1) * tiles_dev):
            source = source_ref[position]
            shard = divide(source, tiles_dev)
            mine = shard == me
            slots[jnp.where(mine, place, tiles_dev)] = source - shard * tiles_dev
            place = place + mine.astype(jnp.int32)
    rows_copy.wait()
    for place in range(tiles_dev):
        tile = rows[pl.ds(pl.multiple_of(slots[place] * TILE, TILE), TILE), :]
        row = place * TILE
        if row < rows_dev - quarter_rows:
            low_ref[row : row + TILE] = tile
        else:
            row_here = row - (rows_dev - quarter_rows)
            last_ref[row_here : row_here + TILE] = tile
        if row >= quarter_rows:
            high_ref[row - quarter_rows : row - quarter_rows + TILE] = tile
        else:
            start_ref[row : row + TILE] = tile


def hold_kernel(*refs):
    count = (len(refs) - 1) // 2
    sems = refs[-1]
    copies = [
        pltpu.make_async_copy(refs[i], refs[count + i], sems.at[i]) for i in range(count)
    ]
    for copy in copies:
        copy.start()
    for copy in copies:
        copy.wait()


def hold(*arrays):
    return pl.pallas_call(
        hold_kernel,
        out_shape=tuple(jax.ShapeDtypeStruct(a.shape, a.dtype) for a in arrays),
        in_specs=[HBM] * len(arrays),
        out_specs=(VMEM,) * len(arrays),
        scratch_shapes=[pltpu.SemaphoreType.DMA((len(arrays),))],
        compiler_params=params(8),
        cost_estimate=pl.CostEstimate(flops=0, bytes_accessed=8 << 20, transcendentals=0),
        name="hold_call",
    )(*arrays)


def tables_kernel(source_ref, utt_ref, rank_ref, key_utt_ref, filled):
    total = source_ref.shape[0]
    tiles_dev = total // COUNT
    per_pair = tiles_dev // COUNT
    for pair in range(COUNT * COUNT):
        filled[pair] = 0

    def one(position, carried):
        pair = (source_ref[position] // tiles_dev) * COUNT + position // tiles_dev
        rank = filled[pair]
        filled[pair] = rank + 1
        rank_ref[position] = rank
        key_utt_ref[pair * per_pair + rank] = utt_ref[position]
        return carried

    lax.fori_loop(0, total, one, 0, unroll=4)


def held_tiles(me_ref, source_ref, rank_ref, rows_dev):
    me = me_ref[0]
    tiles_dev = rows_dev // TILE
    total = tiles_dev * COUNT
    for i in range(tiles_dev + 2):
        position = jnp.clip(me * tiles_dev - 1 + i, 0, total - 1)
        source = source_ref[position] // tiles_dev
        quarter = quarter_of(source, position // tiles_dev)
        row = quarter * (rows_dev // COUNT) + rank_ref[position] * TILE
        yield i, me ^ source, quarter, row


def early_kernel(
    me_ref, source_ref, rank_ref,
    low, last, high, near, near_last, inner, inner_end,
    key_weight, value_weight, key_ref, value_ref, grouped, rows,
):
    me = me_ref[0]
    is_end = (me == 0) | (me == COUNT - 1)
    rows_dev = high.shape[0] + last.shape[0]
    piece = low.shape[0]
    quarter_rows = last.shape[0]
    rows[0:piece] = low[...]
    rows[piece:rows_dev] = last[...]
    base = rows_dev
    rows[base : base + piece] = near[...]

    @pl.when(is_end)
    def _():
        rows[base + piece : base + 2 * piece] = inner_end[...]

    @pl.when(jnp.logical_not(is_end))
    def _():
        rows[base + piece : base + 2 * piece] = inner[...]

    rows[base + 2 * piece :] = near_last[...]
    for i, apart, quarter, row in held_tiles(me_ref, source_ref, rank_ref, rows_dev):
        second = jnp.where(is_end, 2, 3)
        place = row
        place = jnp.where(
            apart == 1, jnp.where(quarter == 3, base + 2 * piece - 3 * quarter_rows, base) + row, place
        )
        place = jnp.where(apart == second, base + piece - quarter_rows + row, place)

        @pl.when((apart <= 1) | (apart == second))
        def _(i=i, place=place):
            grouped[i * TILE : (i + 1) * TILE] = rows[
                pl.ds(pl.multiple_of(place, TILE), TILE), :
            ]

    normed = layer_norm(rows[...]).astype(jnp.bfloat16)
    key_ref[...] = project(normed, key_weight)
    value_ref[...] = project(normed, value_weight)


def lay_kernel(first_ref, second_ref, out_ref):
    rows = first_ref.shape[0]
    out_ref[:rows] = first_ref[...]
    out_ref[rows:] = second_ref[...]


def final_kernel(
    me_ref, source_ref, utt_ref, rank_ref, key_utt_table,
    early_grouped, far, far_end, early_key, early_value, middle_key, middle_value,
    key_weight, value_weight, query_weight, output_weight, taps, scale, shift,
    out_ref, grouped, query_utt, padded, residual_rows, late,
):
    me = me_ref[0]
    is_end = (me == 0) | (me == COUNT - 1)
    rows_dev = out_ref.shape[0]
    tiles_dev = rows_dev // TILE
    total = tiles_dev * COUNT
    first = me * tiles_dev - 1
    per_pair = tiles_dev // COUNT

    @pl.when(is_end)
    def _():
        late[...] = far_end[...]

    @pl.when(jnp.logical_not(is_end))
    def _():
        late[...] = far[...]

    third = jnp.where(is_end, 3, 2)
    for i, apart, _, row in held_tiles(me_ref, source_ref, rank_ref, rows_dev):
        rows_of_tile = slice(i * TILE, (i + 1) * TILE)

        @pl.when(apart == third)
        def _(row=row, rows_of_tile=rows_of_tile):
            grouped[rows_of_tile] = late[pl.ds(pl.multiple_of(row, TILE), TILE), :]

        @pl.when(apart != third)
        def _(rows_of_tile=rows_of_tile):
            grouped[rows_of_tile] = early_grouped[rows_of_tile]

        query_utt[rows_of_tile, :] = jnp.full(
            (TILE, 128), utt_ref[jnp.clip(first + i, 0, total - 1)], jnp.int32
        )
    normed = layer_norm(late[...]).astype(jnp.bfloat16)
    late_key = project(normed, key_weight)
    late_value = project(normed, value_weight)

    near = me ^ 1
    second = me ^ jnp.where(is_end, 2, 3)
    far_shard = me ^ third
    order = [(me, quarter, False) for quarter in (0, 1, 2, 3)]
    order += [(near, quarter, False) for quarter in (0, 1, 2)]
    order += [(second, quarter, False) for quarter in (1, 2, 3)]
    order += [(near, 3, True), (second, 0, True), (far_shard, 3, True)]
    order += [(far_shard, quarter, False) for quarter in (0, 1, 2)]
    lane_tile = lax.broadcasted_iota(jnp.int32, (1, 128), 1) // TILE
    pieces = []
    tile_values = []
    for shard, quarter, inner_only in order:
        target = jnp.where(shard % 2 == 1, quarter, COUNT - 1 - quarter)
        for rank in range(per_pair):
            utt = key_utt_table[(shard * COUNT + target) * per_pair + rank]
            if inner_only:
                utt = jnp.where(is_end, -1, utt)
            tile_values.append(utt)
    per_vector = 128 // TILE
    for start in range(0, len(tile_values), per_vector):
        vector = jnp.full((1, 128), tile_values[start], jnp.int32)
        for k in range(1, per_vector):
            vector = jnp.where(lane_tile == k, tile_values[start + k], vector)
        pieces.append(vector)
    key_utt = jnp.concatenate(pieces, axis=1)
    attend_and_convolve(
        first, total, utt_ref, grouped, query_utt, key_utt,
        [early_key, middle_key, late_key], [early_value, middle_value, late_value],
        query_weight, output_weight, taps, scale, shift, out_ref, padded, residual_rows,
    )


def after(value, other):
    return lax.optimization_barrier((value, other))[0]


def line_block(
    frames, tile_source, tile_utt, query_weight, key_weight, value_weight, output_weight,
    depth_weight, bn_scale, bn_shift,
):
    me = lax.axis_index("ctx").reshape(1)
    rows_dev, width = frames.shape
    quarter = rows_dev // COUNT
    piece = rows_dev - quarter
    total = tile_source.shape[0]
    wide = key_weight.shape[1]

    def shape(rows, columns=width, kind=jnp.bfloat16):
        return jax.ShapeDtypeStruct((rows, columns), kind)

    def cost(rows):
        return pl.CostEstimate(
            flops=4 * rows * width * wide, bytes_accessed=rows * width * 4, transcendentals=rows
        )

    low, last, high, start = pl.pallas_call(
        arrange_kernel,
        out_shape=tuple(pltpu.VMEM((n, width), frames.dtype) for n in (piece, quarter, piece, quarter)),
        in_specs=[SMEM] + [HBM] * 2,
        out_specs=(VMEM,) * 4,
        scratch_shapes=[
            pltpu.SMEM((total,), jnp.int32),
            pltpu.VMEM((rows_dev, width), jnp.bfloat16),
            pltpu.SMEM((rows_dev // TILE + 1,), jnp.int32),
            pltpu.SemaphoreType.DMA((2,)),
        ],
        compiler_params=params(ARRANGE),
        name="arrange",
    )(me, tile_source, frames)

    def swap(value, perm):
        return lax.ppermute(value, "ctx", perm)

    near = swap(low, SWAP_OUTER)
    inner = swap(high, SWAP_INNER)
    rank, key_utt = pl.pallas_call(
        tables_kernel,
        out_shape=(jax.ShapeDtypeStruct((total,), jnp.int32),) * 2,
        in_specs=[SMEM] * 2,
        out_specs=(SMEM, SMEM),
        scratch_shapes=[pltpu.SMEM((COUNT * COUNT,), jnp.int32)],
        compiler_params=params(4),
        name="tables_call",
    )(tile_source, tile_utt)
    (
        key_weight, value_weight, query_weight, output_weight, depth_weight, bn_scale, bn_shift
    ) = hold(
        key_weight, value_weight, query_weight, output_weight, depth_weight,
        bn_scale.reshape(1, -1), bn_shift.reshape(1, -1),
    )
    far = swap(near, SWAP_INNER)
    inner_end = swap(inner, TO_ENDS)
    near_last = swap(after(last, near), FROM_ENDS)
    far_end = swap(far, TO_ENDS)
    rest = pl.pallas_call(
        lay_kernel,
        out_shape=shape(2 * quarter),
        in_specs=[VMEM] * 2,
        out_specs=VMEM,
        compiler_params=params(4),
        name="lay_call",
    )(start, near_last)
    rest = swap(after(rest, far), SWAP_INNER)

    early_rows = rows_dev + 2 * piece + quarter
    early_key, early_value, grouped = pl.pallas_call(
        early_kernel,
        out_shape=(shape(early_rows, wide), shape(early_rows, wide), shape(rows_dev + 2 * TILE)),
        in_specs=[SMEM] * 3 + [VMEM] * 9,
        out_specs=(VMEM,) * 3,
        scratch_shapes=[pltpu.VMEM((early_rows, width), jnp.bfloat16)],
        compiler_params=params(16),
        cost_estimate=cost(early_rows),
        name="early_call",
    )(
        me, tile_source, rank, low, last, high, near, near_last, inner, inner_end,
        key_weight, value_weight,
    )
    middle_key, middle_value = pl.pallas_call(
        key_value_kernel,
        out_shape=(shape(2 * quarter, wide),) * 2,
        in_specs=[VMEM] * 3,
        out_specs=(VMEM,) * 2,
        compiler_params=params(8),
        cost_estimate=cost(2 * quarter),
        name="middle_call",
    )(rest, key_weight, value_weight)
    return pl.pallas_call(
        final_kernel,
        out_shape=shape(rows_dev),
        in_specs=[SMEM] * 5 + [VMEM] * 14,
        out_specs=VMEM,
        scratch_shapes=block_scratch(rows_dev, width) + [pltpu.VMEM((piece, width), jnp.bfloat16)],
        compiler_params=params(28),
        cost_estimate=pl.CostEstimate(
            flops=2 << 30, bytes_accessed=8 << 20, transcendentals=1 << 20
        ),
        name="final",
    )(
        me, tile_source, tile_utt, rank, key_utt,
        grouped, far, far_end, early_key, early_value, middle_key, middle_value,
        key_weight, value_weight, query_weight, output_weight, depth_weight, bn_scale, bn_shift,
    )


def per_device(*arrays):
    tiles_dev = arrays[0].shape[0] // TILE
    if lax.axis_size("ctx") == COUNT and tiles_dev % COUNT == 0:
        return line_block(*arrays)
    return ring_block(*arrays)


def solution(mesh):
    return jax.shard_map(
        per_device,
        mesh=mesh,
        in_specs=(P(("dp", "ctx"), None), P("dp"), P("dp"), P(), P(), P(), P(), P(), P(), P()),
        out_specs=P(("dp", "ctx"), None),
        check_vma=False,
    )
```

```python
import functools
import math

import jax
import jax.numpy as jnp
from jax import lax
from jax.experimental import pallas as pl
from jax.experimental.pallas import tpu as pltpu
from jax.sharding import PartitionSpec as P


HEADS = 4
HEAD_DIM = 128
KERNEL = 31
TILE = 16
UTTS = 4
ALONE = 56
NEGATIVE = -1e30

VMEM = pl.BlockSpec(memory_space=pltpu.VMEM)
SMEM = pl.BlockSpec(memory_space=pltpu.SMEM)
HBM = pl.BlockSpec(memory_space=pltpu.HBM)


def params(mib):
    return pltpu.CompilerParams(vmem_limit_bytes=mib << 20)


def layer_norm(rows):
    values = rows.astype(jnp.float32)
    center = values - jnp.mean(values, axis=-1, keepdims=True)
    spread = jnp.mean(center * center, axis=-1, keepdims=True)
    return center * lax.rsqrt(spread + 1e-05)


def project(rows, weight_ref):
    return jnp.dot(rows, weight_ref[...], preferred_element_type=jnp.float32).astype(jnp.bfloat16)


def attend(
    grouped, query_utt, key_utt, key_parts, value_parts, query_weight, output_weight
):
    queries = project(layer_norm(grouped[...]).astype(jnp.bfloat16), query_weight)
    allowed = query_utt[:, :1] == key_utt
    exponent_scale = math.log2(math.e) / math.sqrt(HEAD_DIM)
    heads = []
    for head in range(HEADS):
        columns = slice(head * HEAD_DIM, (head + 1) * HEAD_DIM)
        key_head = jnp.concatenate([part[:, columns] for part in key_parts], axis=0)
        value_head = jnp.concatenate([part[:, columns] for part in value_parts], axis=0)
        scores = lax.dot_general(
            queries[:, columns],
            key_head,
            (((1,), (1,)), ((), ())),
            preferred_element_type=jnp.float32,
        )
        scores = jnp.where(allowed, scores, NEGATIVE)
        top = jnp.max(scores, axis=-1, keepdims=True)
        weights = jnp.exp2((scores - top) * exponent_scale)
        row_sum = jnp.sum(weights, axis=-1, keepdims=True)
        summed = jnp.dot(
            weights.astype(jnp.bfloat16), value_head, preferred_element_type=jnp.float32
        )
        heads.append((summed / row_sum).astype(jnp.bfloat16))
    attended = jnp.concatenate(heads, axis=1)
    return (
        grouped[...].astype(jnp.float32)
        + jnp.dot(attended, output_weight[...], preferred_element_type=jnp.float32)
    ).astype(jnp.bfloat16)


def convolve(residual, plan, at, half_taps, half_shift, out_hbm, padded, residual_rows, out, sems):
    rows_dev, width = out.shape
    tiles_dev = rows_dev // TILE
    held = tiles_dev + 2
    residual_rows[...] = residual[TILE : TILE + rows_dev]
    shaped = layer_norm(residual).astype(jnp.bfloat16).astype(jnp.float32)
    for i in range(held):
        row = pl.multiple_of(plan[at + i] * TILE, TILE)
        for block in range(width // 128):
            padded[block, pl.ds(row, TILE), :] = shaped[
                i * TILE : (i + 1) * TILE, block * 128 : (block + 1) * 128
            ]
    group = math.gcd(tiles_dev, 4)

    def write(step):
        rows = pl.ds(pl.multiple_of(step * group * TILE, TILE), group * TILE)
        return pltpu.make_async_copy(out.at[rows, :], out_hbm.at[rows, :], sems.at[step])

    def some_tiles(step, carried):
        starts = [
            pl.multiple_of(plan[at + held + step * group + k] * TILE, TILE) for k in range(group)
        ]
        for block in range(width // 128):
            columns = slice(block * 128, (block + 1) * 128)
            shift = jnp.broadcast_to(half_shift[:, columns], (8, 128))
            sums = [[shift, shift] for _ in range(group)]
            windows = [{} for _ in range(group)]
            for tap in range(KERNEL):
                weight = half_taps[tap : tap + 1, columns]
                for k in range(group):
                    for part in range(2):
                        offset = tap + 8 * part
                        if offset not in windows[k]:
                            windows[k][offset] = padded[
                                block, pl.ds(starts[k] + (offset - KERNEL // 2), 8), :
                            ]
                        sums[k][part] = sums[k][part] + windows[k][offset] * weight
            for k in range(group):
                half = jnp.concatenate(sums[k], axis=0)
                rows = pl.ds(pl.multiple_of((step * group + k) * TILE, TILE), TILE)
                kept = residual_rows[rows, columns].astype(jnp.float32)
                out[rows, columns] = (kept + (half + half * jnp.tanh(half))).astype(jnp.bfloat16)
        write(step).start()
        return carried

    steps = tiles_dev // group
    lax.fori_loop(0, steps, some_tiles, 0)
    for step in range(steps):
        write(step).wait()


def plan_places(me, utt_ref, tiles_dev, total, plan, at):
    first = me * tiles_dev - 1
    held = tiles_dev + 2
    place = jnp.int32(1)
    before = utt_ref[jnp.clip(first, 0, total - 1)]
    for i in range(held):
        here = utt_ref[jnp.clip(first + i, 0, total - 1)]
        if i:
            place = place + 1 + (here != before).astype(jnp.int32)
        before = here
        inside = (first + i >= 0) & (first + i < total)
        plan[at + i] = jnp.where(inside, place, padded_rows(tiles_dev) // TILE - 1)
        if 1 <= i <= tiles_dev:
            plan[at + held + i - 1] = place


def padded_rows(tiles_dev):
    return (1 + tiles_dev + 2 + (UTTS - 1) + 2) * TILE


def block_scratch(rows_dev, width):
    tiles_dev = rows_dev // TILE
    return [
        pltpu.VMEM((width // 128, padded_rows(tiles_dev), 128), jnp.float32),
        pltpu.VMEM((rows_dev, width), jnp.bfloat16),
        pltpu.VMEM((rows_dev, width), jnp.bfloat16),
        pltpu.SemaphoreType.DMA((tiles_dev // math.gcd(tiles_dev, 4),)),
    ]


def key_value_kernel(rows_ref, key_weight_ref, value_weight_ref, key_ref, value_ref):
    normed = layer_norm(rows_ref[...]).astype(jnp.bfloat16)
    key_ref[...] = project(normed, key_weight_ref)
    value_ref[...] = project(normed, value_weight_ref)


def key_value(rows, key_weight, value_weight):
    shape = jax.ShapeDtypeStruct((rows.shape[0], key_weight.shape[1]), jnp.bfloat16)
    flops = 4 * rows.shape[0] * rows.shape[1] * key_weight.shape[1]
    return pl.pallas_call(
        key_value_kernel,
        out_shape=(shape, shape),
        in_specs=[VMEM] * 3,
        out_specs=(VMEM, VMEM),
        cost_estimate=pl.CostEstimate(flops=flops, bytes_accessed=3 << 20, transcendentals=0),
        name="key_value",
    )(rows, key_weight, value_weight)


def ring_kernel(count, me_ref, source_ref, utt_ref, key_utt_ref, *refs):
    chunks = refs[:count]
    keys = refs[count : 2 * count]
    values = refs[2 * count : 3 * count]
    query_weight, output_weight, taps, scale, shift, out_hbm = refs[3 * count : 3 * count + 6]
    padded, residual_rows, out, write_sems = refs[3 * count + 6 : 3 * count + 10]
    grouped, query_utt, half_taps, plan, sems = refs[3 * count + 10 :]
    me = me_ref[0]
    tiles_dev = out.shape[0] // TILE
    held = tiles_dev + 2
    total = tiles_dev * count
    first = me * tiles_dev - 1
    padded[...] = jnp.zeros_like(padded)
    half_taps[...] = taps[...] * (0.5 * scale[...])
    for i in range(held):
        position = jnp.clip(first + i, 0, total - 1)
        source = source_ref[position]
        row = pl.multiple_of((source % tiles_dev) * TILE, TILE)
        behind = lax.rem(me - source // tiles_dev + count, count)
        for step in range(count):

            @pl.when(behind == step)
            def _(step=step, row=row, i=i):
                pltpu.make_async_copy(
                    chunks[step].at[pl.ds(row, TILE), :],
                    grouped.at[pl.ds(i * TILE, TILE), :],
                    sems.at[i],
                ).start()

        query_utt[pl.ds(i * TILE, TILE), :] = jnp.full((TILE, 128), utt_ref[position], jnp.int32)
    plan_places(me, utt_ref, tiles_dev, total, plan, 0)
    for i in range(held):
        pltpu.make_async_copy(
            chunks[0].at[pl.ds(0, TILE), :], grouped.at[pl.ds(i * TILE, TILE), :], sems.at[i]
        ).wait()
    residual = attend(
        grouped, query_utt, key_utt_ref[...], keys, values, query_weight, output_weight
    )
    convolve(
        residual, plan, 0, half_taps, 0.5 * shift[...], out_hbm, padded, residual_rows, out,
        write_sems,
    )


def ring_block(
    frames, tile_source, tile_utt, query_weight, key_weight, value_weight, output_weight,
    depth_weight, bn_scale, bn_shift,
):
    count = lax.axis_size("ctx")
    me = lax.axis_index("ctx")
    rows_dev, width = frames.shape
    tiles_dev = rows_dev // TILE
    ring = [(i, (i + 1) % count) for i in range(count)]
    chunks = [frames]
    for _ in range(count - 1):
        chunks.append(lax.ppermute(chunks[-1], "ctx", ring))
    pairs = [key_value(chunk, key_weight, value_weight) for chunk in chunks]
    shards = lax.rem(me - jnp.arange(count, dtype=jnp.int32) + count, count)
    arrived = (shards[:, None] * tiles_dev + jnp.arange(tiles_dev, dtype=jnp.int32)).reshape(-1)
    key_utt = jnp.sum(
        jnp.where(arrived[:, None] == tile_source[None, :], tile_utt[None, :], 0), axis=1
    )
    key_utt = jnp.repeat(key_utt, TILE).reshape(1, -1)
    return pl.pallas_call(
        functools.partial(ring_kernel, count),
        out_shape=jax.ShapeDtypeStruct((rows_dev, width), jnp.bfloat16),
        in_specs=[SMEM] * 3
        + [VMEM]
        + [pl.BlockSpec(memory_space=pl.ANY)] * count
        + [VMEM] * (2 * count + 5),
        out_specs=HBM,
        scratch_shapes=block_scratch(rows_dev, width)
        + [
            pltpu.VMEM((rows_dev + 2 * TILE, width), jnp.bfloat16),
            pltpu.VMEM((rows_dev + 2 * TILE, 128), jnp.int32),
            pltpu.VMEM(depth_weight.shape, jnp.float32),
            pltpu.SMEM((2 * tiles_dev + 2,), jnp.int32),
            pltpu.SemaphoreType.DMA((tiles_dev + 2,)),
        ],
        cost_estimate=pl.CostEstimate(
            flops=2 << 30, bytes_accessed=8 << 20, transcendentals=1 << 20
        ),
        name="ring_block",
    )(
        me.reshape(1), tile_source, tile_utt, key_utt, *chunks,
        *[pair[0] for pair in pairs], *[pair[1] for pair in pairs],
        query_weight, output_weight, depth_weight, bn_scale.reshape(1, -1), bn_shift.reshape(1, -1),
    )


COUNT = 4
SWAP_OUTER = [(0, 1), (1, 0), (2, 3), (3, 2)]
SWAP_INNER = [(1, 2), (2, 1)]
TO_ENDS = [(1, 0), (2, 3)]
FROM_ENDS = [(0, 1), (3, 2)]
OVER_TWO = [(0, 2), (3, 1)]


def quarter_of(source_shard, target):
    return jnp.where(source_shard % 2 == 1, target, COUNT - 1 - target)


def divide(value, by):
    if by & (by - 1) == 0:
        return value >> (by.bit_length() - 1)
    return lax.div(value, by)


def arrange_kernel(
    me_ref, source_hbm, rows_hbm, low_ref, last_ref, high_ref, start_ref, source_ref, rows, slots, sems
):
    me = me_ref[0]
    rows_dev, quarter_rows = rows.shape[0], last_ref.shape[0]
    tiles_dev = rows_dev // TILE
    per_pair = tiles_dev // COUNT
    rows_copy = pltpu.make_async_copy(rows_hbm, rows, sems.at[0])
    source_copy = pltpu.make_async_copy(source_hbm, source_ref, sems.at[1])
    source_copy.start()
    rows_copy.start()
    source_copy.wait()
    for target in range(COUNT):
        place = quarter_of(me, target) * per_pair
        for position in range(target * tiles_dev, (target + 1) * tiles_dev):
            source = source_ref[position]
            shard = divide(source, tiles_dev)
            mine = shard == me
            slots[jnp.where(mine, place, tiles_dev)] = source - shard * tiles_dev
            place = place + mine.astype(jnp.int32)
    rows_copy.wait()
    for place in range(tiles_dev):
        tile = rows[pl.ds(pl.multiple_of(slots[place] * TILE, TILE), TILE), :]
        row = place * TILE
        if row < rows_dev - quarter_rows:
            low_ref[row : row + TILE] = tile
        else:
            row_here = row - (rows_dev - quarter_rows)
            last_ref[row_here : row_here + TILE] = tile
        if row >= quarter_rows:
            high_ref[row - quarter_rows : row - quarter_rows + TILE] = tile
        else:
            start_ref[row : row + TILE] = tile


def hold_kernel(*refs):
    count = (len(refs) - 3) // 2
    arrays, kept = refs[:count], refs[count : 2 * count - 1]
    taps, scale, shift, sems = refs[2 * count - 1 :]
    targets = (*kept[:-2], taps, scale, shift)
    copies = [
        pltpu.make_async_copy(array, target, sems.at[i])
        for i, (array, target) in enumerate(zip(arrays, targets))
    ]
    for copy in copies:
        copy.start()
    for copy in copies:
        copy.wait()
    kept[-2][...] = taps[...] * (0.5 * scale[...])
    kept[-1][...] = 0.5 * shift[...]


def hold(*arrays):
    taps, scale, shift = arrays[-3:]
    kept = (*arrays[:-2], shift)
    return pl.pallas_call(
        hold_kernel,
        out_shape=tuple(pltpu.VMEM(a.shape, a.dtype) for a in kept),
        in_specs=[HBM] * len(arrays),
        out_specs=(VMEM,) * len(kept),
        scratch_shapes=[pltpu.VMEM(a.shape, a.dtype) for a in (taps, scale, shift)]
        + [pltpu.SemaphoreType.DMA((len(arrays),))],
        compiler_params=params(ALONE),
        cost_estimate=pl.CostEstimate(flops=0, bytes_accessed=8 << 20, transcendentals=0),
        name="hold_call",
    )(*arrays)


def plan_sizes(tiles_dev):
    held = tiles_dev + 2
    return held, 2 * held, 3 * held + tiles_dev


def tables_kernel(
    me_ref, source_ref, utt_ref, plan_ref, key_utt_ref, query_utt_ref, filled, ranks, key_utts
):
    me = me_ref[0]
    total = source_ref.shape[0]
    tiles_dev = total // COUNT
    per_pair = tiles_dev // COUNT
    quarter_tiles = per_pair
    for pair in range(COUNT * COUNT):
        filled[pair] = 0

    def one(position, carried):
        pair = divide(source_ref[position], tiles_dev) * COUNT + divide(position, tiles_dev)
        rank = filled[pair]
        filled[pair] = rank + 1
        ranks[position] = rank
        key_utts[pair * per_pair + rank] = utt_ref[position]
        return carried

    lax.fori_loop(0, total, one, 0, unroll=4)
    is_end = (me == 0) | (me == COUNT - 1)
    second = jnp.where(is_end, 2, 3)
    third = jnp.where(is_end, 3, 2)
    held, places_at, _ = plan_sizes(tiles_dev)
    for i in range(held):
        position = jnp.clip(me * tiles_dev - 1 + i, 0, total - 1)
        source = divide(source_ref[position], tiles_dev)
        apart = me ^ source
        quarter = quarter_of(source, divide(position, tiles_dev))
        row = quarter * quarter_tiles + ranks[position]
        early = jnp.where(apart == 0, row, -1)
        near = tiles_dev + row + jnp.where(quarter == COUNT - 1, 3 * quarter_tiles, 0)
        early = jnp.where(apart == 1, near, early)
        early = jnp.where(apart == second, tiles_dev + 2 * quarter_tiles + row, early)
        plan_ref[i] = early
        plan_ref[held + i] = jnp.where(apart == third, row, -1)
        query_utt_ref[i * TILE : (i + 1) * TILE] = jnp.full(
            (TILE, 128), utt_ref[position], jnp.int32
        )
    plan_places(me, utt_ref, tiles_dev, total, plan_ref, places_at)

    near, second, far = me ^ 1, me ^ second, me ^ third
    order = [(me, quarter, False) for quarter in (0, 1, 2, 3)]
    order += [(near, quarter, False) for quarter in (0, 1, 2)]
    order += [(second, quarter, False) for quarter in (1, 2, 3)]
    order += [(near, 3, True), (second, 0, True), (far, 3, True)]
    order += [(far, quarter, False) for quarter in (0, 1, 2)]
    lane_tile = lax.broadcasted_iota(jnp.int32, (1, 128), 1) // TILE
    tile_values = []
    for shard, quarter, inner_only in order:
        target = quarter_of(shard, quarter)
        for rank in range(per_pair):
            utt = key_utts[(shard * COUNT + target) * per_pair + rank]
            if inner_only:
                utt = jnp.where(is_end, -1, utt)
            tile_values.append(utt)
    per_vector = 128 // TILE
    for start in range(0, len(tile_values), per_vector):
        vector = jnp.full((1, 128), tile_values[start], jnp.int32)
        for k in range(1, per_vector):
            vector = jnp.where(lane_tile == k, tile_values[start + k], vector)
        key_utt_ref[:, start * TILE : start * TILE + 128] = vector


def early_kernel(
    me_ref, plan, low, last, near, near_last, inner, inner_end,
    key_weight, value_weight, key_ref, value_ref, grouped, rows,
):
    me = me_ref[0]
    is_end = (me == 0) | (me == COUNT - 1)
    piece, quarter_rows = low.shape[0], last.shape[0]
    base = piece + quarter_rows
    rows[0:piece] = low[...]
    rows[piece:base] = last[...]
    rows[base : base + piece] = near[...]

    @pl.when(is_end)
    def _():
        rows[base + piece : base + 2 * piece] = inner_end[...]

    @pl.when(jnp.logical_not(is_end))
    def _():
        rows[base + piece : base + 2 * piece] = inner[...]

    rows[base + 2 * piece :] = near_last[...]
    for i in range(grouped.shape[0] // TILE):
        place = jnp.maximum(plan[i], 0)
        grouped[i * TILE : (i + 1) * TILE] = rows[
            pl.ds(pl.multiple_of(place * TILE, TILE), TILE), :
        ]
    normed = layer_norm(rows[...]).astype(jnp.bfloat16)
    key_ref[...] = project(normed, key_weight)
    value_ref[...] = project(normed, value_weight)


def lay_kernel(first_ref, second_ref, out_ref):
    rows = first_ref.shape[0]
    out_ref[:rows] = first_ref[...]
    out_ref[rows:] = second_ref[...]


def final_kernel(
    me_ref, plan, query_utt, key_utt, early_grouped, far, far_end,
    early_key, early_value, middle_key, middle_value,
    key_weight, value_weight, query_weight, output_weight, half_taps, half_shift,
    out_hbm, grouped, padded, residual_rows, out, write_sems, late,
):
    me = me_ref[0]
    is_end = (me == 0) | (me == COUNT - 1)
    held, places_at, _ = plan_sizes(out.shape[0] // TILE)

    @pl.when(is_end)
    def _():
        late[...] = far_end[...]

    @pl.when(jnp.logical_not(is_end))
    def _():
        late[...] = far[...]

    for i in range(held):
        row = plan[held + i]

        @pl.when(row >= 0)
        def _(row=row, i=i):
            grouped[i * TILE : (i + 1) * TILE] = late[
                pl.ds(pl.multiple_of(row * TILE, TILE), TILE), :
            ]

    padded[...] = jnp.zeros_like(padded)
    normed = layer_norm(late[...]).astype(jnp.bfloat16)
    late_key = project(normed, key_weight)
    late_value = project(normed, value_weight)
    residual = attend(
        grouped, query_utt, key_utt[...],
        [early_key, middle_key, late_key], [early_value, middle_value, late_value],
        query_weight, output_weight,
    )
    convolve(
        residual, plan, places_at, half_taps, half_shift[...], out_hbm, padded, residual_rows,
        out, write_sems,
    )


def after(value, other):
    return lax.optimization_barrier((value, other))[0]


def line_block(
    frames, tile_source, tile_utt, query_weight, key_weight, value_weight, output_weight,
    depth_weight, bn_scale, bn_shift,
):
    me = lax.axis_index("ctx").reshape(1)
    rows_dev, width = frames.shape
    quarter = rows_dev // COUNT
    piece = rows_dev - quarter
    total = tile_source.shape[0]
    wide = key_weight.shape[1]

    def shape(rows, columns=width, kind=jnp.bfloat16):
        return jax.ShapeDtypeStruct((rows, columns), kind)

    def cost(rows):
        return pl.CostEstimate(
            flops=4 * rows * width * wide, bytes_accessed=rows * width * 4, transcendentals=rows
        )

    low, last, high, start = pl.pallas_call(
        arrange_kernel,
        out_shape=tuple(pltpu.VMEM((n, width), frames.dtype) for n in (piece, quarter, piece, quarter)),
        in_specs=[SMEM] + [HBM] * 2,
        out_specs=(VMEM,) * 4,
        scratch_shapes=[
            pltpu.SMEM((total,), jnp.int32),
            pltpu.VMEM((rows_dev, width), jnp.bfloat16),
            pltpu.SMEM((rows_dev // TILE + 1,), jnp.int32),
            pltpu.SemaphoreType.DMA((2,)),
        ],
        compiler_params=params(ALONE),
        name="arrange",
    )(me, tile_source, frames)

    def swap(value, perm):
        return lax.ppermute(value, "ctx", perm)

    near = swap(low, SWAP_OUTER)
    inner = swap(high, SWAP_INNER)
    held_rows = rows_dev + 2 * TILE
    plan, key_utt, query_utt = pl.pallas_call(
        tables_kernel,
        out_shape=(
            jax.ShapeDtypeStruct((plan_sizes(rows_dev // TILE)[2],), jnp.int32),
            shape(1, total * TILE, jnp.int32),
            shape(held_rows, 128, jnp.int32),
        ),
        in_specs=[SMEM] * 3,
        out_specs=(SMEM, VMEM, VMEM),
        scratch_shapes=[pltpu.SMEM((n,), jnp.int32) for n in (COUNT * COUNT, total, total)],
        compiler_params=params(4),
        name="tables_call",
    )(me, tile_source, tile_utt)
    key_weight, value_weight, query_weight, output_weight, half_taps, half_shift = hold(
        key_weight, value_weight, query_weight, output_weight, depth_weight,
        bn_scale.reshape(1, -1), bn_shift.reshape(1, -1),
    )
    far = swap(low, OVER_TWO)
    inner_end = swap(inner, TO_ENDS)
    near_last = swap(after(last, near), FROM_ENDS)
    far_end = swap(far, TO_ENDS)
    rest = pl.pallas_call(
        lay_kernel,
        out_shape=shape(2 * quarter),
        in_specs=[VMEM] * 2,
        out_specs=VMEM,
        compiler_params=params(4),
        name="lay_call",
    )(start, near_last)
    rest = swap(after(rest, far), SWAP_INNER)

    early_rows = rows_dev + 2 * piece + quarter
    early_key, early_value, grouped = pl.pallas_call(
        early_kernel,
        out_shape=(shape(early_rows, wide), shape(early_rows, wide), shape(held_rows)),
        in_specs=[SMEM] * 2 + [VMEM] * 8,
        out_specs=(VMEM,) * 3,
        scratch_shapes=[pltpu.VMEM((early_rows, width), jnp.bfloat16)],
        compiler_params=params(16),
        cost_estimate=cost(early_rows),
        name="early_call",
    )(me, plan, low, last, near, near_last, inner, inner_end, key_weight, value_weight)
    middle_key, middle_value = pl.pallas_call(
        key_value_kernel,
        out_shape=(shape(2 * quarter, wide),) * 2,
        in_specs=[VMEM] * 3,
        out_specs=(VMEM,) * 2,
        compiler_params=params(8),
        cost_estimate=cost(2 * quarter),
        name="middle_call",
    )(rest, key_weight, value_weight)
    return pl.pallas_call(
        final_kernel,
        out_shape=(shape(rows_dev), shape(held_rows)),
        in_specs=[SMEM] * 2 + [VMEM] * 15,
        out_specs=(HBM, VMEM),
        input_output_aliases={4: 1},
        scratch_shapes=block_scratch(rows_dev, width) + [pltpu.VMEM((piece, width), jnp.bfloat16)],
        compiler_params=params(28),
        cost_estimate=pl.CostEstimate(
            flops=2 << 30, bytes_accessed=8 << 20, transcendentals=1 << 20
        ),
        name="final",
    )(
        me, plan, query_utt, key_utt, grouped, far, far_end,
        early_key, early_value, middle_key, middle_value,
        key_weight, value_weight, query_weight, output_weight, half_taps, half_shift,
    )[0]


def per_device(*arrays):
    tiles_dev = arrays[0].shape[0] // TILE
    if lax.axis_size("ctx") == COUNT and tiles_dev % COUNT == 0:
        return line_block(*arrays)
    return ring_block(*arrays)


def solution(mesh):
    return jax.shard_map(
        per_device,
        mesh=mesh,
        in_specs=(P(("dp", "ctx"), None), P("dp"), P("dp"), P(), P(), P(), P(), P(), P(), P()),
        out_specs=P(("dp", "ctx"), None),
        check_vma=False,
    )
```

```python
import functools
import math

import jax
import jax.numpy as jnp
from jax import lax
from jax.experimental import pallas as pl
from jax.experimental.pallas import tpu as pltpu
from jax.sharding import PartitionSpec as P


HEADS = 4
HEAD_DIM = 128
KERNEL = 31
TILE = 16
UTTS = 4
ALONE = 56
NEGATIVE = -1e30

VMEM = pl.BlockSpec(memory_space=pltpu.VMEM)
SMEM = pl.BlockSpec(memory_space=pltpu.SMEM)
HBM = pl.BlockSpec(memory_space=pltpu.HBM)


def params(mib):
    return pltpu.CompilerParams(vmem_limit_bytes=mib << 20)


def layer_norm(rows):
    values = rows.astype(jnp.float32)
    center = values - jnp.mean(values, axis=-1, keepdims=True)
    spread = jnp.mean(center * center, axis=-1, keepdims=True)
    return center * lax.rsqrt(spread + 1e-05)


def project(rows, weight_ref):
    return jnp.dot(rows, weight_ref[...], preferred_element_type=jnp.float32).astype(jnp.bfloat16)


def attend(
    grouped, query_utt, key_utt, key_parts, value_parts, query_weight, output_weight
):
    queries = project(layer_norm(grouped[...]).astype(jnp.bfloat16), query_weight)
    allowed = query_utt[:, :1] == key_utt
    exponent_scale = math.log2(math.e) / math.sqrt(HEAD_DIM)
    heads = []
    for head in range(HEADS):
        columns = slice(head * HEAD_DIM, (head + 1) * HEAD_DIM)
        key_head = jnp.concatenate([part[:, columns] for part in key_parts], axis=0)
        value_head = jnp.concatenate([part[:, columns] for part in value_parts], axis=0)
        scores = lax.dot_general(
            queries[:, columns],
            key_head,
            (((1,), (1,)), ((), ())),
            preferred_element_type=jnp.float32,
        )
        scores = jnp.where(allowed, scores, NEGATIVE)
        top = jnp.max(scores, axis=-1, keepdims=True)
        weights = jnp.exp2((scores - top) * exponent_scale)
        row_sum = jnp.sum(weights, axis=-1, keepdims=True)
        summed = jnp.dot(
            weights.astype(jnp.bfloat16), value_head, preferred_element_type=jnp.float32
        )
        heads.append((summed / row_sum).astype(jnp.bfloat16))
    attended = jnp.concatenate(heads, axis=1)
    return (
        grouped[...].astype(jnp.float32)
        + jnp.dot(attended, output_weight[...], preferred_element_type=jnp.float32)
    ).astype(jnp.bfloat16)


def convolve(residual, plan, at, half_taps, half_shift, out_hbm, padded, residual_rows, out, sems):
    rows_dev, width = out.shape
    tiles_dev = rows_dev // TILE
    held = tiles_dev + 2
    residual_rows[...] = residual[TILE : TILE + rows_dev]
    shaped = layer_norm(residual).astype(jnp.bfloat16).astype(jnp.float32)
    for i in range(held):
        row = pl.multiple_of(plan[at + i] * TILE, TILE)
        for block in range(width // 128):
            padded[block, pl.ds(row, TILE), :] = shaped[
                i * TILE : (i + 1) * TILE, block * 128 : (block + 1) * 128
            ]
    group = math.gcd(tiles_dev, 4)

    def write(step):
        rows = pl.ds(pl.multiple_of(step * group * TILE, TILE), group * TILE)
        return pltpu.make_async_copy(out.at[rows, :], out_hbm.at[rows, :], sems.at[step])

    def some_tiles(step, carried):
        starts = [
            pl.multiple_of(plan[at + held + step * group + k] * TILE, TILE) for k in range(group)
        ]
        for block in range(width // 128):
            columns = slice(block * 128, (block + 1) * 128)
            shift = jnp.broadcast_to(half_shift[:, columns], (8, 128))
            sums = [[shift, shift] for _ in range(group)]
            windows = [{} for _ in range(group)]
            for tap in range(KERNEL):
                weight = half_taps[tap : tap + 1, columns]
                for k in range(group):
                    for part in range(2):
                        offset = tap + 8 * part
                        if offset not in windows[k]:
                            windows[k][offset] = padded[
                                block, pl.ds(starts[k] + (offset - KERNEL // 2), 8), :
                            ]
                        sums[k][part] = sums[k][part] + windows[k][offset] * weight
            for k in range(group):
                half = jnp.concatenate(sums[k], axis=0)
                rows = pl.ds(pl.multiple_of((step * group + k) * TILE, TILE), TILE)
                kept = residual_rows[rows, columns].astype(jnp.float32)
                out[rows, columns] = (kept + (half + half * jnp.tanh(half))).astype(jnp.bfloat16)
        write(step).start()
        return carried

    steps = tiles_dev // group
    lax.fori_loop(0, steps, some_tiles, 0)
    for step in range(steps):
        write(step).wait()


def plan_places(me, utt_ref, tiles_dev, total, plan, at):
    first = me * tiles_dev - 1
    held = tiles_dev + 2
    place = jnp.int32(1)
    before = utt_ref[jnp.clip(first, 0, total - 1)]
    for i in range(held):
        here = utt_ref[jnp.clip(first + i, 0, total - 1)]
        if i:
            place = place + 1 + (here != before).astype(jnp.int32)
        before = here
        inside = (first + i >= 0) & (first + i < total)
        plan[at + i] = jnp.where(inside, place, padded_rows(tiles_dev) // TILE - 1)
        if 1 <= i <= tiles_dev:
            plan[at + held + i - 1] = place


def padded_rows(tiles_dev):
    return (1 + tiles_dev + 2 + (UTTS - 1) + 2) * TILE


def block_scratch(rows_dev, width):
    tiles_dev = rows_dev // TILE
    return [
        pltpu.VMEM((width // 128, padded_rows(tiles_dev), 128), jnp.float32),
        pltpu.VMEM((rows_dev, width), jnp.bfloat16),
        pltpu.VMEM((rows_dev, width), jnp.bfloat16),
        pltpu.SemaphoreType.DMA((tiles_dev // math.gcd(tiles_dev, 4),)),
    ]


def key_value_kernel(rows_ref, key_weight_ref, value_weight_ref, key_ref, value_ref):
    normed = layer_norm(rows_ref[...]).astype(jnp.bfloat16)
    key_ref[...] = project(normed, key_weight_ref)
    value_ref[...] = project(normed, value_weight_ref)


def key_value(rows, key_weight, value_weight):
    shape = jax.ShapeDtypeStruct((rows.shape[0], key_weight.shape[1]), jnp.bfloat16)
    flops = 4 * rows.shape[0] * rows.shape[1] * key_weight.shape[1]
    return pl.pallas_call(
        key_value_kernel,
        out_shape=(shape, shape),
        in_specs=[VMEM] * 3,
        out_specs=(VMEM, VMEM),
        cost_estimate=pl.CostEstimate(flops=flops, bytes_accessed=3 << 20, transcendentals=0),
        name="key_value",
    )(rows, key_weight, value_weight)


def ring_kernel(count, me_ref, source_ref, utt_ref, key_utt_ref, *refs):
    chunks = refs[:count]
    keys = refs[count : 2 * count]
    values = refs[2 * count : 3 * count]
    query_weight, output_weight, taps, scale, shift, out_hbm = refs[3 * count : 3 * count + 6]
    padded, residual_rows, out, write_sems = refs[3 * count + 6 : 3 * count + 10]
    grouped, query_utt, half_taps, plan, sems = refs[3 * count + 10 :]
    me = me_ref[0]
    tiles_dev = out.shape[0] // TILE
    held = tiles_dev + 2
    total = tiles_dev * count
    first = me * tiles_dev - 1
    padded[...] = jnp.zeros_like(padded)
    half_taps[...] = taps[...] * (0.5 * scale[...])
    for i in range(held):
        position = jnp.clip(first + i, 0, total - 1)
        source = source_ref[position]
        row = pl.multiple_of((source % tiles_dev) * TILE, TILE)
        behind = lax.rem(me - source // tiles_dev + count, count)
        for step in range(count):

            @pl.when(behind == step)
            def _(step=step, row=row, i=i):
                pltpu.make_async_copy(
                    chunks[step].at[pl.ds(row, TILE), :],
                    grouped.at[pl.ds(i * TILE, TILE), :],
                    sems.at[i],
                ).start()

        query_utt[pl.ds(i * TILE, TILE), :] = jnp.full((TILE, 128), utt_ref[position], jnp.int32)
    plan_places(me, utt_ref, tiles_dev, total, plan, 0)
    for i in range(held):
        pltpu.make_async_copy(
            chunks[0].at[pl.ds(0, TILE), :], grouped.at[pl.ds(i * TILE, TILE), :], sems.at[i]
        ).wait()
    residual = attend(
        grouped, query_utt, key_utt_ref[...], keys, values, query_weight, output_weight
    )
    convolve(
        residual, plan, 0, half_taps, 0.5 * shift[...], out_hbm, padded, residual_rows, out,
        write_sems,
    )


def ring_block(
    frames, tile_source, tile_utt, query_weight, key_weight, value_weight, output_weight,
    depth_weight, bn_scale, bn_shift,
):
    count = lax.axis_size("ctx")
    me = lax.axis_index("ctx")
    rows_dev, width = frames.shape
    tiles_dev = rows_dev // TILE
    ring = [(i, (i + 1) % count) for i in range(count)]
    chunks = [frames]
    for _ in range(count - 1):
        chunks.append(lax.ppermute(chunks[-1], "ctx", ring))
    pairs = [key_value(chunk, key_weight, value_weight) for chunk in chunks]
    shards = lax.rem(me - jnp.arange(count, dtype=jnp.int32) + count, count)
    arrived = (shards[:, None] * tiles_dev + jnp.arange(tiles_dev, dtype=jnp.int32)).reshape(-1)
    key_utt = jnp.sum(
        jnp.where(arrived[:, None] == tile_source[None, :], tile_utt[None, :], 0), axis=1
    )
    key_utt = jnp.repeat(key_utt, TILE).reshape(1, -1)
    return pl.pallas_call(
        functools.partial(ring_kernel, count),
        out_shape=jax.ShapeDtypeStruct((rows_dev, width), jnp.bfloat16),
        in_specs=[SMEM] * 3
        + [VMEM]
        + [pl.BlockSpec(memory_space=pl.ANY)] * count
        + [VMEM] * (2 * count + 5),
        out_specs=HBM,
        scratch_shapes=block_scratch(rows_dev, width)
        + [
            pltpu.VMEM((rows_dev + 2 * TILE, width), jnp.bfloat16),
            pltpu.VMEM((rows_dev + 2 * TILE, 128), jnp.int32),
            pltpu.VMEM(depth_weight.shape, jnp.float32),
            pltpu.SMEM((2 * tiles_dev + 2,), jnp.int32),
            pltpu.SemaphoreType.DMA((tiles_dev + 2,)),
        ],
        cost_estimate=pl.CostEstimate(
            flops=2 << 30, bytes_accessed=8 << 20, transcendentals=1 << 20
        ),
        name="ring_block",
    )(
        me.reshape(1), tile_source, tile_utt, key_utt, *chunks,
        *[pair[0] for pair in pairs], *[pair[1] for pair in pairs],
        query_weight, output_weight, depth_weight, bn_scale.reshape(1, -1), bn_shift.reshape(1, -1),
    )


COUNT = 4
SWAP_INNER = [(1, 2), (2, 1)]
TO_ENDS = [(1, 0), (2, 3)]
FROM_ENDS = [(0, 1), (3, 2)]
OVER_TWO = [(0, 2), (3, 1)]


def quarter_of(source_shard, target):
    return jnp.where(source_shard % 2 == 1, target, COUNT - 1 - target)


def divide(value, by):
    if by & (by - 1) == 0:
        return value >> (by.bit_length() - 1)
    return lax.div(value, by)


def arrange_kernel(
    me_ref, source_hbm, rows_hbm, whole_ref, low_ref, last_ref, high_ref, start_ref,
    source_ref, rows, slots, sems,
):
    me = me_ref[0]
    rows_dev, quarter_rows = rows.shape[0], last_ref.shape[0]
    tiles_dev = rows_dev // TILE
    per_pair = tiles_dev // COUNT
    rows_copy = pltpu.make_async_copy(rows_hbm, rows, sems.at[0])
    source_copy = pltpu.make_async_copy(source_hbm, source_ref, sems.at[1])
    source_copy.start()
    rows_copy.start()
    source_copy.wait()
    for target in range(COUNT):
        place = quarter_of(me, target) * per_pair
        for position in range(target * tiles_dev, (target + 1) * tiles_dev):
            source = source_ref[position]
            shard = divide(source, tiles_dev)
            mine = shard == me
            slots[jnp.where(mine, place, tiles_dev)] = source - shard * tiles_dev
            place = place + mine.astype(jnp.int32)
    rows_copy.wait()
    for place in range(tiles_dev):
        tile = rows[pl.ds(pl.multiple_of(slots[place] * TILE, TILE), TILE), :]
        row = place * TILE
        whole_ref[row : row + TILE] = tile
        if row < rows_dev - quarter_rows:
            low_ref[row : row + TILE] = tile
        else:
            row_here = row - (rows_dev - quarter_rows)
            last_ref[row_here : row_here + TILE] = tile
        if row >= quarter_rows:
            high_ref[row - quarter_rows : row - quarter_rows + TILE] = tile
        else:
            start_ref[row : row + TILE] = tile


def hold_kernel(*refs):
    count = (len(refs) - 3) // 2
    arrays, kept = refs[:count], refs[count : 2 * count - 1]
    taps, scale, shift, sems = refs[2 * count - 1 :]
    targets = (*kept[:-2], taps, scale, shift)
    copies = [
        pltpu.make_async_copy(array, target, sems.at[i])
        for i, (array, target) in enumerate(zip(arrays, targets))
    ]
    for copy in copies:
        copy.start()
    for copy in copies:
        copy.wait()
    kept[-2][...] = taps[...] * (0.5 * scale[...])
    kept[-1][...] = 0.5 * shift[...]


def hold(*arrays):
    taps, scale, shift = arrays[-3:]
    kept = (*arrays[:-2], shift)
    return pl.pallas_call(
        hold_kernel,
        out_shape=tuple(pltpu.VMEM(a.shape, a.dtype) for a in kept),
        in_specs=[HBM] * len(arrays),
        out_specs=(VMEM,) * len(kept),
        scratch_shapes=[pltpu.VMEM(a.shape, a.dtype) for a in (taps, scale, shift)]
        + [pltpu.SemaphoreType.DMA((len(arrays),))],
        compiler_params=params(ALONE),
        cost_estimate=pl.CostEstimate(flops=0, bytes_accessed=8 << 20, transcendentals=0),
        name="hold_call",
    )(*arrays)


def plan_sizes(tiles_dev):
    held = tiles_dev + 2
    return held, 2 * held, 3 * held + tiles_dev


def tables_kernel(
    me_ref, source_ref, utt_ref, plan_ref, key_utt_ref, query_utt_ref, filled, ranks, key_utts
):
    me = me_ref[0]
    total = source_ref.shape[0]
    tiles_dev = total // COUNT
    per_pair = tiles_dev // COUNT
    quarter_tiles = per_pair
    for pair in range(COUNT * COUNT):
        filled[pair] = 0

    def one(position, carried):
        pair = divide(source_ref[position], tiles_dev) * COUNT + divide(position, tiles_dev)
        rank = filled[pair]
        filled[pair] = rank + 1
        ranks[position] = rank
        key_utts[pair * per_pair + rank] = utt_ref[position]
        return carried

    lax.fori_loop(0, total, one, 0, unroll=4)
    is_end = (me == 0) | (me == COUNT - 1)
    second = jnp.where(is_end, 2, 3)
    third = jnp.where(is_end, 3, 2)
    held, places_at, _ = plan_sizes(tiles_dev)
    for i in range(held):
        position = jnp.clip(me * tiles_dev - 1 + i, 0, total - 1)
        source = divide(source_ref[position], tiles_dev)
        apart = me ^ source
        quarter = quarter_of(source, divide(position, tiles_dev))
        row = quarter * quarter_tiles + ranks[position]
        early = jnp.where(apart == 0, row, -1)
        near = tiles_dev + row + jnp.where(quarter == COUNT - 1, 3 * quarter_tiles, 0)
        early = jnp.where(apart == 1, near, early)
        early = jnp.where(apart == second, tiles_dev + 2 * quarter_tiles + row, early)
        plan_ref[i] = early
        plan_ref[held + i] = jnp.where(apart == third, row, -1)
        query_utt_ref[i * TILE : (i + 1) * TILE] = jnp.full(
            (TILE, 128), utt_ref[position], jnp.int32
        )
    plan_places(me, utt_ref, tiles_dev, total, plan_ref, places_at)

    near, second, far = me ^ 1, me ^ second, me ^ third
    order = [(me, quarter, False) for quarter in (0, 1, 2, 3)]
    order += [(near, quarter, False) for quarter in (0, 1, 2)]
    order += [(second, quarter, False) for quarter in (1, 2, 3)]
    order += [(near, 3, True), (second, 0, True), (far, 3, True)]
    order += [(far, quarter, False) for quarter in (0, 1, 2)]
    lane_tile = lax.broadcasted_iota(jnp.int32, (1, 128), 1) // TILE
    tile_values = []
    for shard, quarter, inner_only in order:
        target = quarter_of(shard, quarter)
        for rank in range(per_pair):
            utt = key_utts[(shard * COUNT + target) * per_pair + rank]
            if inner_only:
                utt = jnp.where(is_end, -1, utt)
            tile_values.append(utt)
    per_vector = 128 // TILE
    for start in range(0, len(tile_values), per_vector):
        vector = jnp.full((1, 128), tile_values[start], jnp.int32)
        for k in range(1, per_vector):
            vector = jnp.where(lane_tile == k, tile_values[start + k], vector)
        key_utt_ref[:, start * TILE : start * TILE + 128] = vector


def early_kernel(
    me_ref, plan, whole, near_in, near_out, inner, inner_end,
    key_weight, value_weight, key_ref, value_ref, grouped, rows,
):
    me = me_ref[0]
    is_end = (me == 0) | (me == COUNT - 1)
    base, piece = whole.shape[0], near_in.shape[0]
    rows[0:base] = whole[...]

    @pl.when(is_end)
    def _():
        rows[base : base + piece] = near_in[...]
        rows[base + piece : base + 2 * piece] = inner_end[...]
        rows[base + 2 * piece :] = jnp.zeros((base - piece, rows.shape[1]), rows.dtype)

    @pl.when(jnp.logical_not(is_end))
    def _():
        rows[base : base + piece] = near_out[:piece]
        rows[base + piece : base + 2 * piece] = inner[...]
        rows[base + 2 * piece :] = near_out[piece:]

    for i in range(grouped.shape[0] // TILE):
        place = jnp.maximum(plan[i], 0)
        grouped[i * TILE : (i + 1) * TILE] = rows[
            pl.ds(pl.multiple_of(place * TILE, TILE), TILE), :
        ]
    normed = layer_norm(rows[...]).astype(jnp.bfloat16)
    key_ref[...] = project(normed, key_weight)
    value_ref[...] = project(normed, value_weight)


def middle_kernel(first, second, key_weight_ref, value_weight_ref, key_ref, value_ref):
    normed = layer_norm(jnp.concatenate([first[...], second[...]], axis=0)).astype(jnp.bfloat16)
    key_ref[...] = project(normed, key_weight_ref)
    value_ref[...] = project(normed, value_weight_ref)


def final_kernel(
    me_ref, plan, query_utt, key_utt, early_grouped, far, far_end,
    early_key, early_value, middle_key, middle_value,
    key_weight, value_weight, query_weight, output_weight, half_taps, half_shift,
    out_hbm, grouped, padded, residual_rows, out, write_sems, late,
):
    me = me_ref[0]
    is_end = (me == 0) | (me == COUNT - 1)
    held, places_at, _ = plan_sizes(out.shape[0] // TILE)

    @pl.when(is_end)
    def _():
        late[...] = far_end[...]

    @pl.when(jnp.logical_not(is_end))
    def _():
        late[...] = far[...]

    for i in range(held):
        row = plan[held + i]

        @pl.when(row >= 0)
        def _(row=row, i=i):
            grouped[i * TILE : (i + 1) * TILE] = late[
                pl.ds(pl.multiple_of(row * TILE, TILE), TILE), :
            ]

    padded[...] = jnp.zeros_like(padded)
    normed = layer_norm(late[...]).astype(jnp.bfloat16)
    late_key = project(normed, key_weight)
    late_value = project(normed, value_weight)
    residual = attend(
        grouped, query_utt, key_utt[...],
        [early_key, middle_key, late_key], [early_value, middle_value, late_value],
        query_weight, output_weight,
    )
    convolve(
        residual, plan, places_at, half_taps, half_shift[...], out_hbm, padded, residual_rows,
        out, write_sems,
    )


def line_block(
    frames, tile_source, tile_utt, query_weight, key_weight, value_weight, output_weight,
    depth_weight, bn_scale, bn_shift,
):
    me = lax.axis_index("ctx").reshape(1)
    rows_dev, width = frames.shape
    quarter = rows_dev // COUNT
    piece = rows_dev - quarter
    total = tile_source.shape[0]
    wide = key_weight.shape[1]

    def shape(rows, columns=width, kind=jnp.bfloat16):
        return jax.ShapeDtypeStruct((rows, columns), kind)

    def cost(rows):
        return pl.CostEstimate(
            flops=4 * rows * width * wide, bytes_accessed=rows * width * 4, transcendentals=rows
        )

    whole, low, last, high, start = pl.pallas_call(
        arrange_kernel,
        out_shape=tuple(pltpu.VMEM((n, width), frames.dtype) for n in (rows_dev, piece, quarter, piece, quarter)),
        in_specs=[SMEM] + [HBM] * 2,
        out_specs=(VMEM,) * 5,
        scratch_shapes=[
            pltpu.SMEM((total,), jnp.int32),
            pltpu.VMEM((rows_dev, width), jnp.bfloat16),
            pltpu.SMEM((rows_dev // TILE + 1,), jnp.int32),
            pltpu.SemaphoreType.DMA((2,)),
        ],
        compiler_params=params(ALONE),
        name="arrange",
    )(me, tile_source, frames)

    def swap(value, perm):
        return lax.ppermute(value, "ctx", perm)

    near_in = swap(low, TO_ENDS)
    inner = swap(high, SWAP_INNER)
    held_rows = rows_dev + 2 * TILE
    plan, key_utt, query_utt = pl.pallas_call(
        tables_kernel,
        out_shape=(
            jax.ShapeDtypeStruct((plan_sizes(rows_dev // TILE)[2],), jnp.int32),
            shape(1, total * TILE, jnp.int32),
            shape(held_rows, 128, jnp.int32),
        ),
        in_specs=[SMEM] * 3,
        out_specs=(SMEM, VMEM, VMEM),
        scratch_shapes=[pltpu.SMEM((n,), jnp.int32) for n in (COUNT * COUNT, total, total)],
        compiler_params=params(4),
        name="tables_call",
    )(me, tile_source, tile_utt)
    key_weight, value_weight, query_weight, output_weight, half_taps, half_shift = hold(
        key_weight, value_weight, query_weight, output_weight, depth_weight,
        bn_scale.reshape(1, -1), bn_shift.reshape(1, -1),
    )
    far = swap(low, OVER_TWO)
    inner_end = swap(inner, TO_ENDS)
    near_out = swap(whole, FROM_ENDS)
    far_end = swap(far, TO_ENDS)
    inner_start = swap(start, SWAP_INNER)
    far_last = swap(last, OVER_TWO)

    early_rows = rows_dev + 2 * piece + quarter
    early_key, early_value, grouped = pl.pallas_call(
        early_kernel,
        out_shape=(shape(early_rows, wide), shape(early_rows, wide), shape(held_rows)),
        in_specs=[SMEM] * 2 + [VMEM] * 7,
        out_specs=(VMEM,) * 3,
        scratch_shapes=[pltpu.VMEM((early_rows, width), jnp.bfloat16)],
        compiler_params=params(16),
        cost_estimate=cost(early_rows),
        name="early_call",
    )(me, plan, whole, near_in, near_out, inner, inner_end, key_weight, value_weight)
    middle_key, middle_value = pl.pallas_call(
        middle_kernel,
        out_shape=(shape(2 * quarter, wide),) * 2,
        in_specs=[VMEM] * 4,
        out_specs=(VMEM,) * 2,
        compiler_params=params(8),
        cost_estimate=cost(2 * quarter),
        name="middle_call",
    )(inner_start, far_last, key_weight, value_weight)
    return pl.pallas_call(
        final_kernel,
        out_shape=(shape(rows_dev), shape(held_rows)),
        in_specs=[SMEM] * 2 + [VMEM] * 15,
        out_specs=(HBM, VMEM),
        input_output_aliases={4: 1},
        scratch_shapes=block_scratch(rows_dev, width) + [pltpu.VMEM((piece, width), jnp.bfloat16)],
        compiler_params=params(28),
        cost_estimate=pl.CostEstimate(
            flops=2 << 30, bytes_accessed=8 << 20, transcendentals=1 << 20
        ),
        name="final",
    )(
        me, plan, query_utt, key_utt, grouped, far, far_end,
        early_key, early_value, middle_key, middle_value,
        key_weight, value_weight, query_weight, output_weight, half_taps, half_shift,
    )[0]


def per_device(*arrays):
    tiles_dev = arrays[0].shape[0] // TILE
    if lax.axis_size("ctx") == COUNT and tiles_dev % COUNT == 0:
        return line_block(*arrays)
    return ring_block(*arrays)


def solution(mesh):
    return jax.shard_map(
        per_device,
        mesh=mesh,
        in_specs=(P(("dp", "ctx"), None), P("dp"), P("dp"), P(), P(), P(), P(), P(), P(), P()),
        out_specs=P(("dp", "ctx"), None),
        check_vma=False,
    )
```

```python
import functools
import math

import jax
import jax.numpy as jnp
from jax import lax
from jax.experimental import pallas as pl
from jax.experimental.pallas import tpu as pltpu
from jax.sharding import PartitionSpec as P


HEADS = 4
HEAD_DIM = 128
KERNEL = 31
TILE = 16
UTTS = 4
ALONE = 56
NEGATIVE = -1e30

VMEM = pl.BlockSpec(memory_space=pltpu.VMEM)
SMEM = pl.BlockSpec(memory_space=pltpu.SMEM)
HBM = pl.BlockSpec(memory_space=pltpu.HBM)


def params(mib):
    return pltpu.CompilerParams(vmem_limit_bytes=mib << 20)


def layer_norm(rows):
    values = rows.astype(jnp.float32)
    center = values - jnp.mean(values, axis=-1, keepdims=True)
    spread = jnp.mean(center * center, axis=-1, keepdims=True)
    return center * lax.rsqrt(spread + 1e-05)


def project(rows, weight_ref):
    return jnp.dot(rows, weight_ref[...], preferred_element_type=jnp.float32).astype(jnp.bfloat16)


def attend(
    grouped, query_utt, key_utt, key_parts, value_parts, query_weight, output_weight
):
    queries = project(layer_norm(grouped[...]).astype(jnp.bfloat16), query_weight)
    allowed = query_utt[:, :1] == key_utt
    exponent_scale = math.log2(math.e) / math.sqrt(HEAD_DIM)
    heads = []
    for head in range(HEADS):
        columns = slice(head * HEAD_DIM, (head + 1) * HEAD_DIM)
        key_head = jnp.concatenate([part[:, columns] for part in key_parts], axis=0)
        value_head = jnp.concatenate([part[:, columns] for part in value_parts], axis=0)
        scores = lax.dot_general(
            queries[:, columns],
            key_head,
            (((1,), (1,)), ((), ())),
            preferred_element_type=jnp.float32,
        )
        scores = jnp.where(allowed, scores, NEGATIVE)
        top = jnp.max(scores, axis=-1, keepdims=True)
        weights = jnp.exp2((scores - top) * exponent_scale)
        row_sum = jnp.sum(weights, axis=-1, keepdims=True)
        summed = jnp.dot(
            weights.astype(jnp.bfloat16), value_head, preferred_element_type=jnp.float32
        )
        heads.append((summed / row_sum).astype(jnp.bfloat16))
    attended = jnp.concatenate(heads, axis=1)
    return (
        grouped[...].astype(jnp.float32)
        + jnp.dot(attended, output_weight[...], preferred_element_type=jnp.float32)
    ).astype(jnp.bfloat16)


def convolve(residual, plan, at, half_taps, half_shift, out_hbm, padded, residual_rows, out, sems):
    rows_dev, width = out.shape
    tiles_dev = rows_dev // TILE
    held = tiles_dev + 2
    residual_rows[...] = residual[TILE : TILE + rows_dev]
    shaped = layer_norm(residual).astype(jnp.bfloat16).astype(jnp.float32)
    for i in range(held):
        row = pl.multiple_of(plan[at + i] * TILE, TILE)
        for block in range(width // 128):
            padded[block, pl.ds(row, TILE), :] = shaped[
                i * TILE : (i + 1) * TILE, block * 128 : (block + 1) * 128
            ]
    group = math.gcd(tiles_dev, 4)

    def write(step):
        rows = pl.ds(pl.multiple_of(step * group * TILE, TILE), group * TILE)
        return pltpu.make_async_copy(out.at[rows, :], out_hbm.at[rows, :], sems.at[step])

    def some_tiles(step, carried):
        starts = [
            pl.multiple_of(plan[at + held + step * group + k] * TILE, TILE) for k in range(group)
        ]
        for block in range(width // 128):
            columns = slice(block * 128, (block + 1) * 128)
            shift = jnp.broadcast_to(half_shift[:, columns], (8, 128))
            sums = [[shift, shift] for _ in range(group)]
            windows = [{} for _ in range(group)]
            for tap in range(KERNEL):
                weight = half_taps[tap : tap + 1, columns]
                for k in range(group):
                    for part in range(2):
                        offset = tap + 8 * part
                        if offset not in windows[k]:
                            windows[k][offset] = padded[
                                block, pl.ds(starts[k] + (offset - KERNEL // 2), 8), :
                            ]
                        sums[k][part] = sums[k][part] + windows[k][offset] * weight
            for k in range(group):
                half = jnp.concatenate(sums[k], axis=0)
                rows = pl.ds(pl.multiple_of((step * group + k) * TILE, TILE), TILE)
                kept = residual_rows[rows, columns].astype(jnp.float32)
                out[rows, columns] = (kept + (half + half * jnp.tanh(half))).astype(jnp.bfloat16)
        write(step).start()
        return carried

    steps = tiles_dev // group
    lax.fori_loop(0, steps, some_tiles, 0)
    for step in range(steps):
        write(step).wait()


def plan_places(me, utt_ref, tiles_dev, total, plan, at):
    first = me * tiles_dev - 1
    held = tiles_dev + 2
    place = jnp.int32(1)
    before = utt_ref[jnp.clip(first, 0, total - 1)]
    for i in range(held):
        here = utt_ref[jnp.clip(first + i, 0, total - 1)]
        if i:
            place = place + 1 + (here != before).astype(jnp.int32)
        before = here
        inside = (first + i >= 0) & (first + i < total)
        plan[at + i] = jnp.where(inside, place, padded_rows(tiles_dev) // TILE - 1)
        if 1 <= i <= tiles_dev:
            plan[at + held + i - 1] = place


def padded_rows(tiles_dev):
    return (1 + tiles_dev + 2 + (UTTS - 1) + 2) * TILE


def block_scratch(rows_dev, width):
    tiles_dev = rows_dev // TILE
    return [
        pltpu.VMEM((width // 128, padded_rows(tiles_dev), 128), jnp.float32),
        pltpu.VMEM((rows_dev, width), jnp.bfloat16),
        pltpu.VMEM((rows_dev, width), jnp.bfloat16),
        pltpu.SemaphoreType.DMA((tiles_dev // math.gcd(tiles_dev, 4),)),
    ]


def key_value_kernel(rows_ref, key_weight_ref, value_weight_ref, key_ref, value_ref):
    normed = layer_norm(rows_ref[...]).astype(jnp.bfloat16)
    key_ref[...] = project(normed, key_weight_ref)
    value_ref[...] = project(normed, value_weight_ref)


def key_value(rows, key_weight, value_weight):
    shape = jax.ShapeDtypeStruct((rows.shape[0], key_weight.shape[1]), jnp.bfloat16)
    flops = 4 * rows.shape[0] * rows.shape[1] * key_weight.shape[1]
    return pl.pallas_call(
        key_value_kernel,
        out_shape=(shape, shape),
        in_specs=[VMEM] * 3,
        out_specs=(VMEM, VMEM),
        cost_estimate=pl.CostEstimate(flops=flops, bytes_accessed=3 << 20, transcendentals=0),
        name="key_value",
    )(rows, key_weight, value_weight)


def ring_kernel(count, me_ref, source_ref, utt_ref, key_utt_ref, *refs):
    chunks = refs[:count]
    keys = refs[count : 2 * count]
    values = refs[2 * count : 3 * count]
    query_weight, output_weight, taps, scale, shift, out_hbm = refs[3 * count : 3 * count + 6]
    padded, residual_rows, out, write_sems = refs[3 * count + 6 : 3 * count + 10]
    grouped, query_utt, half_taps, plan, sems = refs[3 * count + 10 :]
    me = me_ref[0]
    tiles_dev = out.shape[0] // TILE
    held = tiles_dev + 2
    total = tiles_dev * count
    first = me * tiles_dev - 1
    padded[...] = jnp.zeros_like(padded)
    half_taps[...] = taps[...] * (0.5 * scale[...])
    for i in range(held):
        position = jnp.clip(first + i, 0, total - 1)
        source = source_ref[position]
        row = pl.multiple_of((source % tiles_dev) * TILE, TILE)
        behind = lax.rem(me - source // tiles_dev + count, count)
        for step in range(count):

            @pl.when(behind == step)
            def _(step=step, row=row, i=i):
                pltpu.make_async_copy(
                    chunks[step].at[pl.ds(row, TILE), :],
                    grouped.at[pl.ds(i * TILE, TILE), :],
                    sems.at[i],
                ).start()

        query_utt[pl.ds(i * TILE, TILE), :] = jnp.full((TILE, 128), utt_ref[position], jnp.int32)
    plan_places(me, utt_ref, tiles_dev, total, plan, 0)
    for i in range(held):
        pltpu.make_async_copy(
            chunks[0].at[pl.ds(0, TILE), :], grouped.at[pl.ds(i * TILE, TILE), :], sems.at[i]
        ).wait()
    residual = attend(
        grouped, query_utt, key_utt_ref[...], keys, values, query_weight, output_weight
    )
    convolve(
        residual, plan, 0, half_taps, 0.5 * shift[...], out_hbm, padded, residual_rows, out,
        write_sems,
    )


def ring_block(
    frames, tile_source, tile_utt, query_weight, key_weight, value_weight, output_weight,
    depth_weight, bn_scale, bn_shift,
):
    count = lax.axis_size("ctx")
    me = lax.axis_index("ctx")
    rows_dev, width = frames.shape
    tiles_dev = rows_dev // TILE
    ring = [(i, (i + 1) % count) for i in range(count)]
    chunks = [frames]
    for _ in range(count - 1):
        chunks.append(lax.ppermute(chunks[-1], "ctx", ring))
    pairs = [key_value(chunk, key_weight, value_weight) for chunk in chunks]
    shards = lax.rem(me - jnp.arange(count, dtype=jnp.int32) + count, count)
    arrived = (shards[:, None] * tiles_dev + jnp.arange(tiles_dev, dtype=jnp.int32)).reshape(-1)
    key_utt = jnp.sum(
        jnp.where(arrived[:, None] == tile_source[None, :], tile_utt[None, :], 0), axis=1
    )
    key_utt = jnp.repeat(key_utt, TILE).reshape(1, -1)
    return pl.pallas_call(
        functools.partial(ring_kernel, count),
        out_shape=jax.ShapeDtypeStruct((rows_dev, width), jnp.bfloat16),
        in_specs=[SMEM] * 3
        + [VMEM]
        + [pl.BlockSpec(memory_space=pl.ANY)] * count
        + [VMEM] * (2 * count + 5),
        out_specs=HBM,
        scratch_shapes=block_scratch(rows_dev, width)
        + [
            pltpu.VMEM((rows_dev + 2 * TILE, width), jnp.bfloat16),
            pltpu.VMEM((rows_dev + 2 * TILE, 128), jnp.int32),
            pltpu.VMEM(depth_weight.shape, jnp.float32),
            pltpu.SMEM((2 * tiles_dev + 2,), jnp.int32),
            pltpu.SemaphoreType.DMA((tiles_dev + 2,)),
        ],
        cost_estimate=pl.CostEstimate(
            flops=2 << 30, bytes_accessed=8 << 20, transcendentals=1 << 20
        ),
        name="ring_block",
    )(
        me.reshape(1), tile_source, tile_utt, key_utt, *chunks,
        *[pair[0] for pair in pairs], *[pair[1] for pair in pairs],
        query_weight, output_weight, depth_weight, bn_scale.reshape(1, -1), bn_shift.reshape(1, -1),
    )


COUNT = 4
SWAP_OUTER = [(0, 1), (1, 0), (2, 3), (3, 2)]
SWAP_INNER = [(1, 2), (2, 1)]
TO_ENDS = [(1, 0), (2, 3)]
FROM_ENDS = [(0, 1), (3, 2)]
OVER_TWO = [(0, 2), (3, 1)]


def quarter_of(source_shard, target):
    return jnp.where(source_shard % 2 == 1, target, COUNT - 1 - target)


def divide(value, by):
    if by & (by - 1) == 0:
        return value >> (by.bit_length() - 1)
    return lax.div(value, by)


def arrange_kernel(
    me_ref, source_hbm, rows_hbm, low_ref, last_ref, high_ref, start_ref, source_ref, rows, slots, sems
):
    me = me_ref[0]
    rows_dev, quarter_rows = rows.shape[0], last_ref.shape[0]
    tiles_dev = rows_dev // TILE
    per_pair = tiles_dev // COUNT
    rows_copy = pltpu.make_async_copy(rows_hbm, rows, sems.at[0])
    source_copy = pltpu.make_async_copy(source_hbm, source_ref, sems.at[1])
    source_copy.start()
    rows_copy.start()
    source_copy.wait()
    for target in range(COUNT):
        place = quarter_of(me, target) * per_pair
        for position in range(target * tiles_dev, (target + 1) * tiles_dev):
            source = source_ref[position]
            shard = divide(source, tiles_dev)
            mine = shard == me
            slots[jnp.where(mine, place, tiles_dev)] = source - shard * tiles_dev
            place = place + mine.astype(jnp.int32)
    rows_copy.wait()
    for place in range(tiles_dev):
        tile = rows[pl.ds(pl.multiple_of(slots[place] * TILE, TILE), TILE), :]
        row = place * TILE
        if row < rows_dev - quarter_rows:
            low_ref[row : row + TILE] = tile
        else:
            row_here = row - (rows_dev - quarter_rows)
            last_ref[row_here : row_here + TILE] = tile
        if row >= quarter_rows:
            high_ref[row - quarter_rows : row - quarter_rows + TILE] = tile
        else:
            start_ref[row : row + TILE] = tile


def hold_kernel(*refs):
    count = (len(refs) - 3) // 2
    arrays, kept = refs[:count], refs[count : 2 * count - 1]
    taps, scale, shift, sems = refs[2 * count - 1 :]
    targets = (*kept[:-2], taps, scale, shift)
    copies = [
        pltpu.make_async_copy(array, target, sems.at[i])
        for i, (array, target) in enumerate(zip(arrays, targets))
    ]
    for copy in copies:
        copy.start()
    for copy in copies:
        copy.wait()
    kept[-2][...] = taps[...] * (0.5 * scale[...])
    kept[-1][...] = 0.5 * shift[...]


def hold(*arrays):
    taps, scale, shift = arrays[-3:]
    kept = (*arrays[:-2], shift)
    return pl.pallas_call(
        hold_kernel,
        out_shape=tuple(pltpu.VMEM(a.shape, a.dtype) for a in kept),
        in_specs=[HBM] * len(arrays),
        out_specs=(VMEM,) * len(kept),
        scratch_shapes=[pltpu.VMEM(a.shape, a.dtype) for a in (taps, scale, shift)]
        + [pltpu.SemaphoreType.DMA((len(arrays),))],
        compiler_params=params(ALONE),
        cost_estimate=pl.CostEstimate(flops=0, bytes_accessed=8 << 20, transcendentals=0),
        name="hold_call",
    )(*arrays)


def plan_sizes(tiles_dev):
    held = tiles_dev + 2
    return held, 2 * held, 3 * held + tiles_dev


def tables_kernel(
    me_ref, source_ref, utt_ref, plan_ref, key_utt_ref, query_utt_ref, filled, ranks, key_utts
):
    me = me_ref[0]
    total = source_ref.shape[0]
    tiles_dev = total // COUNT
    per_pair = tiles_dev // COUNT
    quarter_tiles = per_pair
    for pair in range(COUNT * COUNT):
        filled[pair] = 0

    def one(position, carried):
        pair = divide(source_ref[position], tiles_dev) * COUNT + divide(position, tiles_dev)
        rank = filled[pair]
        filled[pair] = rank + 1
        ranks[position] = rank
        key_utts[pair * per_pair + rank] = utt_ref[position]
        return carried

    lax.fori_loop(0, total, one, 0, unroll=4)
    is_end = (me == 0) | (me == COUNT - 1)
    second = jnp.where(is_end, 2, 3)
    third = jnp.where(is_end, 3, 2)
    held, places_at, _ = plan_sizes(tiles_dev)
    for i in range(held):
        position = jnp.clip(me * tiles_dev - 1 + i, 0, total - 1)
        source = divide(source_ref[position], tiles_dev)
        apart = me ^ source
        quarter = quarter_of(source, divide(position, tiles_dev))
        row = quarter * quarter_tiles + ranks[position]
        early = jnp.where(apart == 0, row, -1)
        near_last = (apart == 1) & (quarter == COUNT - 1)
        early = jnp.where((apart == 1) & (quarter < COUNT - 1), tiles_dev + row, early)
        early = jnp.where(apart == second, tiles_dev + 2 * quarter_tiles + row, early)
        plan_ref[i] = early
        plan_ref[held + i] = jnp.where((apart == third) | near_last, row, -1)
        query_utt_ref[i * TILE : (i + 1) * TILE] = jnp.full(
            (TILE, 128), utt_ref[position], jnp.int32
        )
    plan_places(me, utt_ref, tiles_dev, total, plan_ref, places_at)

    near, second, far = me ^ 1, me ^ second, me ^ third
    order = [(me, quarter, False) for quarter in (0, 1, 2, 3)]
    order += [(near, quarter, False) for quarter in (0, 1, 2)]
    order += [(second, quarter, False) for quarter in (1, 2, 3)]
    order += [(near, 3, True), (second, 0, True), (far, 3, True)]
    order += [(far, quarter, False) for quarter in (0, 1, 2)]
    lane_tile = lax.broadcasted_iota(jnp.int32, (1, 128), 1) // TILE
    tile_values = []
    for shard, quarter, inner_only in order:
        target = quarter_of(shard, quarter)
        for rank in range(per_pair):
            utt = key_utts[(shard * COUNT + target) * per_pair + rank]
            if inner_only:
                utt = jnp.where(is_end, -1, utt)
            tile_values.append(utt)
    per_vector = 128 // TILE
    for start in range(0, len(tile_values), per_vector):
        vector = jnp.full((1, 128), tile_values[start], jnp.int32)
        for k in range(1, per_vector):
            vector = jnp.where(lane_tile == k, tile_values[start + k], vector)
        key_utt_ref[:, start * TILE : start * TILE + 128] = vector


def early_kernel(
    me_ref, plan, low, last, near, inner, inner_end,
    key_weight, value_weight, key_ref, value_ref, grouped, rows,
):
    me = me_ref[0]
    is_end = (me == 0) | (me == COUNT - 1)
    piece, quarter_rows = low.shape[0], last.shape[0]
    base = piece + quarter_rows
    rows[0:piece] = low[...]
    rows[piece:base] = last[...]
    rows[base : base + piece] = near[...]

    @pl.when(is_end)
    def _():
        rows[base + piece :] = inner_end[...]

    @pl.when(jnp.logical_not(is_end))
    def _():
        rows[base + piece :] = inner[...]

    for i in range(grouped.shape[0] // TILE):
        place = jnp.maximum(plan[i], 0)
        grouped[i * TILE : (i + 1) * TILE] = rows[
            pl.ds(pl.multiple_of(place * TILE, TILE), TILE), :
        ]
    normed = layer_norm(rows[...]).astype(jnp.bfloat16)
    key_ref[...] = project(normed, key_weight)
    value_ref[...] = project(normed, value_weight)


def middle_kernel(*refs):
    parts, (key_weight, value_weight, key_ref, value_ref) = refs[:-4], refs[-4:]
    rows = jnp.concatenate([part[...] for part in parts], axis=0)
    normed = layer_norm(rows).astype(jnp.bfloat16)
    key_ref[...] = project(normed, key_weight)
    value_ref[...] = project(normed, value_weight)


def final_kernel(
    me_ref, plan, query_utt, key_utt, early_grouped, far, far_end, near_last,
    early_key, early_value, middle_key, middle_value,
    key_weight, value_weight, query_weight, output_weight, half_taps, half_shift,
    out_hbm, grouped, padded, residual_rows, out, write_sems, late,
):
    me = me_ref[0]
    is_end = (me == 0) | (me == COUNT - 1)
    held, places_at, _ = plan_sizes(out.shape[0] // TILE)
    late[far.shape[0] :] = near_last[...]

    @pl.when(is_end)
    def _():
        late[: far.shape[0]] = far_end[...]

    @pl.when(jnp.logical_not(is_end))
    def _():
        late[: far.shape[0]] = far[...]

    for i in range(held):
        row = plan[held + i]

        @pl.when(row >= 0)
        def _(row=row, i=i):
            grouped[i * TILE : (i + 1) * TILE] = late[
                pl.ds(pl.multiple_of(row * TILE, TILE), TILE), :
            ]

    padded[...] = jnp.zeros_like(padded)
    normed = layer_norm(late[: far.shape[0]]).astype(jnp.bfloat16)
    late_key = project(normed, key_weight)
    late_value = project(normed, value_weight)
    residual = attend(
        grouped, query_utt, key_utt[...],
        [early_key, middle_key, late_key], [early_value, middle_value, late_value],
        query_weight, output_weight,
    )
    convolve(
        residual, plan, places_at, half_taps, half_shift[...], out_hbm, padded, residual_rows,
        out, write_sems,
    )


def line_block(
    frames, tile_source, tile_utt, query_weight, key_weight, value_weight, output_weight,
    depth_weight, bn_scale, bn_shift,
):
    me = lax.axis_index("ctx").reshape(1)
    rows_dev, width = frames.shape
    quarter = rows_dev // COUNT
    piece = rows_dev - quarter
    total = tile_source.shape[0]
    wide = key_weight.shape[1]

    def shape(rows, columns=width, kind=jnp.bfloat16):
        return jax.ShapeDtypeStruct((rows, columns), kind)

    def cost(rows):
        return pl.CostEstimate(
            flops=4 * rows * width * wide, bytes_accessed=rows * width * 4, transcendentals=rows
        )

    low, last, high, start = pl.pallas_call(
        arrange_kernel,
        out_shape=tuple(pltpu.VMEM((n, width), frames.dtype) for n in (piece, quarter, piece, quarter)),
        in_specs=[SMEM] + [HBM] * 2,
        out_specs=(VMEM,) * 4,
        scratch_shapes=[
            pltpu.SMEM((total,), jnp.int32),
            pltpu.VMEM((rows_dev, width), jnp.bfloat16),
            pltpu.SMEM((rows_dev // TILE + 1,), jnp.int32),
            pltpu.SemaphoreType.DMA((2,)),
        ],
        compiler_params=params(ALONE),
        name="arrange",
    )(me, tile_source, frames)

    def swap(value, perm):
        return lax.ppermute(value, "ctx", perm)

    near = swap(low, SWAP_OUTER)
    inner = swap(high, SWAP_INNER)
    held_rows = rows_dev + 2 * TILE
    plan, key_utt, query_utt = pl.pallas_call(
        tables_kernel,
        out_shape=(
            jax.ShapeDtypeStruct((plan_sizes(rows_dev // TILE)[2],), jnp.int32),
            shape(1, total * TILE, jnp.int32),
            shape(held_rows, 128, jnp.int32),
        ),
        in_specs=[SMEM] * 3,
        out_specs=(SMEM, VMEM, VMEM),
        scratch_shapes=[pltpu.SMEM((n,), jnp.int32) for n in (COUNT * COUNT, total, total)],
        compiler_params=params(4),
        name="tables_call",
    )(me, tile_source, tile_utt)
    key_weight, value_weight, query_weight, output_weight, half_taps, half_shift = hold(
        key_weight, value_weight, query_weight, output_weight, depth_weight,
        bn_scale.reshape(1, -1), bn_shift.reshape(1, -1),
    )
    far = swap(low, OVER_TWO)
    inner_end = swap(inner, TO_ENDS)
    far_end = swap(far, TO_ENDS)
    far_last = swap(last, OVER_TWO)
    near_last = swap(last, FROM_ENDS)
    inner_start = swap(start, SWAP_INNER)

    early_rows = rows_dev + 2 * piece
    early_key, early_value, grouped = pl.pallas_call(
        early_kernel,
        out_shape=(shape(early_rows, wide), shape(early_rows, wide), shape(held_rows)),
        in_specs=[SMEM] * 2 + [VMEM] * 7,
        out_specs=(VMEM,) * 3,
        scratch_shapes=[pltpu.VMEM((early_rows, width), jnp.bfloat16)],
        compiler_params=params(16),
        cost_estimate=cost(early_rows),
        name="early_call",
    )(me, plan, low, last, near, inner, inner_end, key_weight, value_weight)
    middle_key, middle_value = pl.pallas_call(
        middle_kernel,
        out_shape=(shape(3 * quarter, wide),) * 2,
        in_specs=[VMEM] * 5,
        out_specs=(VMEM,) * 2,
        compiler_params=params(8),
        cost_estimate=cost(3 * quarter),
        name="middle_call",
    )(near_last, inner_start, far_last, key_weight, value_weight)
    return pl.pallas_call(
        final_kernel,
        out_shape=(shape(rows_dev), shape(held_rows)),
        in_specs=[SMEM] * 2 + [VMEM] * 16,
        out_specs=(HBM, VMEM),
        input_output_aliases={4: 1},
        scratch_shapes=block_scratch(rows_dev, width) + [pltpu.VMEM((rows_dev, width), jnp.bfloat16)],
        compiler_params=params(28),
        cost_estimate=pl.CostEstimate(
            flops=2 << 30, bytes_accessed=8 << 20, transcendentals=1 << 20
        ),
        name="final",
    )(
        me, plan, query_utt, key_utt, grouped, far, far_end, near_last,
        early_key, early_value, middle_key, middle_value,
        key_weight, value_weight, query_weight, output_weight, half_taps, half_shift,
    )[0]


def per_device(*arrays):
    tiles_dev = arrays[0].shape[0] // TILE
    if lax.axis_size("ctx") == COUNT and tiles_dev % COUNT == 0:
        return line_block(*arrays)
    return ring_block(*arrays)


def solution(mesh):
    return jax.shard_map(
        per_device,
        mesh=mesh,
        in_specs=(P(("dp", "ctx"), None), P("dp"), P("dp"), P(), P(), P(), P(), P(), P(), P()),
        out_specs=P(("dp", "ctx"), None),
        check_vma=False,
    )
```

```python
import functools
import math

import jax
import jax.numpy as jnp
from jax import lax
from jax.experimental import pallas as pl
from jax.experimental.pallas import tpu as pltpu
from jax.sharding import PartitionSpec as P


HEADS = 4
HEAD_DIM = 128
KERNEL = 31
TILE = 16
UTTS = 4
ALONE = 56
NEGATIVE = -1e30

VMEM = pl.BlockSpec(memory_space=pltpu.VMEM)
SMEM = pl.BlockSpec(memory_space=pltpu.SMEM)
HBM = pl.BlockSpec(memory_space=pltpu.HBM)


def params(mib):
    return pltpu.CompilerParams(vmem_limit_bytes=mib << 20)


def layer_norm(rows):
    values = rows.astype(jnp.float32)
    center = values - jnp.mean(values, axis=-1, keepdims=True)
    spread = jnp.mean(center * center, axis=-1, keepdims=True)
    return center * lax.rsqrt(spread + 1e-05)


def project(rows, weight_ref):
    return jnp.dot(rows, weight_ref[...], preferred_element_type=jnp.float32).astype(jnp.bfloat16)


def attend(
    grouped, query_utt, key_utt, key_parts, value_parts, query_weight, output_weight
):
    queries = project(layer_norm(grouped[...]).astype(jnp.bfloat16), query_weight)
    allowed = query_utt[:, :1] == key_utt
    exponent_scale = math.log2(math.e) / math.sqrt(HEAD_DIM)
    heads = []
    for head in range(HEADS):
        columns = slice(head * HEAD_DIM, (head + 1) * HEAD_DIM)
        key_head = jnp.concatenate([part[:, columns] for part in key_parts], axis=0)
        value_head = jnp.concatenate([part[:, columns] for part in value_parts], axis=0)
        scores = lax.dot_general(
            queries[:, columns],
            key_head,
            (((1,), (1,)), ((), ())),
            preferred_element_type=jnp.float32,
        )
        scores = jnp.where(allowed, scores, NEGATIVE)
        top = jnp.max(scores, axis=-1, keepdims=True)
        weights = jnp.exp2((scores - top) * exponent_scale)
        row_sum = jnp.sum(weights, axis=-1, keepdims=True)
        summed = jnp.dot(
            weights.astype(jnp.bfloat16), value_head, preferred_element_type=jnp.float32
        )
        heads.append((summed / row_sum).astype(jnp.bfloat16))
    attended = jnp.concatenate(heads, axis=1)
    return (
        grouped[...].astype(jnp.float32)
        + jnp.dot(attended, output_weight[...], preferred_element_type=jnp.float32)
    ).astype(jnp.bfloat16)


def convolve(residual, plan, at, half_taps, half_shift, out_hbm, padded, residual_rows, out, sems):
    rows_dev, width = out.shape
    tiles_dev = rows_dev // TILE
    held = tiles_dev + 2
    residual_rows[...] = residual[TILE : TILE + rows_dev]
    shaped = layer_norm(residual).astype(jnp.bfloat16).astype(jnp.float32)
    for i in range(held):
        row = pl.multiple_of(plan[at + i] * TILE, TILE)
        for block in range(width // 128):
            padded[block, pl.ds(row, TILE), :] = shaped[
                i * TILE : (i + 1) * TILE, block * 128 : (block + 1) * 128
            ]
    group = math.gcd(tiles_dev, 4)

    def write(step):
        rows = pl.ds(pl.multiple_of(step * group * TILE, TILE), group * TILE)
        return pltpu.make_async_copy(out.at[rows, :], out_hbm.at[rows, :], sems.at[step])

    def some_tiles(step, carried):
        starts = [
            pl.multiple_of(plan[at + held + step * group + k] * TILE, TILE) for k in range(group)
        ]
        for block in range(width // 128):
            columns = slice(block * 128, (block + 1) * 128)
            shift = jnp.broadcast_to(half_shift[:, columns], (8, 128))
            sums = [[shift, shift] for _ in range(group)]
            windows = [{} for _ in range(group)]
            for tap in range(KERNEL):
                weight = half_taps[tap : tap + 1, columns]
                for k in range(group):
                    for part in range(2):
                        offset = tap + 8 * part
                        if offset not in windows[k]:
                            windows[k][offset] = padded[
                                block, pl.ds(starts[k] + (offset - KERNEL // 2), 8), :
                            ]
                        sums[k][part] = sums[k][part] + windows[k][offset] * weight
            for k in range(group):
                half = jnp.concatenate(sums[k], axis=0)
                rows = pl.ds(pl.multiple_of((step * group + k) * TILE, TILE), TILE)
                kept = residual_rows[rows, columns].astype(jnp.float32)
                out[rows, columns] = (kept + (half + half * jnp.tanh(half))).astype(jnp.bfloat16)
        write(step).start()
        return carried

    steps = tiles_dev // group
    lax.fori_loop(0, steps, some_tiles, 0)
    for step in range(steps):
        write(step).wait()


def plan_places(me, utt_ref, tiles_dev, total, plan, at):
    first = me * tiles_dev - 1
    held = tiles_dev + 2
    place = jnp.int32(1)
    before = utt_ref[jnp.clip(first, 0, total - 1)]
    for i in range(held):
        here = utt_ref[jnp.clip(first + i, 0, total - 1)]
        if i:
            place = place + 1 + (here != before).astype(jnp.int32)
        before = here
        inside = (first + i >= 0) & (first + i < total)
        plan[at + i] = jnp.where(inside, place, padded_rows(tiles_dev) // TILE - 1)
        if 1 <= i <= tiles_dev:
            plan[at + held + i - 1] = place


def padded_rows(tiles_dev):
    return (1 + tiles_dev + 2 + (UTTS - 1) + 2) * TILE


def block_scratch(rows_dev, width):
    tiles_dev = rows_dev // TILE
    return [
        pltpu.VMEM((width // 128, padded_rows(tiles_dev), 128), jnp.float32),
        pltpu.VMEM((rows_dev, width), jnp.bfloat16),
        pltpu.VMEM((rows_dev, width), jnp.bfloat16),
        pltpu.SemaphoreType.DMA((tiles_dev // math.gcd(tiles_dev, 4),)),
    ]


def key_value_kernel(rows_ref, key_weight_ref, value_weight_ref, key_ref, value_ref):
    normed = layer_norm(rows_ref[...]).astype(jnp.bfloat16)
    key_ref[...] = project(normed, key_weight_ref)
    value_ref[...] = project(normed, value_weight_ref)


def key_value(rows, key_weight, value_weight):
    shape = jax.ShapeDtypeStruct((rows.shape[0], key_weight.shape[1]), jnp.bfloat16)
    flops = 4 * rows.shape[0] * rows.shape[1] * key_weight.shape[1]
    return pl.pallas_call(
        key_value_kernel,
        out_shape=(shape, shape),
        in_specs=[VMEM] * 3,
        out_specs=(VMEM, VMEM),
        cost_estimate=pl.CostEstimate(flops=flops, bytes_accessed=3 << 20, transcendentals=0),
        name="key_value",
    )(rows, key_weight, value_weight)


def ring_kernel(count, me_ref, source_ref, utt_ref, key_utt_ref, *refs):
    chunks = refs[:count]
    keys = refs[count : 2 * count]
    values = refs[2 * count : 3 * count]
    query_weight, output_weight, taps, scale, shift, out_hbm = refs[3 * count : 3 * count + 6]
    padded, residual_rows, out, write_sems = refs[3 * count + 6 : 3 * count + 10]
    grouped, query_utt, half_taps, plan, sems = refs[3 * count + 10 :]
    me = me_ref[0]
    tiles_dev = out.shape[0] // TILE
    held = tiles_dev + 2
    total = tiles_dev * count
    first = me * tiles_dev - 1
    padded[...] = jnp.zeros_like(padded)
    half_taps[...] = taps[...] * (0.5 * scale[...])
    for i in range(held):
        position = jnp.clip(first + i, 0, total - 1)
        source = source_ref[position]
        row = pl.multiple_of((source % tiles_dev) * TILE, TILE)
        behind = lax.rem(me - source // tiles_dev + count, count)
        for step in range(count):

            @pl.when(behind == step)
            def _(step=step, row=row, i=i):
                pltpu.make_async_copy(
                    chunks[step].at[pl.ds(row, TILE), :],
                    grouped.at[pl.ds(i * TILE, TILE), :],
                    sems.at[i],
                ).start()

        query_utt[pl.ds(i * TILE, TILE), :] = jnp.full((TILE, 128), utt_ref[position], jnp.int32)
    plan_places(me, utt_ref, tiles_dev, total, plan, 0)
    for i in range(held):
        pltpu.make_async_copy(
            chunks[0].at[pl.ds(0, TILE), :], grouped.at[pl.ds(i * TILE, TILE), :], sems.at[i]
        ).wait()
    residual = attend(
        grouped, query_utt, key_utt_ref[...], keys, values, query_weight, output_weight
    )
    convolve(
        residual, plan, 0, half_taps, 0.5 * shift[...], out_hbm, padded, residual_rows, out,
        write_sems,
    )


def ring_block(
    frames, tile_source, tile_utt, query_weight, key_weight, value_weight, output_weight,
    depth_weight, bn_scale, bn_shift,
):
    count = lax.axis_size("ctx")
    me = lax.axis_index("ctx")
    rows_dev, width = frames.shape
    tiles_dev = rows_dev // TILE
    ring = [(i, (i + 1) % count) for i in range(count)]
    chunks = [frames]
    for _ in range(count - 1):
        chunks.append(lax.ppermute(chunks[-1], "ctx", ring))
    pairs = [key_value(chunk, key_weight, value_weight) for chunk in chunks]
    shards = lax.rem(me - jnp.arange(count, dtype=jnp.int32) + count, count)
    arrived = (shards[:, None] * tiles_dev + jnp.arange(tiles_dev, dtype=jnp.int32)).reshape(-1)
    key_utt = jnp.sum(
        jnp.where(arrived[:, None] == tile_source[None, :], tile_utt[None, :], 0), axis=1
    )
    key_utt = jnp.repeat(key_utt, TILE).reshape(1, -1)
    return pl.pallas_call(
        functools.partial(ring_kernel, count),
        out_shape=jax.ShapeDtypeStruct((rows_dev, width), jnp.bfloat16),
        in_specs=[SMEM] * 3
        + [VMEM]
        + [pl.BlockSpec(memory_space=pl.ANY)] * count
        + [VMEM] * (2 * count + 5),
        out_specs=HBM,
        scratch_shapes=block_scratch(rows_dev, width)
        + [
            pltpu.VMEM((rows_dev + 2 * TILE, width), jnp.bfloat16),
            pltpu.VMEM((rows_dev + 2 * TILE, 128), jnp.int32),
            pltpu.VMEM(depth_weight.shape, jnp.float32),
            pltpu.SMEM((2 * tiles_dev + 2,), jnp.int32),
            pltpu.SemaphoreType.DMA((tiles_dev + 2,)),
        ],
        cost_estimate=pl.CostEstimate(
            flops=2 << 30, bytes_accessed=8 << 20, transcendentals=1 << 20
        ),
        name="ring_block",
    )(
        me.reshape(1), tile_source, tile_utt, key_utt, *chunks,
        *[pair[0] for pair in pairs], *[pair[1] for pair in pairs],
        query_weight, output_weight, depth_weight, bn_scale.reshape(1, -1), bn_shift.reshape(1, -1),
    )


COUNT = 4
SWAP_OUTER = [(0, 1), (1, 0), (2, 3), (3, 2)]
SWAP_INNER = [(1, 2), (2, 1)]
TO_ENDS = [(1, 0), (2, 3)]
FROM_ENDS = [(0, 1), (3, 2)]
OVER_TWO = [(0, 2), (3, 1)]


def quarter_of(source_shard, target):
    return jnp.where(source_shard % 2 == 1, target, COUNT - 1 - target)


def divide(value, by):
    if by & (by - 1) == 0:
        return value >> (by.bit_length() - 1)
    return lax.div(value, by)


def arrange_kernel(
    me_ref, source_hbm, rows_hbm, low_ref, last_ref, high_ref, start_ref, source_ref, rows, slots, sems
):
    me = me_ref[0]
    rows_dev, quarter_rows = rows.shape[0], last_ref.shape[0]
    tiles_dev = rows_dev // TILE
    per_pair = tiles_dev // COUNT
    rows_copy = pltpu.make_async_copy(rows_hbm, rows, sems.at[0])
    source_copy = pltpu.make_async_copy(source_hbm, source_ref, sems.at[1])
    source_copy.start()
    rows_copy.start()
    source_copy.wait()
    for target in range(COUNT):
        place = quarter_of(me, target) * per_pair
        for position in range(target * tiles_dev, (target + 1) * tiles_dev):
            source = source_ref[position]
            shard = divide(source, tiles_dev)
            mine = shard == me
            slots[jnp.where(mine, place, tiles_dev)] = source - shard * tiles_dev
            place = place + mine.astype(jnp.int32)
    rows_copy.wait()
    for place in range(tiles_dev):
        tile = rows[pl.ds(pl.multiple_of(slots[place] * TILE, TILE), TILE), :]
        row = place * TILE
        if row < rows_dev - quarter_rows:
            low_ref[row : row + TILE] = tile
        else:
            row_here = row - (rows_dev - quarter_rows)
            last_ref[row_here : row_here + TILE] = tile
        if row >= quarter_rows:
            high_ref[row - quarter_rows : row - quarter_rows + TILE] = tile
        else:
            start_ref[row : row + TILE] = tile


def hold_kernel(*refs):
    count = (len(refs) - 3) // 2
    arrays, kept = refs[:count], refs[count : 2 * count - 1]
    taps, scale, shift, sems = refs[2 * count - 1 :]
    targets = (*kept[:-2], taps, scale, shift)
    copies = [
        pltpu.make_async_copy(array, target, sems.at[i])
        for i, (array, target) in enumerate(zip(arrays, targets))
    ]
    for copy in copies:
        copy.start()
    for copy in copies:
        copy.wait()
    kept[-2][...] = taps[...] * (0.5 * scale[...])
    kept[-1][...] = 0.5 * shift[...]


def hold(*arrays):
    taps, scale, shift = arrays[-3:]
    kept = (*arrays[:-2], shift)
    return pl.pallas_call(
        hold_kernel,
        out_shape=tuple(pltpu.VMEM(a.shape, a.dtype) for a in kept),
        in_specs=[HBM] * len(arrays),
        out_specs=(VMEM,) * len(kept),
        scratch_shapes=[pltpu.VMEM(a.shape, a.dtype) for a in (taps, scale, shift)]
        + [pltpu.SemaphoreType.DMA((len(arrays),))],
        compiler_params=params(ALONE),
        cost_estimate=pl.CostEstimate(flops=0, bytes_accessed=8 << 20, transcendentals=0),
        name="hold_call",
    )(*arrays)


def plan_sizes(tiles_dev):
    held = tiles_dev + 2
    return held, 3 * held, 4 * held + tiles_dev


def tables_kernel(
    me_ref, source_ref, utt_ref, plan_ref, key_utt_ref, query_utt_ref, filled, ranks, key_utts
):
    me = me_ref[0]
    total = source_ref.shape[0]
    tiles_dev = total // COUNT
    per_pair = tiles_dev // COUNT
    quarter_tiles = per_pair
    for pair in range(COUNT * COUNT):
        filled[pair] = 0

    def one(position, carried):
        pair = divide(source_ref[position], tiles_dev) * COUNT + divide(position, tiles_dev)
        rank = filled[pair]
        filled[pair] = rank + 1
        ranks[position] = rank
        key_utts[pair * per_pair + rank] = utt_ref[position]
        return carried

    lax.fori_loop(0, total, one, 0, unroll=4)
    is_end = (me == 0) | (me == COUNT - 1)
    second = jnp.where(is_end, 2, 3)
    third = jnp.where(is_end, 3, 2)
    held, places_at, _ = plan_sizes(tiles_dev)
    for i in range(held):
        position = jnp.clip(me * tiles_dev - 1 + i, 0, total - 1)
        source = divide(source_ref[position], tiles_dev)
        apart = me ^ source
        quarter = quarter_of(source, divide(position, tiles_dev))
        row = quarter * quarter_tiles + ranks[position]
        early = jnp.where(apart == 0, row, -1)
        near_last = (apart == 1) & (quarter == COUNT - 1)
        early = jnp.where((apart == 1) & (quarter < COUNT - 1), tiles_dev + row, early)
        plan_ref[2 * held + i] = jnp.where(apart == second, row - quarter_tiles, -1)
        plan_ref[i] = early
        plan_ref[held + i] = jnp.where((apart == third) | near_last, row, -1)
        query_utt_ref[i * TILE : (i + 1) * TILE] = jnp.full(
            (TILE, 128), utt_ref[position], jnp.int32
        )
    plan_places(me, utt_ref, tiles_dev, total, plan_ref, places_at)

    near, second, far = me ^ 1, me ^ second, me ^ third
    order = [(me, quarter, False) for quarter in (0, 1, 2, 3)]
    order += [(near, quarter, False) for quarter in (0, 1, 2)]
    order += [(second, quarter, False) for quarter in (1, 2, 3)]
    order += [(near, 3, True), (second, 0, True), (far, 3, True)]
    order += [(far, quarter, False) for quarter in (0, 1, 2)]
    lane_tile = lax.broadcasted_iota(jnp.int32, (1, 128), 1) // TILE
    tile_values = []
    for shard, quarter, inner_only in order:
        target = quarter_of(shard, quarter)
        for rank in range(per_pair):
            utt = key_utts[(shard * COUNT + target) * per_pair + rank]
            if inner_only:
                utt = jnp.where(is_end, -1, utt)
            tile_values.append(utt)
    per_vector = 128 // TILE
    for start in range(0, len(tile_values), per_vector):
        vector = jnp.full((1, 128), tile_values[start], jnp.int32)
        for k in range(1, per_vector):
            vector = jnp.where(lane_tile == k, tile_values[start + k], vector)
        key_utt_ref[:, start * TILE : start * TILE + 128] = vector


def place_tiles(grouped, rows, plan, at):
    for i in range(grouped.shape[0] // TILE):
        place = plan[at + i]

        @pl.when(place >= 0)
        def _(place=place, i=i):
            grouped[i * TILE : (i + 1) * TILE] = rows[
                pl.ds(pl.multiple_of(place * TILE, TILE), TILE), :
            ]


def early_kernel(
    plan, low, last, near, key_weight, value_weight, key_ref, value_ref, grouped, rows
):
    piece, quarter_rows = low.shape[0], last.shape[0]
    base = piece + quarter_rows
    rows[0:piece] = low[...]
    rows[piece:base] = last[...]
    rows[base:] = near[...]
    grouped[...] = jnp.zeros_like(grouped)
    place_tiles(grouped, rows, plan, 0)
    normed = layer_norm(rows[...]).astype(jnp.bfloat16)
    key_ref[...] = project(normed, key_weight)
    value_ref[...] = project(normed, value_weight)


def second_kernel(
    me_ref, plan, early_grouped, inner, inner_end, key_weight, value_weight,
    key_ref, value_ref, grouped, rows,
):
    me = me_ref[0]
    is_end = (me == 0) | (me == COUNT - 1)

    @pl.when(is_end)
    def _():
        rows[...] = inner_end[...]

    @pl.when(jnp.logical_not(is_end))
    def _():
        rows[...] = inner[...]

    place_tiles(grouped, rows, plan, 2 * (grouped.shape[0] // TILE))
    normed = layer_norm(rows[...]).astype(jnp.bfloat16)
    key_ref[...] = project(normed, key_weight)
    value_ref[...] = project(normed, value_weight)


def middle_kernel(*refs):
    parts, (key_weight, value_weight, key_ref, value_ref) = refs[:-4], refs[-4:]
    rows = jnp.concatenate([part[...] for part in parts], axis=0)
    normed = layer_norm(rows).astype(jnp.bfloat16)
    key_ref[...] = project(normed, key_weight)
    value_ref[...] = project(normed, value_weight)


def final_kernel(
    me_ref, plan, query_utt, key_utt, early_grouped, far, far_end, near_last,
    early_key, early_value, second_key, second_value, middle_key, middle_value,
    key_weight, value_weight, query_weight, output_weight, half_taps, half_shift,
    out_hbm, grouped, padded, residual_rows, out, write_sems, late,
):
    me = me_ref[0]
    is_end = (me == 0) | (me == COUNT - 1)
    held, places_at, _ = plan_sizes(out.shape[0] // TILE)
    late[far.shape[0] :] = near_last[...]

    @pl.when(is_end)
    def _():
        late[: far.shape[0]] = far_end[...]

    @pl.when(jnp.logical_not(is_end))
    def _():
        late[: far.shape[0]] = far[...]

    place_tiles(grouped, late, plan, held)
    padded[...] = jnp.zeros_like(padded)
    normed = layer_norm(late[: far.shape[0]]).astype(jnp.bfloat16)
    late_key = project(normed, key_weight)
    late_value = project(normed, value_weight)
    residual = attend(
        grouped, query_utt, key_utt[...],
        [early_key, second_key, middle_key, late_key],
        [early_value, second_value, middle_value, late_value],
        query_weight, output_weight,
    )
    convolve(
        residual, plan, places_at, half_taps, half_shift[...], out_hbm, padded, residual_rows,
        out, write_sems,
    )


def line_block(
    frames, tile_source, tile_utt, query_weight, key_weight, value_weight, output_weight,
    depth_weight, bn_scale, bn_shift,
):
    me = lax.axis_index("ctx").reshape(1)
    rows_dev, width = frames.shape
    quarter = rows_dev // COUNT
    piece = rows_dev - quarter
    total = tile_source.shape[0]
    wide = key_weight.shape[1]

    def shape(rows, columns=width, kind=jnp.bfloat16):
        return jax.ShapeDtypeStruct((rows, columns), kind)

    def cost(rows):
        return pl.CostEstimate(
            flops=4 * rows * width * wide, bytes_accessed=rows * width * 4, transcendentals=rows
        )

    low, last, high, start = pl.pallas_call(
        arrange_kernel,
        out_shape=tuple(pltpu.VMEM((n, width), frames.dtype) for n in (piece, quarter, piece, quarter)),
        in_specs=[SMEM] + [HBM] * 2,
        out_specs=(VMEM,) * 4,
        scratch_shapes=[
            pltpu.SMEM((total,), jnp.int32),
            pltpu.VMEM((rows_dev, width), jnp.bfloat16),
            pltpu.SMEM((rows_dev // TILE + 1,), jnp.int32),
            pltpu.SemaphoreType.DMA((2,)),
        ],
        compiler_params=params(ALONE),
        name="arrange",
    )(me, tile_source, frames)

    def swap(value, perm):
        return lax.ppermute(value, "ctx", perm)

    near = swap(low, SWAP_OUTER)
    inner = swap(high, SWAP_INNER)
    held_rows = rows_dev + 2 * TILE
    plan, key_utt, query_utt = pl.pallas_call(
        tables_kernel,
        out_shape=(
            jax.ShapeDtypeStruct((plan_sizes(rows_dev // TILE)[2],), jnp.int32),
            shape(1, total * TILE, jnp.int32),
            shape(held_rows, 128, jnp.int32),
        ),
        in_specs=[SMEM] * 3,
        out_specs=(SMEM, VMEM, VMEM),
        scratch_shapes=[pltpu.SMEM((n,), jnp.int32) for n in (COUNT * COUNT, total, total)],
        compiler_params=params(4),
        name="tables_call",
    )(me, tile_source, tile_utt)
    key_weight, value_weight, query_weight, output_weight, half_taps, half_shift = hold(
        key_weight, value_weight, query_weight, output_weight, depth_weight,
        bn_scale.reshape(1, -1), bn_shift.reshape(1, -1),
    )
    far = swap(low, OVER_TWO)
    inner_end = swap(inner, TO_ENDS)
    far_end = swap(far, TO_ENDS)
    far_last = swap(last, OVER_TWO)
    near_last = swap(last, FROM_ENDS)
    inner_start = swap(start, SWAP_INNER)

    early_rows = rows_dev + piece
    early_key, early_value, grouped = pl.pallas_call(
        early_kernel,
        out_shape=(shape(early_rows, wide), shape(early_rows, wide), shape(held_rows)),
        in_specs=[SMEM] + [VMEM] * 5,
        out_specs=(VMEM,) * 3,
        scratch_shapes=[pltpu.VMEM((early_rows, width), jnp.bfloat16)],
        compiler_params=params(12),
        cost_estimate=cost(early_rows),
        name="early_call",
    )(plan, low, last, near, key_weight, value_weight)
    second_key, second_value, grouped = pl.pallas_call(
        second_kernel,
        out_shape=(shape(piece, wide), shape(piece, wide), shape(held_rows)),
        in_specs=[SMEM] * 2 + [VMEM] * 5,
        out_specs=(VMEM,) * 3,
        input_output_aliases={2: 2},
        scratch_shapes=[pltpu.VMEM((piece, width), jnp.bfloat16)],
        compiler_params=params(8),
        cost_estimate=cost(piece),
        name="second_call",
    )(me, plan, grouped, inner, inner_end, key_weight, value_weight)
    middle_key, middle_value = pl.pallas_call(
        middle_kernel,
        out_shape=(shape(3 * quarter, wide),) * 2,
        in_specs=[VMEM] * 5,
        out_specs=(VMEM,) * 2,
        compiler_params=params(8),
        cost_estimate=cost(3 * quarter),
        name="middle_call",
    )(near_last, inner_start, far_last, key_weight, value_weight)
    return pl.pallas_call(
        final_kernel,
        out_shape=(shape(rows_dev), shape(held_rows)),
        in_specs=[SMEM] * 2 + [VMEM] * 18,
        out_specs=(HBM, VMEM),
        input_output_aliases={4: 1},
        scratch_shapes=block_scratch(rows_dev, width) + [pltpu.VMEM((rows_dev, width), jnp.bfloat16)],
        compiler_params=params(28),
        cost_estimate=pl.CostEstimate(
            flops=2 << 30, bytes_accessed=8 << 20, transcendentals=1 << 20
        ),
        name="final",
    )(
        me, plan, query_utt, key_utt, grouped, far, far_end, near_last,
        early_key, early_value, second_key, second_value, middle_key, middle_value,
        key_weight, value_weight, query_weight, output_weight, half_taps, half_shift,
    )[0]


def per_device(*arrays):
    tiles_dev = arrays[0].shape[0] // TILE
    if lax.axis_size("ctx") == COUNT and tiles_dev % COUNT == 0:
        return line_block(*arrays)
    return ring_block(*arrays)


def solution(mesh):
    return jax.shard_map(
        per_device,
        mesh=mesh,
        in_specs=(P(("dp", "ctx"), None), P("dp"), P("dp"), P(), P(), P(), P(), P(), P(), P()),
        out_specs=P(("dp", "ctx"), None),
        check_vma=False,
    )
```

```python
import functools
import math

import jax
import jax.numpy as jnp
from jax import lax
from jax.experimental import pallas as pl
from jax.experimental.pallas import tpu as pltpu
from jax.sharding import PartitionSpec as P


HEADS = 4
HEAD_DIM = 128
KERNEL = 31
TILE = 16
UTTS = 4
ALONE = 56
NEGATIVE = -1e30

VMEM = pl.BlockSpec(memory_space=pltpu.VMEM)
SMEM = pl.BlockSpec(memory_space=pltpu.SMEM)
HBM = pl.BlockSpec(memory_space=pltpu.HBM)


def params(mib):
    return pltpu.CompilerParams(vmem_limit_bytes=mib << 20)


def layer_norm(rows):
    values = rows.astype(jnp.float32)
    center = values - jnp.mean(values, axis=-1, keepdims=True)
    spread = jnp.mean(center * center, axis=-1, keepdims=True)
    return center * lax.rsqrt(spread + 1e-05)


def project(rows, weight_ref):
    return jnp.dot(rows, weight_ref[...], preferred_element_type=jnp.float32).astype(jnp.bfloat16)


def mask_bias(query_utt, key_utt):
    return jnp.where(query_utt == key_utt, 0.0, NEGATIVE)


def attend(grouped, bias, key_parts, value_parts, query_weight, output_weight):
    queries = project(layer_norm(grouped[...]).astype(jnp.bfloat16), query_weight)
    ones = jnp.ones((bias.shape[1], HEAD_DIM), jnp.bfloat16)
    exponent_scale = math.log2(math.e) / math.sqrt(HEAD_DIM)
    heads = []
    for head in range(HEADS):
        columns = slice(head * HEAD_DIM, (head + 1) * HEAD_DIM)
        key_head = jnp.concatenate([part[:, columns] for part in key_parts], axis=0)
        value_head = jnp.concatenate([part[:, columns] for part in value_parts], axis=0)
        scores = lax.dot_general(
            queries[:, columns],
            key_head,
            (((1,), (1,)), ((), ())),
            preferred_element_type=jnp.float32,
        )
        scores = scores + bias[...]
        top = jnp.max(scores, axis=-1, keepdims=True)
        weights = jnp.exp2((scores - top) * exponent_scale)
        summed = jnp.dot(
            weights.astype(jnp.bfloat16),
            jnp.concatenate([value_head, ones], axis=1),
            preferred_element_type=jnp.float32,
        )
        heads.append((summed[:, :HEAD_DIM] / summed[:, HEAD_DIM:]).astype(jnp.bfloat16))
    attended = jnp.concatenate(heads, axis=1)
    return (
        grouped[...].astype(jnp.float32)
        + jnp.dot(attended, output_weight[...], preferred_element_type=jnp.float32)
    ).astype(jnp.bfloat16)


def convolve(residual, plan, at, half_taps, half_shift, out_hbm, padded, residual_rows, out, sems):
    rows_dev, width = out.shape
    tiles_dev = rows_dev // TILE
    held = tiles_dev + 2
    residual_rows[...] = residual[TILE : TILE + rows_dev]
    shaped = layer_norm(residual).astype(jnp.bfloat16).astype(jnp.float32)
    for i in range(held):
        row = pl.multiple_of(plan[at + i] * TILE, TILE)
        for block in range(width // 128):
            padded[block, pl.ds(row, TILE), :] = shaped[
                i * TILE : (i + 1) * TILE, block * 128 : (block + 1) * 128
            ]
    group = math.gcd(tiles_dev, 4)

    def write(step):
        rows = pl.ds(pl.multiple_of(step * group * TILE, TILE), group * TILE)
        return pltpu.make_async_copy(out.at[rows, :], out_hbm.at[rows, :], sems.at[step])

    def some_tiles(step, carried):
        starts = [
            pl.multiple_of(plan[at + held + step * group + k] * TILE, TILE) for k in range(group)
        ]
        for block in range(width // 128):
            columns = slice(block * 128, (block + 1) * 128)
            shift = jnp.broadcast_to(half_shift[:, columns], (8, 128))
            sums = [[shift, shift] for _ in range(group)]
            windows = [{} for _ in range(group)]
            for tap in range(KERNEL):
                weight = half_taps[tap : tap + 1, columns]
                for k in range(group):
                    for part in range(2):
                        offset = tap + 8 * part
                        if offset not in windows[k]:
                            windows[k][offset] = padded[
                                block, pl.ds(starts[k] + (offset - KERNEL // 2), 8), :
                            ]
                        sums[k][part] = sums[k][part] + windows[k][offset] * weight
            for k in range(group):
                half = jnp.concatenate(sums[k], axis=0)
                rows = pl.ds(pl.multiple_of((step * group + k) * TILE, TILE), TILE)
                kept = residual_rows[rows, columns].astype(jnp.float32)
                out[rows, columns] = (kept + (half + half * jnp.tanh(half))).astype(jnp.bfloat16)
        write(step).start()
        return carried

    steps = tiles_dev // group
    lax.fori_loop(0, steps, some_tiles, 0)
    for step in range(steps):
        write(step).wait()


def plan_places(me, utt_ref, tiles_dev, total, plan, at):
    first = me * tiles_dev - 1
    held = tiles_dev + 2
    place = jnp.int32(1)
    before = utt_ref[jnp.clip(first, 0, total - 1)]
    for i in range(held):
        here = utt_ref[jnp.clip(first + i, 0, total - 1)]
        if i:
            place = place + 1 + (here != before).astype(jnp.int32)
        before = here
        inside = (first + i >= 0) & (first + i < total)
        plan[at + i] = jnp.where(inside, place, padded_rows(tiles_dev) // TILE - 1)
        if 1 <= i <= tiles_dev:
            plan[at + held + i - 1] = place


def padded_rows(tiles_dev):
    return (1 + tiles_dev + 2 + (UTTS - 1) + 2) * TILE


def block_scratch(rows_dev, width):
    tiles_dev = rows_dev // TILE
    return [
        pltpu.VMEM((width // 128, padded_rows(tiles_dev), 128), jnp.float32),
        pltpu.VMEM((rows_dev, width), jnp.bfloat16),
        pltpu.VMEM((rows_dev, width), jnp.bfloat16),
        pltpu.SemaphoreType.DMA((tiles_dev // math.gcd(tiles_dev, 4),)),
    ]


def key_value_kernel(rows_ref, key_weight_ref, value_weight_ref, key_ref, value_ref):
    normed = layer_norm(rows_ref[...]).astype(jnp.bfloat16)
    key_ref[...] = project(normed, key_weight_ref)
    value_ref[...] = project(normed, value_weight_ref)


def key_value(rows, key_weight, value_weight):
    shape = jax.ShapeDtypeStruct((rows.shape[0], key_weight.shape[1]), jnp.bfloat16)
    flops = 4 * rows.shape[0] * rows.shape[1] * key_weight.shape[1]
    return pl.pallas_call(
        key_value_kernel,
        out_shape=(shape, shape),
        in_specs=[VMEM] * 3,
        out_specs=(VMEM, VMEM),
        cost_estimate=pl.CostEstimate(flops=flops, bytes_accessed=3 << 20, transcendentals=0),
        name="key_value",
    )(rows, key_weight, value_weight)


def ring_kernel(count, me_ref, source_ref, utt_ref, key_utt_ref, *refs):
    chunks = refs[:count]
    keys = refs[count : 2 * count]
    values = refs[2 * count : 3 * count]
    query_weight, output_weight, taps, scale, shift, out_hbm = refs[3 * count : 3 * count + 6]
    padded, residual_rows, out, write_sems = refs[3 * count + 6 : 3 * count + 10]
    grouped, query_utt, half_taps, plan, sems = refs[3 * count + 10 :]
    me = me_ref[0]
    tiles_dev = out.shape[0] // TILE
    held = tiles_dev + 2
    total = tiles_dev * count
    first = me * tiles_dev - 1
    padded[...] = jnp.zeros_like(padded)
    half_taps[...] = taps[...] * (0.5 * scale[...])
    for i in range(held):
        position = jnp.clip(first + i, 0, total - 1)
        source = source_ref[position]
        row = pl.multiple_of((source % tiles_dev) * TILE, TILE)
        behind = lax.rem(me - source // tiles_dev + count, count)
        for step in range(count):

            @pl.when(behind == step)
            def _(step=step, row=row, i=i):
                pltpu.make_async_copy(
                    chunks[step].at[pl.ds(row, TILE), :],
                    grouped.at[pl.ds(i * TILE, TILE), :],
                    sems.at[i],
                ).start()

        query_utt[pl.ds(i * TILE, TILE), :] = jnp.full((TILE, 128), utt_ref[position], jnp.int32)
    plan_places(me, utt_ref, tiles_dev, total, plan, 0)
    for i in range(held):
        pltpu.make_async_copy(
            chunks[0].at[pl.ds(0, TILE), :], grouped.at[pl.ds(i * TILE, TILE), :], sems.at[i]
        ).wait()
    bias = mask_bias(query_utt[:, :1], key_utt_ref[...])
    residual = attend(grouped, bias, keys, values, query_weight, output_weight)
    convolve(
        residual, plan, 0, half_taps, 0.5 * shift[...], out_hbm, padded, residual_rows, out,
        write_sems,
    )


def ring_block(
    frames, tile_source, tile_utt, query_weight, key_weight, value_weight, output_weight,
    depth_weight, bn_scale, bn_shift,
):
    count = lax.axis_size("ctx")
    me = lax.axis_index("ctx")
    rows_dev, width = frames.shape
    tiles_dev = rows_dev // TILE
    ring = [(i, (i + 1) % count) for i in range(count)]
    chunks = [frames]
    for _ in range(count - 1):
        chunks.append(lax.ppermute(chunks[-1], "ctx", ring))
    pairs = [key_value(chunk, key_weight, value_weight) for chunk in chunks]
    shards = lax.rem(me - jnp.arange(count, dtype=jnp.int32) + count, count)
    arrived = (shards[:, None] * tiles_dev + jnp.arange(tiles_dev, dtype=jnp.int32)).reshape(-1)
    key_utt = jnp.sum(
        jnp.where(arrived[:, None] == tile_source[None, :], tile_utt[None, :], 0), axis=1
    )
    key_utt = jnp.repeat(key_utt, TILE).reshape(1, -1)
    return pl.pallas_call(
        functools.partial(ring_kernel, count),
        out_shape=jax.ShapeDtypeStruct((rows_dev, width), jnp.bfloat16),
        in_specs=[SMEM] * 3
        + [VMEM]
        + [pl.BlockSpec(memory_space=pl.ANY)] * count
        + [VMEM] * (2 * count + 5),
        out_specs=HBM,
        scratch_shapes=block_scratch(rows_dev, width)
        + [
            pltpu.VMEM((rows_dev + 2 * TILE, width), jnp.bfloat16),
            pltpu.VMEM((rows_dev + 2 * TILE, 128), jnp.int32),
            pltpu.VMEM(depth_weight.shape, jnp.float32),
            pltpu.SMEM((2 * tiles_dev + 2,), jnp.int32),
            pltpu.SemaphoreType.DMA((tiles_dev + 2,)),
        ],
        cost_estimate=pl.CostEstimate(
            flops=2 << 30, bytes_accessed=8 << 20, transcendentals=1 << 20
        ),
        name="ring_block",
    )(
        me.reshape(1), tile_source, tile_utt, key_utt, *chunks,
        *[pair[0] for pair in pairs], *[pair[1] for pair in pairs],
        query_weight, output_weight, depth_weight, bn_scale.reshape(1, -1), bn_shift.reshape(1, -1),
    )


COUNT = 4
SWAP_OUTER = [(0, 1), (1, 0), (2, 3), (3, 2)]
SWAP_INNER = [(1, 2), (2, 1)]
TO_ENDS = [(1, 0), (2, 3)]
FROM_ENDS = [(0, 1), (3, 2)]
OVER_TWO = [(0, 2), (3, 1)]


def quarter_of(source_shard, target):
    return jnp.where(source_shard % 2 == 1, target, COUNT - 1 - target)


def divide(value, by):
    if by & (by - 1) == 0:
        return value >> (by.bit_length() - 1)
    return lax.div(value, by)


def arrange_kernel(
    me_ref, source_hbm, rows_hbm, low_ref, last_ref, high_ref, start_ref, source_ref, rows, slots, sems
):
    me = me_ref[0]
    rows_dev, quarter_rows = rows.shape[0], last_ref.shape[0]
    tiles_dev = rows_dev // TILE
    per_pair = tiles_dev // COUNT
    rows_copy = pltpu.make_async_copy(rows_hbm, rows, sems.at[0])
    source_copy = pltpu.make_async_copy(source_hbm, source_ref, sems.at[1])
    source_copy.start()
    rows_copy.start()
    source_copy.wait()
    for target in range(COUNT):
        place = quarter_of(me, target) * per_pair
        for position in range(target * tiles_dev, (target + 1) * tiles_dev):
            source = source_ref[position]
            shard = divide(source, tiles_dev)
            mine = shard == me
            slots[jnp.where(mine, place, tiles_dev)] = source - shard * tiles_dev
            place = place + mine.astype(jnp.int32)
    rows_copy.wait()
    for place in range(tiles_dev):
        tile = rows[pl.ds(pl.multiple_of(slots[place] * TILE, TILE), TILE), :]
        row = place * TILE
        if row < rows_dev - quarter_rows:
            low_ref[row : row + TILE] = tile
        else:
            row_here = row - (rows_dev - quarter_rows)
            last_ref[row_here : row_here + TILE] = tile
        if row >= quarter_rows:
            high_ref[row - quarter_rows : row - quarter_rows + TILE] = tile
        else:
            start_ref[row : row + TILE] = tile


def hold_kernel(*refs):
    count = (len(refs) - 3) // 2
    arrays, kept = refs[:count], refs[count : 2 * count - 1]
    taps, scale, shift, sems = refs[2 * count - 1 :]
    targets = (*kept[:-2], taps, scale, shift)
    copies = [
        pltpu.make_async_copy(array, target, sems.at[i])
        for i, (array, target) in enumerate(zip(arrays, targets))
    ]
    for copy in copies:
        copy.start()
    for copy in copies:
        copy.wait()
    kept[-2][...] = taps[...] * (0.5 * scale[...])
    kept[-1][...] = 0.5 * shift[...]


def hold(*arrays):
    taps, scale, shift = arrays[-3:]
    kept = (*arrays[:-2], shift)
    return pl.pallas_call(
        hold_kernel,
        out_shape=tuple(pltpu.VMEM(a.shape, a.dtype) for a in kept),
        in_specs=[HBM] * len(arrays),
        out_specs=(VMEM,) * len(kept),
        scratch_shapes=[pltpu.VMEM(a.shape, a.dtype) for a in (taps, scale, shift)]
        + [pltpu.SemaphoreType.DMA((len(arrays),))],
        compiler_params=params(ALONE),
        cost_estimate=pl.CostEstimate(flops=0, bytes_accessed=8 << 20, transcendentals=0),
        name="hold_call",
    )(*arrays)


def plan_sizes(tiles_dev):
    held = tiles_dev + 2
    return held, 3 * held, 4 * held + tiles_dev


def tables_kernel(
    me_ref, source_ref, utt_ref, plan_ref, bias_ref, padded_ref,
    key_utt_ref, query_utt_ref, filled, ranks, key_utts,
):
    me = me_ref[0]
    total = source_ref.shape[0]
    tiles_dev = total // COUNT
    per_pair = tiles_dev // COUNT
    quarter_tiles = per_pair
    for pair in range(COUNT * COUNT):
        filled[pair] = 0

    def one(position, carried):
        pair = divide(source_ref[position], tiles_dev) * COUNT + divide(position, tiles_dev)
        rank = filled[pair]
        filled[pair] = rank + 1
        ranks[position] = rank
        key_utts[pair * per_pair + rank] = utt_ref[position]
        return carried

    lax.fori_loop(0, total, one, 0, unroll=4)
    is_end = (me == 0) | (me == COUNT - 1)
    second = jnp.where(is_end, 2, 3)
    third = jnp.where(is_end, 3, 2)
    held, places_at, _ = plan_sizes(tiles_dev)
    for i in range(held):
        position = jnp.clip(me * tiles_dev - 1 + i, 0, total - 1)
        source = divide(source_ref[position], tiles_dev)
        apart = me ^ source
        quarter = quarter_of(source, divide(position, tiles_dev))
        row = quarter * quarter_tiles + ranks[position]
        early = jnp.where(apart == 0, row, -1)
        near_last = (apart == 1) & (quarter == COUNT - 1)
        early = jnp.where((apart == 1) & (quarter < COUNT - 1), tiles_dev + row, early)
        plan_ref[2 * held + i] = jnp.where(apart == second, row - quarter_tiles, -1)
        plan_ref[i] = early
        plan_ref[held + i] = jnp.where((apart == third) | near_last, row, -1)
        query_utt_ref[i * TILE : (i + 1) * TILE] = jnp.full(
            (TILE, 128), utt_ref[position], jnp.int32
        )
    plan_places(me, utt_ref, tiles_dev, total, plan_ref, places_at)

    near, second, far = me ^ 1, me ^ second, me ^ third
    order = [(me, quarter, False) for quarter in (0, 1, 2, 3)]
    order += [(near, quarter, False) for quarter in (0, 1, 2)]
    order += [(second, quarter, False) for quarter in (1, 2, 3)]
    order += [(near, 3, True), (second, 0, True), (far, 3, True)]
    order += [(far, quarter, False) for quarter in (0, 1, 2)]
    lane_tile = lax.broadcasted_iota(jnp.int32, (1, 128), 1) // TILE
    tile_values = []
    for shard, quarter, inner_only in order:
        target = quarter_of(shard, quarter)
        for rank in range(per_pair):
            utt = key_utts[(shard * COUNT + target) * per_pair + rank]
            if inner_only:
                utt = jnp.where(is_end, -1, utt)
            tile_values.append(utt)
    per_vector = 128 // TILE
    for start in range(0, len(tile_values), per_vector):
        vector = jnp.full((1, 128), tile_values[start], jnp.int32)
        for k in range(1, per_vector):
            vector = jnp.where(lane_tile == k, tile_values[start + k], vector)
        key_utt_ref[:, start * TILE : start * TILE + 128] = vector
    bias_ref[...] = mask_bias(query_utt_ref[:, :1], key_utt_ref[...])
    padded_ref[...] = jnp.zeros_like(padded_ref)


def place_tiles(grouped, rows, plan, at):
    for i in range(grouped.shape[0] // TILE):
        place = plan[at + i]

        @pl.when(place >= 0)
        def _(place=place, i=i):
            grouped[i * TILE : (i + 1) * TILE] = rows[
                pl.ds(pl.multiple_of(place * TILE, TILE), TILE), :
            ]


def early_kernel(
    plan, low, last, near, key_weight, value_weight, key_ref, value_ref, grouped, rows
):
    piece, quarter_rows = low.shape[0], last.shape[0]
    base = piece + quarter_rows
    rows[0:piece] = low[...]
    rows[piece:base] = last[...]
    rows[base:] = near[...]
    grouped[...] = jnp.zeros_like(grouped)
    place_tiles(grouped, rows, plan, 0)
    normed = layer_norm(rows[...]).astype(jnp.bfloat16)
    key_ref[...] = project(normed, key_weight)
    value_ref[...] = project(normed, value_weight)


def second_kernel(
    me_ref, plan, early_grouped, inner, inner_end, key_weight, value_weight,
    key_ref, value_ref, grouped, rows,
):
    me = me_ref[0]
    is_end = (me == 0) | (me == COUNT - 1)

    @pl.when(is_end)
    def _():
        rows[...] = inner_end[...]

    @pl.when(jnp.logical_not(is_end))
    def _():
        rows[...] = inner[...]

    place_tiles(grouped, rows, plan, 2 * (grouped.shape[0] // TILE))
    normed = layer_norm(rows[...]).astype(jnp.bfloat16)
    key_ref[...] = project(normed, key_weight)
    value_ref[...] = project(normed, value_weight)


def middle_kernel(*refs):
    parts, (key_weight, value_weight, key_ref, value_ref) = refs[:-4], refs[-4:]
    rows = jnp.concatenate([part[...] for part in parts], axis=0)
    normed = layer_norm(rows).astype(jnp.bfloat16)
    key_ref[...] = project(normed, key_weight)
    value_ref[...] = project(normed, value_weight)


def final_kernel(
    me_ref, plan, bias, early_grouped, early_padded, far, far_end, near_last,
    early_key, early_value, second_key, second_value, middle_key, middle_value,
    key_weight, value_weight, query_weight, output_weight, half_taps, half_shift,
    out_hbm, grouped, padded, residual_rows, out, write_sems, late,
):
    me = me_ref[0]
    is_end = (me == 0) | (me == COUNT - 1)
    held, places_at, _ = plan_sizes(out.shape[0] // TILE)
    late[far.shape[0] :] = near_last[...]

    @pl.when(is_end)
    def _():
        late[: far.shape[0]] = far_end[...]

    @pl.when(jnp.logical_not(is_end))
    def _():
        late[: far.shape[0]] = far[...]

    place_tiles(grouped, late, plan, held)
    normed = layer_norm(late[: far.shape[0]]).astype(jnp.bfloat16)
    late_key = project(normed, key_weight)
    late_value = project(normed, value_weight)
    residual = attend(
        grouped, bias,
        [early_key, second_key, middle_key, late_key],
        [early_value, second_value, middle_value, late_value],
        query_weight, output_weight,
    )
    convolve(
        residual, plan, places_at, half_taps, half_shift[...], out_hbm, padded, residual_rows,
        out, write_sems,
    )


def line_block(
    frames, tile_source, tile_utt, query_weight, key_weight, value_weight, output_weight,
    depth_weight, bn_scale, bn_shift,
):
    me = lax.axis_index("ctx").reshape(1)
    rows_dev, width = frames.shape
    quarter = rows_dev // COUNT
    piece = rows_dev - quarter
    total = tile_source.shape[0]
    wide = key_weight.shape[1]

    def shape(rows, columns=width, kind=jnp.bfloat16):
        return jax.ShapeDtypeStruct((rows, columns), kind)

    def cost(rows):
        return pl.CostEstimate(
            flops=4 * rows * width * wide, bytes_accessed=rows * width * 4, transcendentals=rows
        )

    low, last, high, start = pl.pallas_call(
        arrange_kernel,
        out_shape=tuple(pltpu.VMEM((n, width), frames.dtype) for n in (piece, quarter, piece, quarter)),
        in_specs=[SMEM] + [HBM] * 2,
        out_specs=(VMEM,) * 4,
        scratch_shapes=[
            pltpu.SMEM((total,), jnp.int32),
            pltpu.VMEM((rows_dev, width), jnp.bfloat16),
            pltpu.SMEM((rows_dev // TILE + 1,), jnp.int32),
            pltpu.SemaphoreType.DMA((2,)),
        ],
        compiler_params=params(ALONE),
        name="arrange",
    )(me, tile_source, frames)

    def swap(value, perm):
        return lax.ppermute(value, "ctx", perm)

    near = swap(low, SWAP_OUTER)
    inner = swap(high, SWAP_INNER)
    held_rows = rows_dev + 2 * TILE
    padded_shape = jax.ShapeDtypeStruct(
        (width // 128, padded_rows(rows_dev // TILE), 128), jnp.float32
    )
    plan, bias, padded = pl.pallas_call(
        tables_kernel,
        out_shape=(
            jax.ShapeDtypeStruct((plan_sizes(rows_dev // TILE)[2],), jnp.int32),
            shape(held_rows, total * TILE, jnp.float32),
            padded_shape,
        ),
        in_specs=[SMEM] * 3,
        out_specs=(SMEM, VMEM, VMEM),
        scratch_shapes=[
            pltpu.VMEM((1, total * TILE), jnp.int32),
            pltpu.VMEM((held_rows, 128), jnp.int32),
        ]
        + [pltpu.SMEM((n,), jnp.int32) for n in (COUNT * COUNT, total, total)],
        compiler_params=params(8),
        name="tables_call",
    )(me, tile_source, tile_utt)
    key_weight, value_weight, query_weight, output_weight, half_taps, half_shift = hold(
        key_weight, value_weight, query_weight, output_weight, depth_weight,
        bn_scale.reshape(1, -1), bn_shift.reshape(1, -1),
    )
    far = swap(low, OVER_TWO)
    inner_end = swap(inner, TO_ENDS)
    far_end = swap(far, TO_ENDS)
    far_last = swap(last, OVER_TWO)
    near_last = swap(last, FROM_ENDS)
    inner_start = swap(start, SWAP_INNER)

    early_rows = rows_dev + piece
    early_key, early_value, grouped = pl.pallas_call(
        early_kernel,
        out_shape=(shape(early_rows, wide), shape(early_rows, wide), shape(held_rows)),
        in_specs=[SMEM] + [VMEM] * 5,
        out_specs=(VMEM,) * 3,
        scratch_shapes=[pltpu.VMEM((early_rows, width), jnp.bfloat16)],
        compiler_params=params(12),
        cost_estimate=cost(early_rows),
        name="early_call",
    )(plan, low, last, near, key_weight, value_weight)
    second_key, second_value, grouped = pl.pallas_call(
        second_kernel,
        out_shape=(shape(piece, wide), shape(piece, wide), shape(held_rows)),
        in_specs=[SMEM] * 2 + [VMEM] * 5,
        out_specs=(VMEM,) * 3,
        input_output_aliases={2: 2},
        scratch_shapes=[pltpu.VMEM((piece, width), jnp.bfloat16)],
        compiler_params=params(8),
        cost_estimate=cost(piece),
        name="second_call",
    )(me, plan, grouped, inner, inner_end, key_weight, value_weight)
    middle_key, middle_value = pl.pallas_call(
        middle_kernel,
        out_shape=(shape(3 * quarter, wide),) * 2,
        in_specs=[VMEM] * 5,
        out_specs=(VMEM,) * 2,
        compiler_params=params(8),
        cost_estimate=cost(3 * quarter),
        name="middle_call",
    )(near_last, inner_start, far_last, key_weight, value_weight)
    return pl.pallas_call(
        final_kernel,
        out_shape=(shape(rows_dev), shape(held_rows), padded_shape),
        in_specs=[SMEM] * 2 + [VMEM] * 18,
        out_specs=(HBM, VMEM, VMEM),
        input_output_aliases={3: 1, 4: 2},
        scratch_shapes=block_scratch(rows_dev, width)[1:] + [pltpu.VMEM((rows_dev, width), jnp.bfloat16)],
        compiler_params=params(28),
        cost_estimate=pl.CostEstimate(
            flops=2 << 30, bytes_accessed=8 << 20, transcendentals=1 << 20
        ),
        name="final",
    )(
        me, plan, bias, grouped, padded, far, far_end, near_last,
        early_key, early_value, second_key, second_value, middle_key, middle_value,
        key_weight, value_weight, query_weight, output_weight, half_taps, half_shift,
    )[0]


def per_device(*arrays):
    tiles_dev = arrays[0].shape[0] // TILE
    if lax.axis_size("ctx") == COUNT and tiles_dev % COUNT == 0:
        return line_block(*arrays)
    return ring_block(*arrays)


def solution(mesh):
    return jax.shard_map(
        per_device,
        mesh=mesh,
        in_specs=(P(("dp", "ctx"), None), P("dp"), P("dp"), P(), P(), P(), P(), P(), P(), P()),
        out_specs=P(("dp", "ctx"), None),
        check_vma=False,
    )
```

```python
import functools
import math

import jax
import jax.numpy as jnp
from jax import lax
from jax.experimental import pallas as pl
from jax.experimental.pallas import tpu as pltpu
from jax.sharding import PartitionSpec as P


HEADS = 4
HEAD_DIM = 128
KERNEL = 31
TILE = 16
UTTS = 4
ALONE = 56
NEGATIVE = -1e30

VMEM = pl.BlockSpec(memory_space=pltpu.VMEM)
SMEM = pl.BlockSpec(memory_space=pltpu.SMEM)
HBM = pl.BlockSpec(memory_space=pltpu.HBM)


def params(mib):
    return pltpu.CompilerParams(vmem_limit_bytes=mib << 20)


def layer_norm(rows):
    values = rows.astype(jnp.float32)
    center = values - jnp.mean(values, axis=-1, keepdims=True)
    spread = jnp.mean(center * center, axis=-1, keepdims=True)
    return center * lax.rsqrt(spread + 1e-05)


def project(rows, weight_ref):
    return jnp.dot(rows, weight_ref[...], preferred_element_type=jnp.float32).astype(jnp.bfloat16)


def attend(
    grouped, query_utt, key_utt, key_parts, value_parts, query_weight, output_weight
):
    queries = project(layer_norm(grouped[...]).astype(jnp.bfloat16), query_weight)
    allowed = query_utt[:, :1] == key_utt
    exponent_scale = math.log2(math.e) / math.sqrt(HEAD_DIM)
    heads = []
    for head in range(HEADS):
        columns = slice(head * HEAD_DIM, (head + 1) * HEAD_DIM)
        key_head = jnp.concatenate([part[:, columns] for part in key_parts], axis=0)
        value_head = jnp.concatenate([part[:, columns] for part in value_parts], axis=0)
        scores = lax.dot_general(
            queries[:, columns],
            key_head,
            (((1,), (1,)), ((), ())),
            preferred_element_type=jnp.float32,
        )
        scores = jnp.where(allowed, scores, NEGATIVE)
        top = jnp.max(scores, axis=-1, keepdims=True)
        weights = jnp.exp2((scores - top) * exponent_scale)
        row_sum = jnp.sum(weights, axis=-1, keepdims=True)
        summed = jnp.dot(
            weights.astype(jnp.bfloat16), value_head, preferred_element_type=jnp.float32
        )
        heads.append((summed / row_sum).astype(jnp.bfloat16))
    attended = jnp.concatenate(heads, axis=1)
    return (
        grouped[...].astype(jnp.float32)
        + jnp.dot(attended, output_weight[...], preferred_element_type=jnp.float32)
    ).astype(jnp.bfloat16)


def convolve(residual, plan, at, half_taps, half_shift, out_hbm, padded, residual_rows, out, sems):
    rows_dev, width = out.shape
    tiles_dev = rows_dev // TILE
    held = tiles_dev + 2
    residual_rows[...] = residual[TILE : TILE + rows_dev]
    shaped = layer_norm(residual).astype(jnp.bfloat16).astype(jnp.float32)
    for i in range(held):
        row = pl.multiple_of(plan[at + i] * TILE, TILE)
        for block in range(width // 128):
            padded[block, pl.ds(row, TILE), :] = shaped[
                i * TILE : (i + 1) * TILE, block * 128 : (block + 1) * 128
            ]
    group = math.gcd(tiles_dev, 4)

    def write(step):
        rows = pl.ds(pl.multiple_of(step * group * TILE, TILE), group * TILE)
        return pltpu.make_async_copy(out.at[rows, :], out_hbm.at[rows, :], sems.at[step])

    def some_tiles(step, carried):
        starts = [
            pl.multiple_of(plan[at + held + step * group + k] * TILE, TILE) for k in range(group)
        ]
        for block in range(width // 128):
            columns = slice(block * 128, (block + 1) * 128)
            shift = jnp.broadcast_to(half_shift[:, columns], (8, 128))
            sums = [[shift, shift] for _ in range(group)]
            windows = [{} for _ in range(group)]
            for tap in range(KERNEL):
                weight = half_taps[tap : tap + 1, columns]
                for k in range(group):
                    for part in range(2):
                        offset = tap + 8 * part
                        if offset not in windows[k]:
                            windows[k][offset] = padded[
                                block, pl.ds(starts[k] + (offset - KERNEL // 2), 8), :
                            ]
                        sums[k][part] = sums[k][part] + windows[k][offset] * weight
            for k in range(group):
                half = jnp.concatenate(sums[k], axis=0)
                rows = pl.ds(pl.multiple_of((step * group + k) * TILE, TILE), TILE)
                kept = residual_rows[rows, columns].astype(jnp.float32)
                out[rows, columns] = (kept + (half + half * jnp.tanh(half))).astype(jnp.bfloat16)
        write(step).start()
        return carried

    steps = tiles_dev // group
    lax.fori_loop(0, steps, some_tiles, 0)
    for step in range(steps):
        write(step).wait()


def plan_places(me, utt_ref, tiles_dev, total, plan, at):
    first = me * tiles_dev - 1
    held = tiles_dev + 2
    place = jnp.int32(1)
    before = utt_ref[jnp.clip(first, 0, total - 1)]
    for i in range(held):
        here = utt_ref[jnp.clip(first + i, 0, total - 1)]
        if i:
            place = place + 1 + (here != before).astype(jnp.int32)
        before = here
        inside = (first + i >= 0) & (first + i < total)
        plan[at + i] = jnp.where(inside, place, padded_rows(tiles_dev) // TILE - 1)
        if 1 <= i <= tiles_dev:
            plan[at + held + i - 1] = place


def padded_rows(tiles_dev):
    return (1 + tiles_dev + 2 + (UTTS - 1) + 2) * TILE


def block_scratch(rows_dev, width):
    tiles_dev = rows_dev // TILE
    return [
        pltpu.VMEM((width // 128, padded_rows(tiles_dev), 128), jnp.float32),
        pltpu.VMEM((rows_dev, width), jnp.bfloat16),
        pltpu.VMEM((rows_dev, width), jnp.bfloat16),
        pltpu.SemaphoreType.DMA((tiles_dev // math.gcd(tiles_dev, 4),)),
    ]


def key_value_kernel(rows_ref, key_weight_ref, value_weight_ref, key_ref, value_ref):
    normed = layer_norm(rows_ref[...]).astype(jnp.bfloat16)
    key_ref[...] = project(normed, key_weight_ref)
    value_ref[...] = project(normed, value_weight_ref)


def key_value(rows, key_weight, value_weight):
    shape = jax.ShapeDtypeStruct((rows.shape[0], key_weight.shape[1]), jnp.bfloat16)
    flops = 4 * rows.shape[0] * rows.shape[1] * key_weight.shape[1]
    return pl.pallas_call(
        key_value_kernel,
        out_shape=(shape, shape),
        in_specs=[VMEM] * 3,
        out_specs=(VMEM, VMEM),
        cost_estimate=pl.CostEstimate(flops=flops, bytes_accessed=3 << 20, transcendentals=0),
        name="key_value",
    )(rows, key_weight, value_weight)


def ring_kernel(count, me_ref, source_ref, utt_ref, key_utt_ref, *refs):
    chunks = refs[:count]
    keys = refs[count : 2 * count]
    values = refs[2 * count : 3 * count]
    query_weight, output_weight, taps, scale, shift, out_hbm = refs[3 * count : 3 * count + 6]
    padded, residual_rows, out, write_sems = refs[3 * count + 6 : 3 * count + 10]
    grouped, query_utt, half_taps, plan, sems = refs[3 * count + 10 :]
    me = me_ref[0]
    tiles_dev = out.shape[0] // TILE
    held = tiles_dev + 2
    total = tiles_dev * count
    first = me * tiles_dev - 1
    padded[...] = jnp.zeros_like(padded)
    half_taps[...] = taps[...] * (0.5 * scale[...])
    for i in range(held):
        position = jnp.clip(first + i, 0, total - 1)
        source = source_ref[position]
        row = pl.multiple_of((source % tiles_dev) * TILE, TILE)
        behind = lax.rem(me - source // tiles_dev + count, count)
        for step in range(count):

            @pl.when(behind == step)
            def _(step=step, row=row, i=i):
                pltpu.make_async_copy(
                    chunks[step].at[pl.ds(row, TILE), :],
                    grouped.at[pl.ds(i * TILE, TILE), :],
                    sems.at[i],
                ).start()

        query_utt[pl.ds(i * TILE, TILE), :] = jnp.full((TILE, 128), utt_ref[position], jnp.int32)
    plan_places(me, utt_ref, tiles_dev, total, plan, 0)
    for i in range(held):
        pltpu.make_async_copy(
            chunks[0].at[pl.ds(0, TILE), :], grouped.at[pl.ds(i * TILE, TILE), :], sems.at[i]
        ).wait()
    residual = attend(
        grouped, query_utt, key_utt_ref[...], keys, values, query_weight, output_weight
    )
    convolve(
        residual, plan, 0, half_taps, 0.5 * shift[...], out_hbm, padded, residual_rows, out,
        write_sems,
    )


def ring_block(
    frames, tile_source, tile_utt, query_weight, key_weight, value_weight, output_weight,
    depth_weight, bn_scale, bn_shift,
):
    count = lax.axis_size("ctx")
    me = lax.axis_index("ctx")
    rows_dev, width = frames.shape
    tiles_dev = rows_dev // TILE
    ring = [(i, (i + 1) % count) for i in range(count)]
    chunks = [frames]
    for _ in range(count - 1):
        chunks.append(lax.ppermute(chunks[-1], "ctx", ring))
    pairs = [key_value(chunk, key_weight, value_weight) for chunk in chunks]
    shards = lax.rem(me - jnp.arange(count, dtype=jnp.int32) + count, count)
    arrived = (shards[:, None] * tiles_dev + jnp.arange(tiles_dev, dtype=jnp.int32)).reshape(-1)
    key_utt = jnp.sum(
        jnp.where(arrived[:, None] == tile_source[None, :], tile_utt[None, :], 0), axis=1
    )
    key_utt = jnp.repeat(key_utt, TILE).reshape(1, -1)
    return pl.pallas_call(
        functools.partial(ring_kernel, count),
        out_shape=jax.ShapeDtypeStruct((rows_dev, width), jnp.bfloat16),
        in_specs=[SMEM] * 3
        + [VMEM]
        + [pl.BlockSpec(memory_space=pl.ANY)] * count
        + [VMEM] * (2 * count + 5),
        out_specs=HBM,
        scratch_shapes=block_scratch(rows_dev, width)
        + [
            pltpu.VMEM((rows_dev + 2 * TILE, width), jnp.bfloat16),
            pltpu.VMEM((rows_dev + 2 * TILE, 128), jnp.int32),
            pltpu.VMEM(depth_weight.shape, jnp.float32),
            pltpu.SMEM((2 * tiles_dev + 2,), jnp.int32),
            pltpu.SemaphoreType.DMA((tiles_dev + 2,)),
        ],
        cost_estimate=pl.CostEstimate(
            flops=2 << 30, bytes_accessed=8 << 20, transcendentals=1 << 20
        ),
        name="ring_block",
    )(
        me.reshape(1), tile_source, tile_utt, key_utt, *chunks,
        *[pair[0] for pair in pairs], *[pair[1] for pair in pairs],
        query_weight, output_weight, depth_weight, bn_scale.reshape(1, -1), bn_shift.reshape(1, -1),
    )


COUNT = 4
SWAP_OUTER = [(0, 1), (1, 0), (2, 3), (3, 2)]
SWAP_INNER = [(1, 2), (2, 1)]
TO_ENDS = [(1, 0), (2, 3)]
FROM_ENDS = [(0, 1), (3, 2)]
OVER_TWO = [(0, 2), (3, 1)]


def quarter_of(source_shard, target):
    return jnp.where(source_shard % 2 == 1, target, COUNT - 1 - target)


def divide(value, by):
    if by & (by - 1) == 0:
        return value >> (by.bit_length() - 1)
    return lax.div(value, by)


def arrange_kernel(
    me_ref, source_hbm, rows_hbm, low_ref, last_ref, high_ref, start_ref, source_ref, rows, slots, sems
):
    me = me_ref[0]
    rows_dev, quarter_rows = rows.shape[0], last_ref.shape[0]
    tiles_dev = rows_dev // TILE
    per_pair = tiles_dev // COUNT
    rows_copy = pltpu.make_async_copy(rows_hbm, rows, sems.at[0])
    source_copy = pltpu.make_async_copy(source_hbm, source_ref, sems.at[1])
    source_copy.start()
    rows_copy.start()
    source_copy.wait()
    for target in range(COUNT):
        place = quarter_of(me, target) * per_pair
        for position in range(target * tiles_dev, (target + 1) * tiles_dev):
            source = source_ref[position]
            shard = divide(source, tiles_dev)
            mine = shard == me
            slots[jnp.where(mine, place, tiles_dev)] = source - shard * tiles_dev
            place = place + mine.astype(jnp.int32)
    rows_copy.wait()
    for place in range(tiles_dev):
        tile = rows[pl.ds(pl.multiple_of(slots[place] * TILE, TILE), TILE), :]
        row = place * TILE
        if row < rows_dev - quarter_rows:
            low_ref[row : row + TILE] = tile
        else:
            row_here = row - (rows_dev - quarter_rows)
            last_ref[row_here : row_here + TILE] = tile
        if row >= quarter_rows:
            high_ref[row - quarter_rows : row - quarter_rows + TILE] = tile
        else:
            start_ref[row : row + TILE] = tile


def hold_kernel(*refs):
    count = (len(refs) - 3) // 2
    arrays, kept = refs[:count], refs[count : 2 * count - 1]
    taps, scale, shift, sems = refs[2 * count - 1 :]
    targets = (*kept[:-2], taps, scale, shift)
    copies = [
        pltpu.make_async_copy(array, target, sems.at[i])
        for i, (array, target) in enumerate(zip(arrays, targets))
    ]
    for copy in copies:
        copy.start()
    for copy in copies:
        copy.wait()
    kept[-2][...] = taps[...] * (0.5 * scale[...])
    kept[-1][...] = 0.5 * shift[...]


def hold(*arrays):
    taps, scale, shift = arrays[-3:]
    kept = (*arrays[:-2], shift)
    return pl.pallas_call(
        hold_kernel,
        out_shape=tuple(pltpu.VMEM(a.shape, a.dtype) for a in kept),
        in_specs=[HBM] * len(arrays),
        out_specs=(VMEM,) * len(kept),
        scratch_shapes=[pltpu.VMEM(a.shape, a.dtype) for a in (taps, scale, shift)]
        + [pltpu.SemaphoreType.DMA((len(arrays),))],
        compiler_params=params(ALONE),
        cost_estimate=pl.CostEstimate(flops=0, bytes_accessed=8 << 20, transcendentals=0),
        name="hold_call",
    )(*arrays)


def plan_sizes(tiles_dev):
    held = tiles_dev + 2
    return held, 3 * held, 4 * held + tiles_dev


def tables_kernel(
    me_ref, source_ref, utt_ref, plan_ref, key_utt_ref, query_utt_ref, padded_ref,
    filled, ranks, key_utts,
):
    me = me_ref[0]
    total = source_ref.shape[0]
    tiles_dev = total // COUNT
    per_pair = tiles_dev // COUNT
    quarter_tiles = per_pair
    for pair in range(COUNT * COUNT):
        filled[pair] = 0

    def one(position, carried):
        pair = divide(source_ref[position], tiles_dev) * COUNT + divide(position, tiles_dev)
        rank = filled[pair]
        filled[pair] = rank + 1
        ranks[position] = rank
        key_utts[pair * per_pair + rank] = utt_ref[position]
        return carried

    lax.fori_loop(0, total, one, 0, unroll=4)
    is_end = (me == 0) | (me == COUNT - 1)
    second = jnp.where(is_end, 2, 3)
    third = jnp.where(is_end, 3, 2)
    held, places_at, _ = plan_sizes(tiles_dev)
    for i in range(held):
        position = jnp.clip(me * tiles_dev - 1 + i, 0, total - 1)
        source = divide(source_ref[position], tiles_dev)
        apart = me ^ source
        quarter = quarter_of(source, divide(position, tiles_dev))
        row = quarter * quarter_tiles + ranks[position]
        early = jnp.where(apart == 0, row, -1)
        near_last = (apart == 1) & (quarter == COUNT - 1)
        early = jnp.where((apart == 1) & (quarter < COUNT - 1), tiles_dev + row, early)
        plan_ref[2 * held + i] = jnp.where(apart == second, row - quarter_tiles, -1)
        plan_ref[i] = early
        plan_ref[held + i] = jnp.where((apart == third) | near_last, row, -1)
        query_utt_ref[i * TILE : (i + 1) * TILE] = jnp.full(
            (TILE, 128), utt_ref[position], jnp.int32
        )
    plan_places(me, utt_ref, tiles_dev, total, plan_ref, places_at)

    near, second, far = me ^ 1, me ^ second, me ^ third
    order = [(me, quarter, False) for quarter in (0, 1, 2, 3)]
    order += [(near, quarter, False) for quarter in (0, 1, 2)]
    order += [(second, quarter, False) for quarter in (1, 2, 3)]
    order += [(near, 3, True), (second, 0, True), (far, 3, True)]
    order += [(far, quarter, False) for quarter in (0, 1, 2)]
    lane_tile = lax.broadcasted_iota(jnp.int32, (1, 128), 1) // TILE
    tile_values = []
    for shard, quarter, inner_only in order:
        target = quarter_of(shard, quarter)
        for rank in range(per_pair):
            utt = key_utts[(shard * COUNT + target) * per_pair + rank]
            if inner_only:
                utt = jnp.where(is_end, -1, utt)
            tile_values.append(utt)
    per_vector = 128 // TILE
    for start in range(0, len(tile_values), per_vector):
        vector = jnp.full((1, 128), tile_values[start], jnp.int32)
        for k in range(1, per_vector):
            vector = jnp.where(lane_tile == k, tile_values[start + k], vector)
        key_utt_ref[:, start * TILE : start * TILE + 128] = vector
    padded_ref[...] = jnp.zeros_like(padded_ref)


def place_tiles(grouped, rows, plan, at):
    for i in range(grouped.shape[0] // TILE):
        place = plan[at + i]

        @pl.when(place >= 0)
        def _(place=place, i=i):
            grouped[i * TILE : (i + 1) * TILE] = rows[
                pl.ds(pl.multiple_of(place * TILE, TILE), TILE), :
            ]


def early_kernel(
    plan, low, last, near, key_weight, value_weight, key_ref, value_ref, grouped, rows
):
    piece, quarter_rows = low.shape[0], last.shape[0]
    base = piece + quarter_rows
    rows[0:piece] = low[...]
    rows[piece:base] = last[...]
    rows[base:] = near[...]
    grouped[...] = jnp.zeros_like(grouped)
    place_tiles(grouped, rows, plan, 0)
    normed = layer_norm(rows[...]).astype(jnp.bfloat16)
    key_ref[...] = project(normed, key_weight)
    value_ref[...] = project(normed, value_weight)


def second_kernel(
    me_ref, plan, early_grouped, inner, inner_end, key_weight, value_weight,
    key_ref, value_ref, grouped, rows,
):
    me = me_ref[0]
    is_end = (me == 0) | (me == COUNT - 1)

    @pl.when(is_end)
    def _():
        rows[...] = inner_end[...]

    @pl.when(jnp.logical_not(is_end))
    def _():
        rows[...] = inner[...]

    place_tiles(grouped, rows, plan, 2 * (grouped.shape[0] // TILE))
    normed = layer_norm(rows[...]).astype(jnp.bfloat16)
    key_ref[...] = project(normed, key_weight)
    value_ref[...] = project(normed, value_weight)


def middle_kernel(*refs):
    parts, (key_weight, value_weight, key_ref, value_ref) = refs[:-4], refs[-4:]
    rows = jnp.concatenate([part[...] for part in parts], axis=0)
    normed = layer_norm(rows).astype(jnp.bfloat16)
    key_ref[...] = project(normed, key_weight)
    value_ref[...] = project(normed, value_weight)


def final_kernel(
    me_ref, plan, query_utt, key_utt, early_grouped, zeros, far, far_end, near_last,
    early_key, early_value, second_key, second_value, middle_key, middle_value,
    key_weight, value_weight, query_weight, output_weight, half_taps, half_shift,
    out_hbm, grouped, padded, residual_rows, out, write_sems, late,
):
    me = me_ref[0]
    is_end = (me == 0) | (me == COUNT - 1)
    held, places_at, _ = plan_sizes(out.shape[0] // TILE)
    late[far.shape[0] :] = near_last[...]

    @pl.when(is_end)
    def _():
        late[: far.shape[0]] = far_end[...]

    @pl.when(jnp.logical_not(is_end))
    def _():
        late[: far.shape[0]] = far[...]

    place_tiles(grouped, late, plan, held)
    normed = layer_norm(late[: far.shape[0]]).astype(jnp.bfloat16)
    late_key = project(normed, key_weight)
    late_value = project(normed, value_weight)
    residual = attend(
        grouped, query_utt, key_utt[...],
        [early_key, second_key, middle_key, late_key],
        [early_value, second_value, middle_value, late_value],
        query_weight, output_weight,
    )
    convolve(
        residual, plan, places_at, half_taps, half_shift[...], out_hbm, padded, residual_rows,
        out, write_sems,
    )


def line_block(
    frames, tile_source, tile_utt, query_weight, key_weight, value_weight, output_weight,
    depth_weight, bn_scale, bn_shift,
):
    me = lax.axis_index("ctx").reshape(1)
    rows_dev, width = frames.shape
    quarter = rows_dev // COUNT
    piece = rows_dev - quarter
    total = tile_source.shape[0]
    wide = key_weight.shape[1]

    def shape(rows, columns=width, kind=jnp.bfloat16):
        return jax.ShapeDtypeStruct((rows, columns), kind)

    def cost(rows):
        return pl.CostEstimate(
            flops=4 * rows * width * wide, bytes_accessed=rows * width * 4, transcendentals=rows
        )

    low, last, high, start = pl.pallas_call(
        arrange_kernel,
        out_shape=tuple(pltpu.VMEM((n, width), frames.dtype) for n in (piece, quarter, piece, quarter)),
        in_specs=[SMEM] + [HBM] * 2,
        out_specs=(VMEM,) * 4,
        scratch_shapes=[
            pltpu.SMEM((total,), jnp.int32),
            pltpu.VMEM((rows_dev, width), jnp.bfloat16),
            pltpu.SMEM((rows_dev // TILE + 1,), jnp.int32),
            pltpu.SemaphoreType.DMA((2,)),
        ],
        compiler_params=params(ALONE),
        name="arrange",
    )(me, tile_source, frames)

    def swap(value, perm):
        return lax.ppermute(value, "ctx", perm)

    near = swap(low, SWAP_OUTER)
    inner = swap(high, SWAP_INNER)
    held_rows = rows_dev + 2 * TILE
    padded_shape = jax.ShapeDtypeStruct(
        (width // 128, padded_rows(rows_dev // TILE), 128), jnp.float32
    )
    plan, key_utt, query_utt, padded = pl.pallas_call(
        tables_kernel,
        out_shape=(
            jax.ShapeDtypeStruct((plan_sizes(rows_dev // TILE)[2],), jnp.int32),
            shape(1, total * TILE, jnp.int32),
            shape(held_rows, 128, jnp.int32),
            padded_shape,
        ),
        in_specs=[SMEM] * 3,
        out_specs=(SMEM, VMEM, VMEM, VMEM),
        scratch_shapes=[pltpu.SMEM((n,), jnp.int32) for n in (COUNT * COUNT, total, total)],
        compiler_params=params(8),
        name="tables_call",
    )(me, tile_source, tile_utt)
    key_weight, value_weight, query_weight, output_weight, half_taps, half_shift = hold(
        key_weight, value_weight, query_weight, output_weight, depth_weight,
        bn_scale.reshape(1, -1), bn_shift.reshape(1, -1),
    )
    far = swap(low, OVER_TWO)
    inner_end = swap(inner, TO_ENDS)
    far_end = swap(far, TO_ENDS)
    far_last = swap(last, OVER_TWO)
    near_last = swap(last, FROM_ENDS)
    inner_start = swap(start, SWAP_INNER)

    early_rows = rows_dev + piece
    early_key, early_value, grouped = pl.pallas_call(
        early_kernel,
        out_shape=(shape(early_rows, wide), shape(early_rows, wide), shape(held_rows)),
        in_specs=[SMEM] + [VMEM] * 5,
        out_specs=(VMEM,) * 3,
        scratch_shapes=[pltpu.VMEM((early_rows, width), jnp.bfloat16)],
        compiler_params=params(12),
        cost_estimate=cost(early_rows),
        name="early_call",
    )(plan, low, last, near, key_weight, value_weight)
    second_key, second_value, grouped = pl.pallas_call(
        second_kernel,
        out_shape=(shape(piece, wide), shape(piece, wide), shape(held_rows)),
        in_specs=[SMEM] * 2 + [VMEM] * 5,
        out_specs=(VMEM,) * 3,
        input_output_aliases={2: 2},
        scratch_shapes=[pltpu.VMEM((piece, width), jnp.bfloat16)],
        compiler_params=params(8),
        cost_estimate=cost(piece),
        name="second_call",
    )(me, plan, grouped, inner, inner_end, key_weight, value_weight)
    middle_key, middle_value = pl.pallas_call(
        middle_kernel,
        out_shape=(shape(3 * quarter, wide),) * 2,
        in_specs=[VMEM] * 5,
        out_specs=(VMEM,) * 2,
        compiler_params=params(8),
        cost_estimate=cost(3 * quarter),
        name="middle_call",
    )(near_last, inner_start, far_last, key_weight, value_weight)
    return pl.pallas_call(
        final_kernel,
        out_shape=(shape(rows_dev), shape(held_rows), padded_shape),
        in_specs=[SMEM] * 2 + [VMEM] * 19,
        out_specs=(HBM, VMEM, VMEM),
        input_output_aliases={4: 1, 5: 2},
        scratch_shapes=block_scratch(rows_dev, width)[1:] + [pltpu.VMEM((rows_dev, width), jnp.bfloat16)],
        compiler_params=params(28),
        cost_estimate=pl.CostEstimate(
            flops=2 << 30, bytes_accessed=8 << 20, transcendentals=1 << 20
        ),
        name="final",
    )(
        me, plan, query_utt, key_utt, grouped, padded, far, far_end, near_last,
        early_key, early_value, second_key, second_value, middle_key, middle_value,
        key_weight, value_weight, query_weight, output_weight, half_taps, half_shift,
    )[0]


def per_device(*arrays):
    tiles_dev = arrays[0].shape[0] // TILE
    if lax.axis_size("ctx") == COUNT and tiles_dev % COUNT == 0:
        return line_block(*arrays)
    return ring_block(*arrays)


def solution(mesh):
    return jax.shard_map(
        per_device,
        mesh=mesh,
        in_specs=(P(("dp", "ctx"), None), P("dp"), P("dp"), P(), P(), P(), P(), P(), P(), P()),
        out_specs=P(("dp", "ctx"), None),
        check_vma=False,
    )
```

```python
import functools
import math

import jax
import jax.numpy as jnp
from jax import lax
from jax.experimental import pallas as pl
from jax.experimental.pallas import tpu as pltpu
from jax.sharding import PartitionSpec as P


HEADS = 4
HEAD_DIM = 128
KERNEL = 31
TILE = 16
UTTS = 4
ALONE = 56
NEGATIVE = -1e30

VMEM = pl.BlockSpec(memory_space=pltpu.VMEM)
SMEM = pl.BlockSpec(memory_space=pltpu.SMEM)
HBM = pl.BlockSpec(memory_space=pltpu.HBM)


def params(mib):
    return pltpu.CompilerParams(vmem_limit_bytes=mib << 20)


def layer_norm(rows):
    values = rows.astype(jnp.float32)
    center = values - jnp.mean(values, axis=-1, keepdims=True)
    spread = jnp.mean(center * center, axis=-1, keepdims=True)
    return center * lax.rsqrt(spread + 1e-05)


def project(rows, weight_ref):
    return jnp.dot(rows, weight_ref[...], preferred_element_type=jnp.float32).astype(jnp.bfloat16)


def attend(
    grouped, query_utt, key_utt, key_parts, value_parts, query_weight, output_weight
):
    queries = project(layer_norm(grouped[...]).astype(jnp.bfloat16), query_weight)
    allowed = query_utt[:, :1] == key_utt
    exponent_scale = math.log2(math.e) / math.sqrt(HEAD_DIM)
    heads = []
    for head in range(HEADS):
        columns = slice(head * HEAD_DIM, (head + 1) * HEAD_DIM)
        key_head = jnp.concatenate([part[:, columns] for part in key_parts], axis=0)
        value_head = jnp.concatenate([part[:, columns] for part in value_parts], axis=0)
        scores = lax.dot_general(
            queries[:, columns],
            key_head,
            (((1,), (1,)), ((), ())),
            preferred_element_type=jnp.float32,
        )
        scores = jnp.where(allowed, scores, NEGATIVE)
        top = jnp.max(scores, axis=-1, keepdims=True)
        weights = jnp.exp2((scores - top) * exponent_scale)
        row_sum = jnp.sum(weights, axis=-1, keepdims=True)
        summed = jnp.dot(
            weights.astype(jnp.bfloat16), value_head, preferred_element_type=jnp.float32
        )
        heads.append((summed / row_sum).astype(jnp.bfloat16))
    attended = jnp.concatenate(heads, axis=1)
    return (
        grouped[...].astype(jnp.float32)
        + jnp.dot(attended, output_weight[...], preferred_element_type=jnp.float32)
    ).astype(jnp.bfloat16)


def convolve(residual, plan, at, half_taps, half_shift, out_hbm, padded, residual_rows, out, sems):
    rows_dev, width = out.shape
    tiles_dev = rows_dev // TILE
    held = tiles_dev + 2
    residual_rows[...] = residual[TILE : TILE + rows_dev]
    shaped = layer_norm(residual).astype(jnp.bfloat16).astype(jnp.float32)
    for i in range(held):
        row = pl.multiple_of(plan[at + i] * TILE, TILE)
        for block in range(width // 128):
            padded[block, pl.ds(row, TILE), :] = shaped[
                i * TILE : (i + 1) * TILE, block * 128 : (block + 1) * 128
            ]
    group = math.gcd(tiles_dev, 4)

    def write(step):
        rows = pl.ds(pl.multiple_of(step * group * TILE, TILE), group * TILE)
        return pltpu.make_async_copy(out.at[rows, :], out_hbm.at[rows, :], sems.at[step])

    def some_tiles(step, carried):
        starts = [
            pl.multiple_of(plan[at + held + step * group + k] * TILE, TILE) for k in range(group)
        ]
        for block in range(width // 128):
            columns = slice(block * 128, (block + 1) * 128)
            shift = jnp.broadcast_to(half_shift[:, columns], (8, 128))
            sums = [[shift, shift] for _ in range(group)]
            windows = [{} for _ in range(group)]
            for tap in range(KERNEL):
                weight = half_taps[tap : tap + 1, columns]
                for k in range(group):
                    for part in range(2):
                        offset = tap + 8 * part
                        if offset not in windows[k]:
                            windows[k][offset] = padded[
                                block, pl.ds(starts[k] + (offset - KERNEL // 2), 8), :
                            ]
                        sums[k][part] = sums[k][part] + windows[k][offset] * weight
            for k in range(group):
                half = jnp.concatenate(sums[k], axis=0)
                rows = pl.ds(pl.multiple_of((step * group + k) * TILE, TILE), TILE)
                kept = residual_rows[rows, columns].astype(jnp.float32)
                out[rows, columns] = (kept + (half + half * jnp.tanh(half))).astype(jnp.bfloat16)
        write(step).start()
        return carried

    steps = tiles_dev // group
    lax.fori_loop(0, steps, some_tiles, 0)
    for step in range(steps):
        write(step).wait()


def plan_places(me, utt_ref, tiles_dev, total, plan, at):
    first = me * tiles_dev - 1
    held = tiles_dev + 2
    place = jnp.int32(1)
    before = utt_ref[jnp.clip(first, 0, total - 1)]
    for i in range(held):
        here = utt_ref[jnp.clip(first + i, 0, total - 1)]
        if i:
            place = place + 1 + (here != before).astype(jnp.int32)
        before = here
        inside = (first + i >= 0) & (first + i < total)
        plan[at + i] = jnp.where(inside, place, padded_rows(tiles_dev) // TILE - 1)
        if 1 <= i <= tiles_dev:
            plan[at + held + i - 1] = place


def padded_rows(tiles_dev):
    return (1 + tiles_dev + 2 + (UTTS - 1) + 2) * TILE


def block_scratch(rows_dev, width):
    tiles_dev = rows_dev // TILE
    return [
        pltpu.VMEM((width // 128, padded_rows(tiles_dev), 128), jnp.float32),
        pltpu.VMEM((rows_dev, width), jnp.bfloat16),
        pltpu.VMEM((rows_dev, width), jnp.bfloat16),
        pltpu.SemaphoreType.DMA((tiles_dev // math.gcd(tiles_dev, 4),)),
    ]


def key_value_kernel(rows_ref, key_weight_ref, value_weight_ref, key_ref, value_ref):
    normed = layer_norm(rows_ref[...]).astype(jnp.bfloat16)
    key_ref[...] = project(normed, key_weight_ref)
    value_ref[...] = project(normed, value_weight_ref)


def key_value(rows, key_weight, value_weight):
    shape = jax.ShapeDtypeStruct((rows.shape[0], key_weight.shape[1]), jnp.bfloat16)
    flops = 4 * rows.shape[0] * rows.shape[1] * key_weight.shape[1]
    return pl.pallas_call(
        key_value_kernel,
        out_shape=(shape, shape),
        in_specs=[VMEM] * 3,
        out_specs=(VMEM, VMEM),
        cost_estimate=pl.CostEstimate(flops=flops, bytes_accessed=3 << 20, transcendentals=0),
        name="key_value",
    )(rows, key_weight, value_weight)


def ring_kernel(count, me_ref, source_ref, utt_ref, key_utt_ref, *refs):
    chunks = refs[:count]
    keys = refs[count : 2 * count]
    values = refs[2 * count : 3 * count]
    query_weight, output_weight, taps, scale, shift, out_hbm = refs[3 * count : 3 * count + 6]
    padded, residual_rows, out, write_sems = refs[3 * count + 6 : 3 * count + 10]
    grouped, query_utt, half_taps, plan, sems = refs[3 * count + 10 :]
    me = me_ref[0]
    tiles_dev = out.shape[0] // TILE
    held = tiles_dev + 2
    total = tiles_dev * count
    first = me * tiles_dev - 1
    padded[...] = jnp.zeros_like(padded)
    half_taps[...] = taps[...] * (0.5 * scale[...])
    for i in range(held):
        position = jnp.clip(first + i, 0, total - 1)
        source = source_ref[position]
        row = pl.multiple_of((source % tiles_dev) * TILE, TILE)
        behind = lax.rem(me - source // tiles_dev + count, count)
        for step in range(count):

            @pl.when(behind == step)
            def _(step=step, row=row, i=i):
                pltpu.make_async_copy(
                    chunks[step].at[pl.ds(row, TILE), :],
                    grouped.at[pl.ds(i * TILE, TILE), :],
                    sems.at[i],
                ).start()

        query_utt[pl.ds(i * TILE, TILE), :] = jnp.full((TILE, 128), utt_ref[position], jnp.int32)
    plan_places(me, utt_ref, tiles_dev, total, plan, 0)
    for i in range(held):
        pltpu.make_async_copy(
            chunks[0].at[pl.ds(0, TILE), :], grouped.at[pl.ds(i * TILE, TILE), :], sems.at[i]
        ).wait()
    residual = attend(
        grouped, query_utt, key_utt_ref[...], keys, values, query_weight, output_weight
    )
    convolve(
        residual, plan, 0, half_taps, 0.5 * shift[...], out_hbm, padded, residual_rows, out,
        write_sems,
    )


def ring_block(
    frames, tile_source, tile_utt, query_weight, key_weight, value_weight, output_weight,
    depth_weight, bn_scale, bn_shift,
):
    count = lax.axis_size("ctx")
    me = lax.axis_index("ctx")
    rows_dev, width = frames.shape
    tiles_dev = rows_dev // TILE
    ring = [(i, (i + 1) % count) for i in range(count)]
    chunks = [frames]
    for _ in range(count - 1):
        chunks.append(lax.ppermute(chunks[-1], "ctx", ring))
    pairs = [key_value(chunk, key_weight, value_weight) for chunk in chunks]
    shards = lax.rem(me - jnp.arange(count, dtype=jnp.int32) + count, count)
    arrived = (shards[:, None] * tiles_dev + jnp.arange(tiles_dev, dtype=jnp.int32)).reshape(-1)
    key_utt = jnp.sum(
        jnp.where(arrived[:, None] == tile_source[None, :], tile_utt[None, :], 0), axis=1
    )
    key_utt = jnp.repeat(key_utt, TILE).reshape(1, -1)
    return pl.pallas_call(
        functools.partial(ring_kernel, count),
        out_shape=jax.ShapeDtypeStruct((rows_dev, width), jnp.bfloat16),
        in_specs=[SMEM] * 3
        + [VMEM]
        + [pl.BlockSpec(memory_space=pl.ANY)] * count
        + [VMEM] * (2 * count + 5),
        out_specs=HBM,
        scratch_shapes=block_scratch(rows_dev, width)
        + [
            pltpu.VMEM((rows_dev + 2 * TILE, width), jnp.bfloat16),
            pltpu.VMEM((rows_dev + 2 * TILE, 128), jnp.int32),
            pltpu.VMEM(depth_weight.shape, jnp.float32),
            pltpu.SMEM((2 * tiles_dev + 2,), jnp.int32),
            pltpu.SemaphoreType.DMA((tiles_dev + 2,)),
        ],
        cost_estimate=pl.CostEstimate(
            flops=2 << 30, bytes_accessed=8 << 20, transcendentals=1 << 20
        ),
        name="ring_block",
    )(
        me.reshape(1), tile_source, tile_utt, key_utt, *chunks,
        *[pair[0] for pair in pairs], *[pair[1] for pair in pairs],
        query_weight, output_weight, depth_weight, bn_scale.reshape(1, -1), bn_shift.reshape(1, -1),
    )


COUNT = 4
SWAP_OUTER = [(0, 1), (1, 0), (2, 3), (3, 2)]
SWAP_INNER = [(1, 2), (2, 1)]
TO_ENDS = [(1, 0), (2, 3)]
FROM_ENDS = [(0, 1), (3, 2)]
OVER_TWO = [(0, 2), (3, 1)]


def quarter_of(source_shard, target):
    return jnp.where(source_shard % 2 == 1, target, COUNT - 1 - target)


def divide(value, by):
    if by & (by - 1) == 0:
        return value >> (by.bit_length() - 1)
    return lax.div(value, by)


def arrange_kernel(
    me_ref, source_hbm, rows_hbm, low_ref, last_ref, high_ref, start_ref, source_ref, rows, slots, sems
):
    me = me_ref[0]
    rows_dev, quarter_rows = rows.shape[0], last_ref.shape[0]
    tiles_dev = rows_dev // TILE
    per_pair = tiles_dev // COUNT
    rows_copy = pltpu.make_async_copy(rows_hbm, rows, sems.at[0])
    source_copy = pltpu.make_async_copy(source_hbm, source_ref, sems.at[1])
    source_copy.start()
    rows_copy.start()
    source_copy.wait()
    for target in range(COUNT):
        place = quarter_of(me, target) * per_pair
        for position in range(target * tiles_dev, (target + 1) * tiles_dev):
            source = source_ref[position]
            shard = divide(source, tiles_dev)
            mine = shard == me
            slots[jnp.where(mine, place, tiles_dev)] = source - shard * tiles_dev
            place = place + mine.astype(jnp.int32)
    rows_copy.wait()
    for place in range(tiles_dev):
        tile = rows[pl.ds(pl.multiple_of(slots[place] * TILE, TILE), TILE), :]
        row = place * TILE
        if row < rows_dev - quarter_rows:
            low_ref[row : row + TILE] = tile
        else:
            row_here = row - (rows_dev - quarter_rows)
            last_ref[row_here : row_here + TILE] = tile
        if row >= quarter_rows:
            high_ref[row - quarter_rows : row - quarter_rows + TILE] = tile
        else:
            start_ref[row : row + TILE] = tile


def hold_kernel(*refs):
    count = (len(refs) - 3) // 2
    arrays, kept = refs[:count], refs[count : 2 * count - 1]
    taps, scale, shift, sems = refs[2 * count - 1 :]
    targets = (*kept[:-2], taps, scale, shift)
    copies = [
        pltpu.make_async_copy(array, target, sems.at[i])
        for i, (array, target) in enumerate(zip(arrays, targets))
    ]
    for copy in copies:
        copy.start()
    for copy in copies:
        copy.wait()
    kept[-2][...] = taps[...] * (0.5 * scale[...])
    kept[-1][...] = 0.5 * shift[...]


def hold(*arrays):
    taps, scale, shift = arrays[-3:]
    kept = (*arrays[:-2], shift)
    return pl.pallas_call(
        hold_kernel,
        out_shape=tuple(pltpu.VMEM(a.shape, a.dtype) for a in kept),
        in_specs=[HBM] * len(arrays),
        out_specs=(VMEM,) * len(kept),
        scratch_shapes=[pltpu.VMEM(a.shape, a.dtype) for a in (taps, scale, shift)]
        + [pltpu.SemaphoreType.DMA((len(arrays),))],
        compiler_params=params(ALONE),
        cost_estimate=pl.CostEstimate(flops=0, bytes_accessed=8 << 20, transcendentals=0),
        name="hold_call",
    )(*arrays)


def plan_sizes(tiles_dev):
    held = tiles_dev + 2
    return held, 3 * held, 4 * held + tiles_dev


def tables_kernel(
    me_ref, source_ref, utt_ref, plan_ref, key_utt_ref, query_utt_ref, padded_ref,
    filled, ranks, key_utts,
):
    me = me_ref[0]
    total = source_ref.shape[0]
    tiles_dev = total // COUNT
    per_pair = tiles_dev // COUNT
    quarter_tiles = per_pair
    for pair in range(COUNT * COUNT):
        filled[pair] = 0

    def one(position, carried):
        pair = divide(source_ref[position], tiles_dev) * COUNT + divide(position, tiles_dev)
        rank = filled[pair]
        filled[pair] = rank + 1
        ranks[position] = rank
        key_utts[pair * per_pair + rank] = utt_ref[position]
        return carried

    lax.fori_loop(0, total, one, 0, unroll=4)
    is_end = (me == 0) | (me == COUNT - 1)
    second = jnp.where(is_end, 2, 3)
    third = jnp.where(is_end, 3, 2)
    held, places_at, _ = plan_sizes(tiles_dev)
    for i in range(held):
        position = jnp.clip(me * tiles_dev - 1 + i, 0, total - 1)
        source = divide(source_ref[position], tiles_dev)
        apart = me ^ source
        quarter = quarter_of(source, divide(position, tiles_dev))
        row = quarter * quarter_tiles + ranks[position]
        early = jnp.where(apart == 0, row, -1)
        near_last = (apart == 1) & (quarter == COUNT - 1)
        early = jnp.where((apart == 1) & (quarter < COUNT - 1), tiles_dev + row, early)
        plan_ref[2 * held + i] = jnp.where(apart == second, row - quarter_tiles, -1)
        plan_ref[i] = early
        plan_ref[held + i] = jnp.where((apart == third) | near_last, row, -1)
        query_utt_ref[i * TILE : (i + 1) * TILE] = jnp.full(
            (TILE, 128), utt_ref[position], jnp.int32
        )
    plan_places(me, utt_ref, tiles_dev, total, plan_ref, places_at)

    near, second, far = me ^ 1, me ^ second, me ^ third
    order = [(me, quarter, False) for quarter in (0, 1, 2, 3)]
    order += [(near, quarter, False) for quarter in (0, 1, 2)]
    order += [(second, quarter, False) for quarter in (1, 2, 3)]
    order += [(far, quarter, False) for quarter in (0, 1, 2)]
    order += [(near, 3, True), (second, 0, True), (far, 3, True)]
    lane_tile = lax.broadcasted_iota(jnp.int32, (1, 128), 1) // TILE
    tile_values = []
    for shard, quarter, inner_only in order:
        target = quarter_of(shard, quarter)
        for rank in range(per_pair):
            utt = key_utts[(shard * COUNT + target) * per_pair + rank]
            if inner_only:
                utt = jnp.where(is_end, -1, utt)
            tile_values.append(utt)
    per_vector = 128 // TILE
    for start in range(0, len(tile_values), per_vector):
        vector = jnp.full((1, 128), tile_values[start], jnp.int32)
        for k in range(1, per_vector):
            vector = jnp.where(lane_tile == k, tile_values[start + k], vector)
        key_utt_ref[:, start * TILE : start * TILE + 128] = vector
    padded_ref[...] = jnp.zeros_like(padded_ref)


def place_tiles(grouped, rows, plan, at):
    for i in range(grouped.shape[0] // TILE):
        place = plan[at + i]

        @pl.when(place >= 0)
        def _(place=place, i=i):
            grouped[i * TILE : (i + 1) * TILE] = rows[
                pl.ds(pl.multiple_of(place * TILE, TILE), TILE), :
            ]


def early_kernel(
    plan, low, last, near, key_weight, value_weight, key_ref, value_ref, grouped, rows
):
    piece, quarter_rows = low.shape[0], last.shape[0]
    base = piece + quarter_rows
    rows[0:piece] = low[...]
    rows[piece:base] = last[...]
    rows[base:] = near[...]
    grouped[...] = jnp.zeros_like(grouped)
    place_tiles(grouped, rows, plan, 0)
    normed = layer_norm(rows[...]).astype(jnp.bfloat16)
    key_ref[...] = project(normed, key_weight)
    value_ref[...] = project(normed, value_weight)


def second_kernel(
    me_ref, plan, early_grouped, inner, inner_end, key_weight, value_weight,
    key_ref, value_ref, grouped, rows,
):
    me = me_ref[0]
    is_end = (me == 0) | (me == COUNT - 1)

    @pl.when(is_end)
    def _():
        rows[...] = inner_end[...]

    @pl.when(jnp.logical_not(is_end))
    def _():
        rows[...] = inner[...]

    place_tiles(grouped, rows, plan, 2 * (grouped.shape[0] // TILE))
    normed = layer_norm(rows[...]).astype(jnp.bfloat16)
    key_ref[...] = project(normed, key_weight)
    value_ref[...] = project(normed, value_weight)


def middle_kernel(me_ref, *refs):
    me = me_ref[0]
    is_end = (me == 0) | (me == COUNT - 1)
    parts, (key_weight, value_weight, key_ref, value_ref) = refs[:-4], refs[-4:]

    @pl.when(is_end)
    def _():
        key_ref[...] = jnp.zeros_like(key_ref)
        value_ref[...] = jnp.zeros_like(value_ref)

    @pl.when(jnp.logical_not(is_end))
    def _():
        rows = jnp.concatenate([part[...] for part in parts], axis=0)
        normed = layer_norm(rows).astype(jnp.bfloat16)
        key_ref[...] = project(normed, key_weight)
        value_ref[...] = project(normed, value_weight)


def final_kernel(
    me_ref, plan, query_utt, key_utt, early_grouped, zeros, far, far_end, near_last,
    early_key, early_value, second_key, second_value, middle_key, middle_value,
    key_weight, value_weight, query_weight, output_weight, half_taps, half_shift,
    out_hbm, grouped, padded, residual_rows, out, write_sems, late, residual,
):
    me = me_ref[0]
    is_end = (me == 0) | (me == COUNT - 1)
    held, places_at, _ = plan_sizes(out.shape[0] // TILE)
    late[far.shape[0] :] = near_last[...]

    @pl.when(is_end)
    def _():
        late[: far.shape[0]] = far_end[...]

    @pl.when(jnp.logical_not(is_end))
    def _():
        late[: far.shape[0]] = far[...]

    place_tiles(grouped, late, plan, held)
    normed = layer_norm(late[: far.shape[0]]).astype(jnp.bfloat16)
    late_key = project(normed, key_weight)
    late_value = project(normed, value_weight)
    keys = [early_key, second_key, late_key, middle_key]
    values = [early_value, second_value, late_value, middle_value]
    used = key_utt.shape[1] - middle_key.shape[0]

    @pl.when(is_end)
    def _():
        residual[...] = attend(
            grouped, query_utt, key_utt[:, :used], keys[:-1], values[:-1],
            query_weight, output_weight,
        )

    @pl.when(jnp.logical_not(is_end))
    def _():
        residual[...] = attend(
            grouped, query_utt, key_utt[...], keys, values, query_weight, output_weight
        )

    convolve(
        residual[...], plan, places_at, half_taps, half_shift[...], out_hbm, padded, residual_rows,
        out, write_sems,
    )


def line_block(
    frames, tile_source, tile_utt, query_weight, key_weight, value_weight, output_weight,
    depth_weight, bn_scale, bn_shift,
):
    me = lax.axis_index("ctx").reshape(1)
    rows_dev, width = frames.shape
    quarter = rows_dev // COUNT
    piece = rows_dev - quarter
    total = tile_source.shape[0]
    wide = key_weight.shape[1]

    def shape(rows, columns=width, kind=jnp.bfloat16):
        return jax.ShapeDtypeStruct((rows, columns), kind)

    def cost(rows):
        return pl.CostEstimate(
            flops=4 * rows * width * wide, bytes_accessed=rows * width * 4, transcendentals=rows
        )

    low, last, high, start = pl.pallas_call(
        arrange_kernel,
        out_shape=tuple(pltpu.VMEM((n, width), frames.dtype) for n in (piece, quarter, piece, quarter)),
        in_specs=[SMEM] + [HBM] * 2,
        out_specs=(VMEM,) * 4,
        scratch_shapes=[
            pltpu.SMEM((total,), jnp.int32),
            pltpu.VMEM((rows_dev, width), jnp.bfloat16),
            pltpu.SMEM((rows_dev // TILE + 1,), jnp.int32),
            pltpu.SemaphoreType.DMA((2,)),
        ],
        compiler_params=params(ALONE),
        name="arrange",
    )(me, tile_source, frames)

    def swap(value, perm):
        return lax.ppermute(value, "ctx", perm)

    near = swap(low, SWAP_OUTER)
    inner = swap(high, SWAP_INNER)
    held_rows = rows_dev + 2 * TILE
    padded_shape = jax.ShapeDtypeStruct(
        (width // 128, padded_rows(rows_dev // TILE), 128), jnp.float32
    )
    plan, key_utt, query_utt, padded = pl.pallas_call(
        tables_kernel,
        out_shape=(
            jax.ShapeDtypeStruct((plan_sizes(rows_dev // TILE)[2],), jnp.int32),
            shape(1, total * TILE, jnp.int32),
            shape(held_rows, 128, jnp.int32),
            padded_shape,
        ),
        in_specs=[SMEM] * 3,
        out_specs=(SMEM, VMEM, VMEM, VMEM),
        scratch_shapes=[pltpu.SMEM((n,), jnp.int32) for n in (COUNT * COUNT, total, total)],
        compiler_params=params(8),
        name="tables_call",
    )(me, tile_source, tile_utt)
    key_weight, value_weight, query_weight, output_weight, half_taps, half_shift = hold(
        key_weight, value_weight, query_weight, output_weight, depth_weight,
        bn_scale.reshape(1, -1), bn_shift.reshape(1, -1),
    )
    far = swap(low, OVER_TWO)
    inner_end = swap(inner, TO_ENDS)
    far_end = swap(far, TO_ENDS)
    far_last = swap(last, OVER_TWO)
    near_last = swap(last, FROM_ENDS)
    inner_start = swap(start, SWAP_INNER)

    early_rows = rows_dev + piece
    early_key, early_value, grouped = pl.pallas_call(
        early_kernel,
        out_shape=(shape(early_rows, wide), shape(early_rows, wide), shape(held_rows)),
        in_specs=[SMEM] + [VMEM] * 5,
        out_specs=(VMEM,) * 3,
        scratch_shapes=[pltpu.VMEM((early_rows, width), jnp.bfloat16)],
        compiler_params=params(12),
        cost_estimate=cost(early_rows),
        name="early_call",
    )(plan, low, last, near, key_weight, value_weight)
    second_key, second_value, grouped = pl.pallas_call(
        second_kernel,
        out_shape=(shape(piece, wide), shape(piece, wide), shape(held_rows)),
        in_specs=[SMEM] * 2 + [VMEM] * 5,
        out_specs=(VMEM,) * 3,
        input_output_aliases={2: 2},
        scratch_shapes=[pltpu.VMEM((piece, width), jnp.bfloat16)],
        compiler_params=params(8),
        cost_estimate=cost(piece),
        name="second_call",
    )(me, plan, grouped, inner, inner_end, key_weight, value_weight)
    middle_key, middle_value = pl.pallas_call(
        middle_kernel,
        out_shape=(shape(3 * quarter, wide),) * 2,
        in_specs=[SMEM] + [VMEM] * 5,
        out_specs=(VMEM,) * 2,
        compiler_params=params(8),
        cost_estimate=cost(3 * quarter),
        name="middle_call",
    )(me, near_last, inner_start, far_last, key_weight, value_weight)
    return pl.pallas_call(
        final_kernel,
        out_shape=(shape(rows_dev), shape(held_rows), padded_shape),
        in_specs=[SMEM] * 2 + [VMEM] * 19,
        out_specs=(HBM, VMEM, VMEM),
        input_output_aliases={4: 1, 5: 2},
        scratch_shapes=block_scratch(rows_dev, width)[1:]
        + [pltpu.VMEM((rows, width), jnp.bfloat16) for rows in (rows_dev, held_rows)],
        compiler_params=params(28),
        cost_estimate=pl.CostEstimate(
            flops=2 << 30, bytes_accessed=8 << 20, transcendentals=1 << 20
        ),
        name="final",
    )(
        me, plan, query_utt, key_utt, grouped, padded, far, far_end, near_last,
        early_key, early_value, second_key, second_value, middle_key, middle_value,
        key_weight, value_weight, query_weight, output_weight, half_taps, half_shift,
    )[0]


def per_device(*arrays):
    tiles_dev = arrays[0].shape[0] // TILE
    if lax.axis_size("ctx") == COUNT and tiles_dev % COUNT == 0:
        return line_block(*arrays)
    return ring_block(*arrays)


def solution(mesh):
    return jax.shard_map(
        per_device,
        mesh=mesh,
        in_specs=(P(("dp", "ctx"), None), P("dp"), P("dp"), P(), P(), P(), P(), P(), P(), P()),
        out_specs=P(("dp", "ctx"), None),
        check_vma=False,
    )
```

```python
import functools
import math

import jax
import jax.numpy as jnp
from jax import lax
from jax.experimental import pallas as pl
from jax.experimental.pallas import tpu as pltpu
from jax.sharding import PartitionSpec as P


HEADS = 4
HEAD_DIM = 128
KERNEL = 31
TILE = 16
UTTS = 4
ALONE = 56
NEGATIVE = -1e30

VMEM = pl.BlockSpec(memory_space=pltpu.VMEM)
SMEM = pl.BlockSpec(memory_space=pltpu.SMEM)
HBM = pl.BlockSpec(memory_space=pltpu.HBM)


def params(mib):
    return pltpu.CompilerParams(vmem_limit_bytes=mib << 20)


def layer_norm(rows):
    values = rows.astype(jnp.float32)
    center = values - jnp.mean(values, axis=-1, keepdims=True)
    spread = jnp.mean(center * center, axis=-1, keepdims=True)
    return center * lax.rsqrt(spread + 1e-05)


def project(rows, weight_ref):
    return jnp.dot(rows, weight_ref[...], preferred_element_type=jnp.float32).astype(jnp.bfloat16)


def attend(
    grouped, query_utt, key_utt, key_parts, value_parts, query_weight, output_weight
):
    queries = project(layer_norm(grouped[...]).astype(jnp.bfloat16), query_weight)
    allowed = query_utt[:, :1] == key_utt
    exponent_scale = math.log2(math.e) / math.sqrt(HEAD_DIM)
    heads = []
    for head in range(HEADS):
        columns = slice(head * HEAD_DIM, (head + 1) * HEAD_DIM)
        key_head = jnp.concatenate([part[:, columns] for part in key_parts], axis=0)
        value_head = jnp.concatenate([part[:, columns] for part in value_parts], axis=0)
        scores = lax.dot_general(
            queries[:, columns],
            key_head,
            (((1,), (1,)), ((), ())),
            preferred_element_type=jnp.float32,
        )
        scores = jnp.where(allowed, scores, NEGATIVE)
        top = jnp.max(scores, axis=-1, keepdims=True)
        weights = jnp.exp2((scores - top) * exponent_scale)
        row_sum = jnp.sum(weights, axis=-1, keepdims=True)
        summed = jnp.dot(
            weights.astype(jnp.bfloat16), value_head, preferred_element_type=jnp.float32
        )
        heads.append((summed / row_sum).astype(jnp.bfloat16))
    attended = jnp.concatenate(heads, axis=1)
    return (
        grouped[...].astype(jnp.float32)
        + jnp.dot(attended, output_weight[...], preferred_element_type=jnp.float32)
    ).astype(jnp.bfloat16)


def convolve(residual, plan, at, half_taps, half_shift, out_hbm, padded, residual_rows, out, sems):
    rows_dev, width = out.shape
    tiles_dev = rows_dev // TILE
    held = tiles_dev + 2
    residual_rows[...] = residual[TILE : TILE + rows_dev]
    shaped = layer_norm(residual).astype(jnp.bfloat16).astype(jnp.float32)
    for i in range(held):
        row = pl.multiple_of(plan[at + i] * TILE, TILE)
        for block in range(width // 128):
            padded[block, pl.ds(row, TILE), :] = shaped[
                i * TILE : (i + 1) * TILE, block * 128 : (block + 1) * 128
            ]
    group = math.gcd(tiles_dev, 4)

    def write(step):
        rows = pl.ds(pl.multiple_of(step * group * TILE, TILE), group * TILE)
        return pltpu.make_async_copy(out.at[rows, :], out_hbm.at[rows, :], sems.at[step])

    def some_tiles(step, carried):
        starts = [
            pl.multiple_of(plan[at + held + step * group + k] * TILE, TILE) for k in range(group)
        ]
        for block in range(width // 128):
            columns = slice(block * 128, (block + 1) * 128)
            shift = jnp.broadcast_to(half_shift[:, columns], (8, 128))
            sums = [[shift, shift] for _ in range(group)]
            windows = [{} for _ in range(group)]
            for tap in range(KERNEL):
                weight = half_taps[tap : tap + 1, columns]
                for k in range(group):
                    for part in range(2):
                        offset = tap + 8 * part
                        if offset not in windows[k]:
                            windows[k][offset] = padded[
                                block, pl.ds(starts[k] + (offset - KERNEL // 2), 8), :
                            ]
                        sums[k][part] = sums[k][part] + windows[k][offset] * weight
            for k in range(group):
                half = jnp.concatenate(sums[k], axis=0)
                rows = pl.ds(pl.multiple_of((step * group + k) * TILE, TILE), TILE)
                kept = residual_rows[rows, columns].astype(jnp.float32)
                out[rows, columns] = (kept + (half + half * jnp.tanh(half))).astype(jnp.bfloat16)
        write(step).start()
        return carried

    steps = tiles_dev // group
    lax.fori_loop(0, steps, some_tiles, 0)
    for step in range(steps):
        write(step).wait()


def plan_places(me, utt_ref, tiles_dev, total, plan, at):
    first = me * tiles_dev - 1
    held = tiles_dev + 2
    place = jnp.int32(1)
    before = utt_ref[jnp.clip(first, 0, total - 1)]
    for i in range(held):
        here = utt_ref[jnp.clip(first + i, 0, total - 1)]
        if i:
            place = place + 1 + (here != before).astype(jnp.int32)
        before = here
        inside = (first + i >= 0) & (first + i < total)
        plan[at + i] = jnp.where(inside, place, padded_rows(tiles_dev) // TILE - 1)
        if 1 <= i <= tiles_dev:
            plan[at + held + i - 1] = place


def padded_rows(tiles_dev):
    return (1 + tiles_dev + 2 + (UTTS - 1) + 2) * TILE


def block_scratch(rows_dev, width):
    tiles_dev = rows_dev // TILE
    return [
        pltpu.VMEM((width // 128, padded_rows(tiles_dev), 128), jnp.float32),
        pltpu.VMEM((rows_dev, width), jnp.bfloat16),
        pltpu.VMEM((rows_dev, width), jnp.bfloat16),
        pltpu.SemaphoreType.DMA((tiles_dev // math.gcd(tiles_dev, 4),)),
    ]


def key_value_kernel(rows_ref, key_weight_ref, value_weight_ref, key_ref, value_ref):
    normed = layer_norm(rows_ref[...]).astype(jnp.bfloat16)
    key_ref[...] = project(normed, key_weight_ref)
    value_ref[...] = project(normed, value_weight_ref)


def key_value(rows, key_weight, value_weight):
    shape = jax.ShapeDtypeStruct((rows.shape[0], key_weight.shape[1]), jnp.bfloat16)
    flops = 4 * rows.shape[0] * rows.shape[1] * key_weight.shape[1]
    return pl.pallas_call(
        key_value_kernel,
        out_shape=(shape, shape),
        in_specs=[VMEM] * 3,
        out_specs=(VMEM, VMEM),
        cost_estimate=pl.CostEstimate(flops=flops, bytes_accessed=3 << 20, transcendentals=0),
        name="key_value",
    )(rows, key_weight, value_weight)


def ring_kernel(count, me_ref, source_ref, utt_ref, key_utt_ref, *refs):
    chunks = refs[:count]
    keys = refs[count : 2 * count]
    values = refs[2 * count : 3 * count]
    query_weight, output_weight, taps, scale, shift, out_hbm = refs[3 * count : 3 * count + 6]
    padded, residual_rows, out, write_sems = refs[3 * count + 6 : 3 * count + 10]
    grouped, query_utt, half_taps, plan, sems = refs[3 * count + 10 :]
    me = me_ref[0]
    tiles_dev = out.shape[0] // TILE
    held = tiles_dev + 2
    total = tiles_dev * count
    first = me * tiles_dev - 1
    padded[...] = jnp.zeros_like(padded)
    half_taps[...] = taps[...] * (0.5 * scale[...])
    for i in range(held):
        position = jnp.clip(first + i, 0, total - 1)
        source = source_ref[position]
        row = pl.multiple_of((source % tiles_dev) * TILE, TILE)
        behind = lax.rem(me - source // tiles_dev + count, count)
        for step in range(count):

            @pl.when(behind == step)
            def _(step=step, row=row, i=i):
                pltpu.make_async_copy(
                    chunks[step].at[pl.ds(row, TILE), :],
                    grouped.at[pl.ds(i * TILE, TILE), :],
                    sems.at[i],
                ).start()

        query_utt[pl.ds(i * TILE, TILE), :] = jnp.full((TILE, 128), utt_ref[position], jnp.int32)
    plan_places(me, utt_ref, tiles_dev, total, plan, 0)
    for i in range(held):
        pltpu.make_async_copy(
            chunks[0].at[pl.ds(0, TILE), :], grouped.at[pl.ds(i * TILE, TILE), :], sems.at[i]
        ).wait()
    residual = attend(
        grouped, query_utt, key_utt_ref[...], keys, values, query_weight, output_weight
    )
    convolve(
        residual, plan, 0, half_taps, 0.5 * shift[...], out_hbm, padded, residual_rows, out,
        write_sems,
    )


def ring_block(
    frames, tile_source, tile_utt, query_weight, key_weight, value_weight, output_weight,
    depth_weight, bn_scale, bn_shift,
):
    count = lax.axis_size("ctx")
    me = lax.axis_index("ctx")
    rows_dev, width = frames.shape
    tiles_dev = rows_dev // TILE
    ring = [(i, (i + 1) % count) for i in range(count)]
    chunks = [frames]
    for _ in range(count - 1):
        chunks.append(lax.ppermute(chunks[-1], "ctx", ring))
    pairs = [key_value(chunk, key_weight, value_weight) for chunk in chunks]
    shards = lax.rem(me - jnp.arange(count, dtype=jnp.int32) + count, count)
    arrived = (shards[:, None] * tiles_dev + jnp.arange(tiles_dev, dtype=jnp.int32)).reshape(-1)
    key_utt = jnp.sum(
        jnp.where(arrived[:, None] == tile_source[None, :], tile_utt[None, :], 0), axis=1
    )
    key_utt = jnp.repeat(key_utt, TILE).reshape(1, -1)
    return pl.pallas_call(
        functools.partial(ring_kernel, count),
        out_shape=jax.ShapeDtypeStruct((rows_dev, width), jnp.bfloat16),
        in_specs=[SMEM] * 3
        + [VMEM]
        + [pl.BlockSpec(memory_space=pl.ANY)] * count
        + [VMEM] * (2 * count + 5),
        out_specs=HBM,
        scratch_shapes=block_scratch(rows_dev, width)
        + [
            pltpu.VMEM((rows_dev + 2 * TILE, width), jnp.bfloat16),
            pltpu.VMEM((rows_dev + 2 * TILE, 128), jnp.int32),
            pltpu.VMEM(depth_weight.shape, jnp.float32),
            pltpu.SMEM((2 * tiles_dev + 2,), jnp.int32),
            pltpu.SemaphoreType.DMA((tiles_dev + 2,)),
        ],
        cost_estimate=pl.CostEstimate(
            flops=2 << 30, bytes_accessed=8 << 20, transcendentals=1 << 20
        ),
        name="ring_block",
    )(
        me.reshape(1), tile_source, tile_utt, key_utt, *chunks,
        *[pair[0] for pair in pairs], *[pair[1] for pair in pairs],
        query_weight, output_weight, depth_weight, bn_scale.reshape(1, -1), bn_shift.reshape(1, -1),
    )


COUNT = 4
SWAP_OUTER = [(0, 1), (1, 0), (2, 3), (3, 2)]
SWAP_INNER = [(1, 2), (2, 1)]
TO_ENDS = [(1, 0), (2, 3)]
FROM_ENDS = [(0, 1), (3, 2)]
OVER_TWO = [(0, 2), (3, 1)]


def quarter_of(source_shard, target):
    return jnp.where(source_shard % 2 == 1, target, COUNT - 1 - target)


def divide(value, by):
    if by & (by - 1) == 0:
        return value >> (by.bit_length() - 1)
    return lax.div(value, by)


def arrange_kernel(
    me_ref, source_hbm, rows_hbm, low_ref, last_ref, high_ref, start_ref, source_ref, rows, slots, sems
):
    me = me_ref[0]
    rows_dev, quarter_rows = rows.shape[0], last_ref.shape[0]
    tiles_dev = rows_dev // TILE
    per_pair = tiles_dev // COUNT
    rows_copy = pltpu.make_async_copy(rows_hbm, rows, sems.at[0])
    source_copy = pltpu.make_async_copy(source_hbm, source_ref, sems.at[1])
    source_copy.start()
    rows_copy.start()
    source_copy.wait()
    for target in range(COUNT):
        place = quarter_of(me, target) * per_pair
        for position in range(target * tiles_dev, (target + 1) * tiles_dev):
            source = source_ref[position]
            shard = divide(source, tiles_dev)
            mine = shard == me
            slots[jnp.where(mine, place, tiles_dev)] = source - shard * tiles_dev
            place = place + mine.astype(jnp.int32)
    rows_copy.wait()
    for place in range(tiles_dev):
        tile = rows[pl.ds(pl.multiple_of(slots[place] * TILE, TILE), TILE), :]
        row = place * TILE
        if row < rows_dev - quarter_rows:
            low_ref[row : row + TILE] = tile
        else:
            row_here = row - (rows_dev - quarter_rows)
            last_ref[row_here : row_here + TILE] = tile
        if row >= quarter_rows:
            high_ref[row - quarter_rows : row - quarter_rows + TILE] = tile
        else:
            start_ref[row : row + TILE] = tile


def hold_kernel(*refs):
    count = (len(refs) - 3) // 2
    arrays, kept = refs[:count], refs[count : 2 * count - 1]
    taps, scale, shift, sems = refs[2 * count - 1 :]
    targets = (*kept[:-2], taps, scale, shift)
    copies = [
        pltpu.make_async_copy(array, target, sems.at[i])
        for i, (array, target) in enumerate(zip(arrays, targets))
    ]
    for copy in copies:
        copy.start()
    for copy in copies:
        copy.wait()
    kept[-2][...] = taps[...] * (0.5 * scale[...])
    kept[-1][...] = 0.5 * shift[...]


def hold(*arrays):
    taps, scale, shift = arrays[-3:]
    kept = (*arrays[:-2], shift)
    return pl.pallas_call(
        hold_kernel,
        out_shape=tuple(pltpu.VMEM(a.shape, a.dtype) for a in kept),
        in_specs=[HBM] * len(arrays),
        out_specs=(VMEM,) * len(kept),
        scratch_shapes=[pltpu.VMEM(a.shape, a.dtype) for a in (taps, scale, shift)]
        + [pltpu.SemaphoreType.DMA((len(arrays),))],
        compiler_params=params(ALONE),
        cost_estimate=pl.CostEstimate(flops=0, bytes_accessed=8 << 20, transcendentals=0),
        name="hold_call",
    )(*arrays)


def plan_sizes(tiles_dev):
    held = tiles_dev + 2
    return held, 3 * held, 4 * held + tiles_dev


def tables_kernel(
    me_ref, source_ref, utt_ref, plan_ref, key_utt_ref, query_utt_ref, padded_ref,
    filled, ranks, key_utts,
):
    me = me_ref[0]
    total = source_ref.shape[0]
    tiles_dev = total // COUNT
    per_pair = tiles_dev // COUNT
    quarter_tiles = per_pair
    for pair in range(COUNT * COUNT):
        filled[pair] = 0

    def one(position, carried):
        pair = divide(source_ref[position], tiles_dev) * COUNT + divide(position, tiles_dev)
        rank = filled[pair]
        filled[pair] = rank + 1
        ranks[position] = rank
        key_utts[pair * per_pair + rank] = utt_ref[position]
        return carried

    lax.fori_loop(0, total, one, 0, unroll=4)
    is_end = (me == 0) | (me == COUNT - 1)
    second = jnp.where(is_end, 2, 3)
    third = jnp.where(is_end, 3, 2)
    held, places_at, _ = plan_sizes(tiles_dev)
    for i in range(held):
        position = jnp.clip(me * tiles_dev - 1 + i, 0, total - 1)
        source = divide(source_ref[position], tiles_dev)
        apart = me ^ source
        quarter = quarter_of(source, divide(position, tiles_dev))
        row = quarter * quarter_tiles + ranks[position]
        early = jnp.where(apart == 0, row, -1)
        near_last = (apart == 1) & (quarter == COUNT - 1)
        early = jnp.where((apart == 1) & (quarter < COUNT - 1), tiles_dev + row, early)
        plan_ref[2 * held + i] = jnp.where(apart == second, row - quarter_tiles, -1)
        plan_ref[i] = early
        plan_ref[held + i] = jnp.where((apart == third) | near_last, row, -1)
        query_utt_ref[i * TILE : (i + 1) * TILE] = jnp.full(
            (TILE, 128), utt_ref[position], jnp.int32
        )
    plan_places(me, utt_ref, tiles_dev, total, plan_ref, places_at)

    near, second, far = me ^ 1, me ^ second, me ^ third
    order = [(me, quarter, False) for quarter in (0, 1, 2, 3)]
    order += [(near, quarter, False) for quarter in (0, 1, 2)]
    order += [(second, quarter, False) for quarter in (1, 2, 3)]
    order += [(near, 3, True), (second, 0, True), (far, 3, True)]
    order += [(far, quarter, False) for quarter in (0, 1, 2)]
    lane_tile = lax.broadcasted_iota(jnp.int32, (1, 128), 1) // TILE
    tile_values = []
    for shard, quarter, inner_only in order:
        target = quarter_of(shard, quarter)
        for rank in range(per_pair):
            utt = key_utts[(shard * COUNT + target) * per_pair + rank]
            if inner_only:
                utt = jnp.where(is_end, -1, utt)
            tile_values.append(utt)
    per_vector = 128 // TILE
    for start in range(0, len(tile_values), per_vector):
        vector = jnp.full((1, 128), tile_values[start], jnp.int32)
        for k in range(1, per_vector):
            vector = jnp.where(lane_tile == k, tile_values[start + k], vector)
        key_utt_ref[:, start * TILE : start * TILE + 128] = vector
    padded_ref[...] = jnp.zeros_like(padded_ref)


def place_tiles(grouped, rows, plan, at):
    for i in range(grouped.shape[0] // TILE):
        place = plan[at + i]

        @pl.when(place >= 0)
        def _(place=place, i=i):
            grouped[i * TILE : (i + 1) * TILE] = rows[
                pl.ds(pl.multiple_of(place * TILE, TILE), TILE), :
            ]


def early_kernel(
    plan, low, last, near, key_weight, value_weight, key_ref, value_ref, grouped, rows
):
    piece, quarter_rows = low.shape[0], last.shape[0]
    base = piece + quarter_rows
    rows[0:piece] = low[...]
    rows[piece:base] = last[...]
    rows[base:] = near[...]
    grouped[...] = jnp.zeros_like(grouped)
    place_tiles(grouped, rows, plan, 0)
    normed = layer_norm(rows[...]).astype(jnp.bfloat16)
    key_ref[...] = project(normed, key_weight)
    value_ref[...] = project(normed, value_weight)


def second_kernel(
    me_ref, plan, early_grouped, inner, inner_end, key_weight, value_weight,
    key_ref, value_ref, grouped, rows,
):
    me = me_ref[0]
    is_end = (me == 0) | (me == COUNT - 1)

    @pl.when(is_end)
    def _():
        rows[...] = inner_end[...]

    @pl.when(jnp.logical_not(is_end))
    def _():
        rows[...] = inner[...]

    place_tiles(grouped, rows, plan, 2 * (grouped.shape[0] // TILE))
    normed = layer_norm(rows[...]).astype(jnp.bfloat16)
    key_ref[...] = project(normed, key_weight)
    value_ref[...] = project(normed, value_weight)


def middle_kernel(me_ref, *refs):
    me = me_ref[0]
    is_end = (me == 0) | (me == COUNT - 1)
    parts, (key_weight, value_weight, key_ref, value_ref) = refs[:-4], refs[-4:]

    @pl.when(is_end)
    def _():
        key_ref[...] = jnp.zeros_like(key_ref)
        value_ref[...] = jnp.zeros_like(value_ref)

    @pl.when(jnp.logical_not(is_end))
    def _():
        rows = jnp.concatenate([part[...] for part in parts], axis=0)
        normed = layer_norm(rows).astype(jnp.bfloat16)
        key_ref[...] = project(normed, key_weight)
        value_ref[...] = project(normed, value_weight)


def final_kernel(
    me_ref, plan, query_utt, key_utt, early_grouped, zeros, far, far_end, near_last,
    early_key, early_value, second_key, second_value, middle_key, middle_value,
    key_weight, value_weight, query_weight, output_weight, half_taps, half_shift,
    out_hbm, grouped, padded, residual_rows, out, write_sems, late,
):
    me = me_ref[0]
    is_end = (me == 0) | (me == COUNT - 1)
    held, places_at, _ = plan_sizes(out.shape[0] // TILE)
    late[far.shape[0] :] = near_last[...]

    @pl.when(is_end)
    def _():
        late[: far.shape[0]] = far_end[...]

    @pl.when(jnp.logical_not(is_end))
    def _():
        late[: far.shape[0]] = far[...]

    place_tiles(grouped, late, plan, held)
    normed = layer_norm(late[: far.shape[0]]).astype(jnp.bfloat16)
    late_key = project(normed, key_weight)
    late_value = project(normed, value_weight)
    residual = attend(
        grouped, query_utt, key_utt[...],
        [early_key, second_key, middle_key, late_key],
        [early_value, second_value, middle_value, late_value],
        query_weight, output_weight,
    )
    convolve(
        residual, plan, places_at, half_taps, half_shift[...], out_hbm, padded, residual_rows,
        out, write_sems,
    )


def line_block(
    frames, tile_source, tile_utt, query_weight, key_weight, value_weight, output_weight,
    depth_weight, bn_scale, bn_shift,
):
    me = lax.axis_index("ctx").reshape(1)
    rows_dev, width = frames.shape
    quarter = rows_dev // COUNT
    piece = rows_dev - quarter
    total = tile_source.shape[0]
    wide = key_weight.shape[1]

    def shape(rows, columns=width, kind=jnp.bfloat16):
        return jax.ShapeDtypeStruct((rows, columns), kind)

    def cost(rows):
        return pl.CostEstimate(
            flops=4 * rows * width * wide, bytes_accessed=rows * width * 4, transcendentals=rows
        )

    low, last, high, start = pl.pallas_call(
        arrange_kernel,
        out_shape=tuple(pltpu.VMEM((n, width), frames.dtype) for n in (piece, quarter, piece, quarter)),
        in_specs=[SMEM] + [HBM] * 2,
        out_specs=(VMEM,) * 4,
        scratch_shapes=[
            pltpu.SMEM((total,), jnp.int32),
            pltpu.VMEM((rows_dev, width), jnp.bfloat16),
            pltpu.SMEM((rows_dev // TILE + 1,), jnp.int32),
            pltpu.SemaphoreType.DMA((2,)),
        ],
        compiler_params=params(ALONE),
        name="arrange",
    )(me, tile_source, frames)

    def swap(value, perm):
        return lax.ppermute(value, "ctx", perm)

    near = swap(low, SWAP_OUTER)
    inner = swap(high, SWAP_INNER)
    held_rows = rows_dev + 2 * TILE
    padded_shape = jax.ShapeDtypeStruct(
        (width // 128, padded_rows(rows_dev // TILE), 128), jnp.float32
    )
    plan, key_utt, query_utt, padded = pl.pallas_call(
        tables_kernel,
        out_shape=(
            jax.ShapeDtypeStruct((plan_sizes(rows_dev // TILE)[2],), jnp.int32),
            shape(1, total * TILE, jnp.int32),
            shape(held_rows, 128, jnp.int32),
            padded_shape,
        ),
        in_specs=[SMEM] * 3,
        out_specs=(SMEM, VMEM, VMEM, VMEM),
        scratch_shapes=[pltpu.SMEM((n,), jnp.int32) for n in (COUNT * COUNT, total, total)],
        compiler_params=params(8),
        name="tables_call",
    )(me, tile_source, tile_utt)
    key_weight, value_weight, query_weight, output_weight, half_taps, half_shift = hold(
        key_weight, value_weight, query_weight, output_weight, depth_weight,
        bn_scale.reshape(1, -1), bn_shift.reshape(1, -1),
    )
    far = swap(low, OVER_TWO)
    inner_end = swap(inner, TO_ENDS)
    far_end = swap(far, TO_ENDS)
    far_last = swap(last, OVER_TWO)
    near_last = swap(last, FROM_ENDS)
    inner_start = swap(start, SWAP_INNER)

    early_rows = rows_dev + piece
    early_key, early_value, grouped = pl.pallas_call(
        early_kernel,
        out_shape=(shape(early_rows, wide), shape(early_rows, wide), shape(held_rows)),
        in_specs=[SMEM] + [VMEM] * 5,
        out_specs=(VMEM,) * 3,
        scratch_shapes=[pltpu.VMEM((early_rows, width), jnp.bfloat16)],
        compiler_params=params(12),
        cost_estimate=cost(early_rows),
        name="early_call",
    )(plan, low, last, near, key_weight, value_weight)
    second_key, second_value, grouped = pl.pallas_call(
        second_kernel,
        out_shape=(shape(piece, wide), shape(piece, wide), shape(held_rows)),
        in_specs=[SMEM] * 2 + [VMEM] * 5,
        out_specs=(VMEM,) * 3,
        input_output_aliases={2: 2},
        scratch_shapes=[pltpu.VMEM((piece, width), jnp.bfloat16)],
        compiler_params=params(8),
        cost_estimate=cost(piece),
        name="second_call",
    )(me, plan, grouped, inner, inner_end, key_weight, value_weight)
    middle_key, middle_value = pl.pallas_call(
        middle_kernel,
        out_shape=(shape(3 * quarter, wide),) * 2,
        in_specs=[SMEM] + [VMEM] * 5,
        out_specs=(VMEM,) * 2,
        compiler_params=params(8),
        cost_estimate=cost(3 * quarter),
        name="middle_call",
    )(me, near_last, inner_start, far_last, key_weight, value_weight)
    return pl.pallas_call(
        final_kernel,
        out_shape=(shape(rows_dev), shape(held_rows), padded_shape),
        in_specs=[SMEM] * 2 + [VMEM] * 19,
        out_specs=(HBM, VMEM, VMEM),
        input_output_aliases={4: 1, 5: 2},
        scratch_shapes=block_scratch(rows_dev, width)[1:] + [pltpu.VMEM((rows_dev, width), jnp.bfloat16)],
        compiler_params=params(28),
        cost_estimate=pl.CostEstimate(
            flops=2 << 30, bytes_accessed=8 << 20, transcendentals=1 << 20
        ),
        name="final",
    )(
        me, plan, query_utt, key_utt, grouped, padded, far, far_end, near_last,
        early_key, early_value, second_key, second_value, middle_key, middle_value,
        key_weight, value_weight, query_weight, output_weight, half_taps, half_shift,
    )[0]


def per_device(*arrays):
    tiles_dev = arrays[0].shape[0] // TILE
    if lax.axis_size("ctx") == COUNT and tiles_dev % COUNT == 0:
        return line_block(*arrays)
    return ring_block(*arrays)


def solution(mesh):
    return jax.shard_map(
        per_device,
        mesh=mesh,
        in_specs=(P(("dp", "ctx"), None), P("dp"), P("dp"), P(), P(), P(), P(), P(), P(), P()),
        out_specs=P(("dp", "ctx"), None),
        check_vma=False,
    )
```
